1024 devices in a mesh: gx: 16 (over y, core), gy: 4 (over x), gz: 16 (over z).
Axes of the slice: x: 4, y: 8, z: 16, core: 2. Of those that a mesh axis runs over, the one named last changes fastest.
Arguments:
- source: float32 [256, 32, 4096], P('gx', 'gy', 'gz'), may hold values from -8 to 8
- phase_mask: int32 [256, 32, 4096], P('gx', 'gy', 'gz'), may hold values 0 or 1
- density_factor: float32 [256, 32, 4096], P('gx', 'gy', 'gz'), may hold values from 0.5 to 2
Outputs:
- pressure: float32 [256, 32, 4096], P('gx', 'gy', 'gz')
The draws below stay inside these ranges and needn't reach their ends.
All inputs are finite; a program needn't handle non-finite values. No bound on the sum of `phase_mask` on one device may be relied on, other than what follows from the above.
Results may differ from the reference program's by a relative error of at most 0.0001.
Values sent between devices are 32-bit elements; how exact they have to be, the bound alone decides.
A program may use at most 64 MiB of HBM per device.

```python
import math
import jax
import jax.numpy as jnp

LEVELS = 2
COARSE_SWEEPS = 8
NX = 256
NY = 32
NZ = 4096


def draw_source(key, part):
    values_drawn = jax.random.truncated_normal(key, -6.0, 6.0, (NX, NY, NZ), jnp.float32)
    return values_drawn


def set_ends(drawn, key, least, high):
    longest = drawn.shape.index(max(drawn.shape))
    spots = []
    for shift in (0, 1):
        where = [jax.random.randint(jax.random.fold_in(key, axis), (), 0, length) for axis, length in enumerate(drawn.shape)]
        where[longest] = (where[longest] + shift) % drawn.shape[longest]
        spots.append(tuple(where))
    return drawn.at[spots[0]].set(least).at[spots[1]].set(high)


def level_of(key, extent, split, least, largest):
    gain, own = 1.0, jax.random.fold_in(key, 6)
    for dim, parts in split:
        steps = jnp.exp(jax.random.uniform(jax.random.fold_in(own, dim), (parts,), jnp.float32, least / len(split), largest / len(split)))
        gain = gain * jnp.repeat(steps, extent[dim] // parts).reshape([-1 if axis == dim else 1 for axis in range(len(extent))])
    return gain


def setup_inputs(seed: int = 0) -> dict:
    splits = jax.random.split(jax.random.key(seed), 4)
    source = draw_source(jax.random.fold_in(splits[3], 71), 0)
    phase_mask = set_ends((jax.random.randint(splits[1], (NX, NY, NZ), 0, 4) < 1).astype(jnp.int32), jax.random.fold_in(splits[1], 1), 0, 1)
    density_factor = jnp.clip(jnp.exp(math.log(2.0) - 1.3862944 * jax.random.uniform(splits[2], (NX, NY, NZ), jnp.float32) ** level_of(splits[2], (NX, NY, NZ), ((0, 16), (1, 4), (2, 16)), -0.2, 0.2)), 0.5, 2.0)
    return {"source": source, "phase_mask": phase_mask, "density_factor": density_factor}


GAS_DENSITY = 0.001
RELAXATION = 0.8
NEIGHBOURS = ((1, 0, 0), (-1, 0, 0), (0, 1, 0), (0, -1, 0), (0, 0, 1), (0, 0, -1))


def shifted(padded, offset):
    return padded[1 + offset[0]:padded.shape[0] - 1 + offset[0],
                  1 + offset[1]:padded.shape[1] - 1 + offset[1],
                  1 + offset[2]:padded.shape[2] - 1 + offset[2]]


def coarsen(cell_values):
    return cell_values.reshape(cell_values.shape[0] // 2, 2, cell_values.shape[1] // 2, 2,
                               cell_values.shape[2] // 2, 2).sum(axis=(1, 3, 5))


def refine(cell_values):
    widened = jnp.broadcast_to(cell_values[:, None, :, None, :, None],
                               (cell_values.shape[0], 2, cell_values.shape[1], 2, cell_values.shape[2], 2))
    return widened.reshape(2 * cell_values.shape[0], 2 * cell_values.shape[1], 2 * cell_values.shape[2])


def diagonal_of(density):
    padded = jnp.pad(density, 1)
    diagonal = jnp.zeros_like(density)
    for offset in NEIGHBOURS:
        diagonal = diagonal + 2.0 / (density + shifted(padded, offset))
    return diagonal


def operate_on(cell_values, density, diagonal):
    padded_density = jnp.pad(density, 1)
    padded_values = jnp.pad(cell_values, 1)
    result = diagonal * cell_values
    for offset in NEIGHBOURS:
        result = result - 2.0 / (density + shifted(padded_density, offset)) * shifted(padded_values, offset)
    return result


def multigrid(source_here, densities, level_index):
    density = densities[level_index]
    diagonal = diagonal_of(density)
    iterate = RELAXATION * source_here / diagonal
    if level_index == LEVELS:
        for sweep_index in range(COARSE_SWEEPS - 1):
            iterate = iterate + RELAXATION * (source_here - operate_on(iterate, density, diagonal)) / diagonal
        return iterate
    iterate = iterate + RELAXATION * (source_here - operate_on(iterate, density, diagonal)) / diagonal
    residual = source_here - operate_on(iterate, density, diagonal)
    correction = multigrid(0.5 * coarsen(residual), densities, level_index + 1)
    iterate = iterate + refine(correction)
    return iterate + RELAXATION * (source_here - operate_on(iterate, density, diagonal)) / diagonal


def reference(source, phase_mask, density_factor):
    density = jnp.where(phase_mask == 1, GAS_DENSITY, 1.0) * density_factor
    densities = [density]
    for level_index in range(LEVELS):
        densities.append(0.125 * coarsen(densities[-1]))
    return multigrid(source, densities, 0)
```

```python
import jax
import jax.numpy as jnp
from jax import lax
from jax.experimental import pallas as pl
from jax.experimental.pallas import tpu as pltpu
from jax.sharding import PartitionSpec as P

GAS_DENSITY = 0.001
RELAXATION = 0.8
KEEP = 1.0 - RELAXATION
COARSE_SWEEPS = 8
MESH = pl.DeviceIdType.MESH
CHUNK = 4
COPIES = 66


def iota(shape, axis):
    return lax.broadcasted_iota(jnp.int32, shape, axis)


def dot(a, b):
    return jnp.dot(a, b, precision=lax.Precision.HIGHEST, preferred_element_type=jnp.float32)


def kernel(src, mask, fac, out, V0, YS0, YH0, ZS0, ZH0, CX0, C0, INV0, DIAG0, R0,
           V1, YS1, YH1, ZS1, ZH1, G, SE, ZE, XB, XD, send_sem, recv_sem):
    nx, ny, nz = lax.axis_size("gx"), lax.axis_size("gy"), lax.axis_size("gz")
    sizes = {"gx": nx, "gy": ny, "gz": nz}
    at = {axis: lax.axis_index(axis) for axis in sizes}
    gy = at["gy"]
    f32 = jnp.float32

    def peer(axis, d):
        return {axis: lax.rem(at[axis] + (d + sizes[axis]), sizes[axis])}

    def exists(axis, d):
        place = at[axis] + d
        return (place >= 0) & (place < sizes[axis])

    copies = []

    def post(source, target, axis, d):
        k = len(copies)
        copy = pltpu.make_async_remote_copy(
            src_ref=source, dst_ref=target, send_sem=send_sem.at[k], recv_sem=recv_sem.at[k],
            device_id=peer(axis, d), device_id_type=MESH)
        copy.start()
        copies.append(copy)
        return copy

    sent = set()

    def arrived(group):
        for copy in group:
            copy.wait_recv()

    def left(group):
        for copy in group:
            copy.wait_send()
            sent.add(id(copy))

    def faces(V, YS, YH, ZS, ZH, k, planes):
        return [
            post(V.at[k, 1], V.at[k, planes + 1], "gx", -1),
            post(V.at[k, planes], V.at[k, 0], "gx", 1),
            post(YS.at[k, 0], YH.at[k, 1], "gy", -1),
            post(YS.at[k, 1], YH.at[k, 0], "gy", 1),
            post(ZS.at[k, 0], ZH.at[k, 1], "gz", -1),
            post(ZS.at[k, 1], ZH.at[k, 0], "gz", 1),
        ]

    def trim(V, YH, ZH, k, planes):
        V[k, 0] = jnp.where(exists("gx", -1), V[k, 0], 0.0)
        V[k, planes + 1] = jnp.where(exists("gx", 1), V[k, planes + 1], 0.0)
        for side, d in ((0, -1), (1, 1)):
            YH[k, side] = jnp.where(exists("gy", d), YH[k, side], 0.0)
            ZH[k, side] = jnp.where(exists("gz", d), ZH[k, side], 0.0)

    barrier = pltpu.get_barrier_semaphore()
    partners = [("gx", d) for d in (-1, 1, -2, 2, -3, 3)] + [("gy", d) for d in (1, 2, 3)] + [("gz", d) for d in (-1, 1)]
    for axis, d in partners:
        pl.semaphore_signal(barrier, inc=1, device_id=peer(axis, d), device_id_type=MESH)

    row8 = iota((8, 128), 0)
    lane8 = iota((8, 128), 1)

    row0 = iota((CHUNK, 8, 256), 1)
    lane0 = iota((CHUNK, 8, 256), 2)
    chunks = range(0, 16, CHUNK)

    def pack_y0(k, c, v):
        for i in range(CHUNK):
            YS0[k, 0, c + i:c + i + 1, :] = v[i, 0:1, :]
            YS0[k, 1, c + i:c + i + 1, :] = v[i, 7:8, :]

    def pack_z0(held, c, v):
        low, high = held
        for i in range(CHUNK):
            low = jnp.where(lane8 == c + i, jnp.broadcast_to(v[i, :, 0:1], (8, 128)), low)
            high = jnp.where(lane8 == c + i, jnp.broadcast_to(v[i, :, 255:256], (8, 128)), high)
        return low, high

    def spread_z0(packed, c):
        return jnp.stack([jnp.broadcast_to(packed[:, c + i:c + i + 1], (8, 256)) for i in range(CHUNK)])

    def rows_y0(ref, c):
        return jnp.stack([jnp.broadcast_to(ref[c + i:c + i + 1, :], (8, 256)) for i in range(CHUNK)])

    def shifts0(v, y_low, y_high, z_low, z_high):
        return (jnp.where(row0 == 7, y_high, pltpu.roll(v, 7, 1)),
                jnp.where(row0 == 0, y_low, pltpu.roll(v, 1, 1)),
                jnp.where(lane0 == 255, z_high, pltpu.roll(v, 255, 2)),
                jnp.where(lane0 == 0, z_low, pltpu.roll(v, 1, 2)))

    def halo0(k, c, zh):
        return (rows_y0(YH0.at[k, 0], c), rows_y0(YH0.at[k, 1], c), spread_z0(zh[0], c), spread_z0(zh[1], c))

    def around0(c, below, above, shifted):
        total = CX0[c:c + CHUNK] * below + CX0[c + 1:c + 1 + CHUNK] * above
        for n in range(4):
            total = total + C0[n, c:c + CHUNK] * shifted[n]
        return total

    zeros8 = jnp.zeros((8, 128), f32)
    held = (zeros8, zeros8)
    for c in chunks:
        rho = jnp.where(mask[c:c + CHUNK] == 1, GAS_DENSITY, 1.0) * fac[c:c + CHUNK]
        V0[0, 1 + c:1 + c + CHUNK] = rho
        pack_y0(0, c, rho)
        held = pack_z0(held, c, rho)
    ZS0[0, 0], ZS0[0, 1] = held
    pl.semaphore_wait(barrier, len(partners))
    rho0_faces = faces(V0, YS0, YH0, ZS0, ZH0, 0, 16)

    row1 = iota((8, 8, 128), 1)
    lane1 = iota((8, 8, 128), 2)
    own1 = (row1 >= 2) & (row1 < 6)
    pairs0 = (lax.shift_right_logical(iota((256, 128), 0), 1) == iota((256, 128), 1)).astype(f32)
    pairs1 = (lax.shift_right_logical(iota((128, 128), 0), 1) == iota((128, 128), 1)).astype(f32)

    def down0(field):
        t = field.reshape(8, 2, 8, 256)
        t = t[:, 0] + t[:, 1]
        t = dot(t.reshape(64, 256), pairs0).reshape(8, 8, 128)
        t = t + pltpu.roll(t, 7, 1)
        t = jnp.where(row1 == 2, pltpu.roll(t, 2, 1),
                      jnp.where(row1 == 3, pltpu.roll(t, 1, 1), jnp.where(row1 == 4, t, pltpu.roll(t, 7, 1))))
        return jnp.where(own1, t, 0.0)

    def down1(field):
        t = field.reshape(4, 2, 8, 128)
        t = t[:, 0] + t[:, 1]
        t = t + pltpu.roll(t, 7, 1)
        packed = zeros8
        for x in range(4):
            for half in range(2):
                shift = (2 * x + half - 2 - 2 * half) % 8
                moved = pltpu.roll(t[x], shift, 0) if shift else t[x]
                packed = jnp.where(row8 == 2 * x + half, moved, packed)
        return dot(packed, pairs1)

    def stage1(k, v):
        V1[k, 1:9] = v
        low, high = zeros8, zeros8
        for p in range(8):
            YS1[k, 0, p:p + 1, :] = v[p, 2:3, :]
            YS1[k, 1, p:p + 1, :] = v[p, 5:6, :]
            low = jnp.where(lane8 == p, jnp.broadcast_to(v[p, :, 0:1], (8, 128)), low)
            high = jnp.where(lane8 == p, jnp.broadcast_to(v[p, :, 127:128], (8, 128)), high)
        ZS1[k, 0], ZS1[k, 1] = low, high
        return faces(V1, YS1, YH1, ZS1, ZH1, k, 8)

    def settle1(k, group):
        arrived(group)
        left(group)
        trim(V1, YH1, ZH1, k, 8)
        for p in range(8):
            V1[k, 1 + p] = jnp.where(row8 == 1, YH1[k, 0, p:p + 1, :], jnp.where(row8 == 6, YH1[k, 1, p:p + 1, :], V1[k, 1 + p]))

    def spread_z1(k):
        low, high = ZH1[k, 0], ZH1[k, 1]
        return (jnp.stack([jnp.broadcast_to(low[:, p:p + 1], (8, 128)) for p in range(8)]),
                jnp.stack([jnp.broadcast_to(high[:, p:p + 1], (8, 128)) for p in range(8)]))

    def shifts1(v, z_low, z_high):
        return (pltpu.roll(v, 7, 1), pltpu.roll(v, 1, 1),
                jnp.where(lane1 == 127, z_high, pltpu.roll(v, 127, 2)),
                jnp.where(lane1 == 0, z_low, pltpu.roll(v, 1, 2)))

    def gather_y2(k, packed):
        G[k, gy] = packed
        return [post(G.at[k, gy], G.at[k, gy], "gy", d) for d in (1, 2, 3)]

    def gather_z2(k):
        for x in range(4):
            t = zeros8
            for q in range(4):
                shift = (2 * (q - x)) % 8
                moved = pltpu.roll(G[k, q], shift, 0) if shift else G[k, q]
                t = jnp.where(lax.shift_right_logical(row8, 1) == q, moved, t)
            SE[k, x] = t
        return [post(SE.at[k], ZE.at[k, 1], "gz", -1), post(SE.at[k], ZE.at[k, 0], "gz", 1)]

    def widen_z2(k):
        lane = iota((4, 8, 128), 2)
        low = jnp.where(exists("gz", -1), ZE[k, 0], 0.0)
        high = jnp.where(exists("gz", 1), ZE[k, 1], 0.0)
        return jnp.where(lane < 64, SE[k], pltpu.roll(jnp.where(lane < 32, high, low), 64, 2))

    rho1 = 0.125 * down0(V0[0, 1:17])
    rho1_faces = stage1(0, rho1)
    rho2_y = gather_y2(0, 0.125 * down1(rho1))

    arrived(rho0_faces)
    trim(V0, YH0, ZH0, 0, 16)
    for c in range(17):
        CX0[c] = 2.0 / (V0[0, c] + V0[0, c + 1])
    zh = (ZH0[0, 0], ZH0[0, 1])
    held = (zeros8, zeros8)
    for c in chunks:
        rho = V0[0, 1 + c:1 + c + CHUNK]
        shifted = shifts0(rho, *halo0(0, c, zh))
        diag = CX0[c:c + CHUNK] + CX0[c + 1:c + 1 + CHUNK]
        for n in range(4):
            coupling = 2.0 / (rho + shifted[n])
            C0[n, c:c + CHUNK] = coupling
            diag = diag + coupling
        inv = RELAXATION / diag
        DIAG0[c:c + CHUNK] = diag
        INV0[c:c + CHUNK] = inv
        v = inv * src[c:c + CHUNK]
        V0[1, 1 + c:1 + c + CHUNK] = v
        pack_y0(1, c, v)
        held = pack_z0(held, c, v)
    ZS0[1, 0], ZS0[1, 1] = held
    v1_faces = faces(V0, YS0, YH0, ZS0, ZH0, 1, 16)

    arrived(rho2_y)
    rho2_z = gather_z2(0)

    settle1(0, rho1_faces)
    rho = V1[0, 1:9]
    x_low1 = 2.0 / (rho + V1[0, 0:8])
    x_high1 = 2.0 / (rho + V1[0, 2:10])
    around1_c = [2.0 / (rho + other) for other in shifts1(rho, *spread_z1(0))]
    diag1 = x_low1 + x_high1 + ((around1_c[0] + around1_c[1]) + (around1_c[2] + around1_c[3]))
    inv1 = RELAXATION / diag1

    def around1(k_or_v, z_low, z_high):
        v = k_or_v
        total = x_low1 * v[0:8] + x_high1 * v[2:10]
        for coupling, other in zip(around1_c, shifts1(v[1:9], z_low, z_high)):
            total = total + coupling * other
        return total

    arrived(v1_faces)
    trim(V0, YH0, ZH0, 1, 16)
    zh = (ZH0[1, 0], ZH0[1, 1])
    held = (zeros8, zeros8)
    for c in chunks:
        v = V0[1, 1 + c:1 + c + CHUNK]
        total = around0(c, V0[1, c:c + CHUNK], V0[1, c + 2:c + 2 + CHUNK], shifts0(v, *halo0(1, c, zh)))
        v = KEEP * v + INV0[c:c + CHUNK] * (src[c:c + CHUNK] + total)
        V0[2, 1 + c:1 + c + CHUNK] = v
        pack_y0(2, c, v)
        held = pack_z0(held, c, v)
    ZS0[2, 0], ZS0[2, 1] = held
    v2_faces = faces(V0, YS0, YH0, ZS0, ZH0, 2, 16)

    arrived(rho2_z)
    XD[9:13] = widen_z2(0)
    rho2_x = [post(XD.at[9:13], XD.at[9 - 4 * d:13 - 4 * d], "gx", d) for d in (-2, -1, 1, 2)]
    rho2_x += [post(XD.at[12], XD.at[0], "gx", 3), post(XD.at[9], XD.at[21], "gx", -3)]

    arrived(v2_faces)
    trim(V0, YH0, ZH0, 2, 16)
    zh = (ZH0[2, 0], ZH0[2, 1])
    for c in chunks:
        v = V0[2, 1 + c:1 + c + CHUNK]
        total = around0(c, V0[2, c:c + CHUNK], V0[2, c + 2:c + 2 + CHUNK], shifts0(v, *halo0(2, c, zh)))
        R0[c:c + CHUNK] = src[c:c + CHUNK] + total - DIAG0[c:c + CHUNK] * v
    b1 = 0.5 * down0(R0[...])
    w1_faces = stage1(1, jnp.where(own1, inv1 * b1, 0.0))

    arrived(rho2_x)
    for d in (-2, -1, 1, 2):
        XD[9 - 4 * d:13 - 4 * d] = jnp.where(exists("gx", -d), XD[9 - 4 * d:13 - 4 * d], 0.0)
    XD[0] = jnp.where(exists("gx", -3), XD[0], 0.0)
    XD[21] = jnp.where(exists("gx", 3), XD[21], 0.0)

    def coupling2(a, b):
        total = a + b
        return jnp.where(total > 0.0, 2.0 / total, 0.0)

    row2 = iota((20, 8, 128), 1)
    rho = XD[1:21]
    cx2 = coupling2(XD[0:21], XD[1:22])
    y_up = coupling2(rho, jnp.where(row2 == 7, 0.0, pltpu.roll(rho, 7, 1)))
    y_down = coupling2(rho, jnp.where(row2 == 0, 0.0, pltpu.roll(rho, 1, 1)))
    z_up = coupling2(rho, pltpu.roll(rho, 127, 2))
    z_down = coupling2(rho, pltpu.roll(rho, 1, 2))
    diag2 = cx2[0:20] + cx2[1:21] + ((y_up + y_down) + (z_up + z_down))
    inv2 = jnp.where(rho > 0.0, RELAXATION / diag2, 0.0)
    y_up = jnp.where(row2 == 7, 0.0, y_up)
    y_down = jnp.where(row2 == 0, 0.0, y_down)

    settle1(1, w1_faces)
    w = V1[1]
    w2 = KEEP * w[1:9] + inv1 * (b1 + around1(w, *spread_z1(1)))
    w2_faces = stage1(2, jnp.where(own1, w2, 0.0))
    settle1(2, w2_faces)
    w = V1[2]
    w_low, w_high = spread_z1(2)
    r1 = jnp.where(own1, b1 + around1(w, w_low, w_high) - diag1 * w[1:9], 0.0)

    arrived(gather_y2(1, 0.5 * down1(r1)))
    arrived(gather_z2(1))
    XB[8:12] = widen_z2(1)
    arrived([post(XB.at[8:12], XB.at[8 - 4 * d:12 - 4 * d], "gx", d) for d in (-2, -1, 1, 2)])
    for d in (-2, -1, 1, 2):
        XB[8 - 4 * d:12 - 4 * d] = jnp.where(exists("gx", -d), XB[8 - 4 * d:12 - 4 * d], 0.0)
    b2 = XB[...]
    v = inv2 * b2
    for k in range(1, COARSE_SWEEPS):
        a, z = k, 20 - k
        here = v[1:-1]
        total = cx2[a:z] * v[:-2] + cx2[a + 1:z + 1] * v[2:]
        total = total + y_up[a:z] * pltpu.roll(here, 7, 1) + y_down[a:z] * pltpu.roll(here, 1, 1)
        total = total + z_up[a:z] * pltpu.roll(here, 127, 2) + z_down[a:z] * pltpu.roll(here, 1, 2)
        v = KEEP * here + inv2[a:z] * (b2[a:z] + total)

    row6 = iota((6, 8, 128), 1)
    s = pltpu.roll(v, lax.rem(2 - 2 * gy + 8, 8), 1)
    t = jnp.where(row6 <= 2, s, jnp.where(row6 <= 4, pltpu.roll(s, 1, 1), pltpu.roll(s, 2, 1)))
    first = jnp.where(exists("gy", -1), 1, 2)
    last = jnp.where(exists("gy", 1), 6, 5)
    t = jnp.where((row6 >= first) & (row6 <= last), t, 0.0)
    from_lane = iota((128, 384), 0)
    to_lane = iota((128, 384), 1)
    wanted = jnp.where(to_lane < 128, lax.shift_right_logical(to_lane, 1), jnp.where(to_lane < 256, 64, 127))
    t = dot(t.reshape(48, 128), (from_lane == wanted).astype(f32)).reshape(6, 8, 384)
    w3 = V1[2] + jnp.stack([t[j, :, 0:128] for j in (0, 1, 1, 2, 2, 3, 3, 4, 4, 5)])
    w_high = w_high + jnp.stack([t[j, :, 128:256] for j in (1, 1, 2, 2, 3, 3, 4, 4)])
    w_low = w_low + jnp.stack([t[j, :, 256:384] for j in (1, 1, 2, 2, 3, 3, 4, 4)])
    e1 = KEEP * w3[1:9] + inv1 * (b1 + around1(w3, w_low, w_high))
    e1_faces = stage1(3, jnp.where(own1, e1, 0.0))
    settle1(3, e1_faces)

    def grow_y(t, axis):
        row = iota(t.shape, axis)
        up, down = pltpu.roll(t, 7, axis), pltpu.roll(t, 1, axis)
        t = jnp.where((row == 3) | (row == 4), t, jnp.where(row < 3, up, down))
        return jnp.where(row == 0, pltpu.roll(up, 7, axis), jnp.where(row == 7, pltpu.roll(down, 1, axis), t))

    pairs = (iota((128, 256), 0) == lax.shift_right_logical(iota((128, 256), 1), 1)).astype(f32)
    e = dot(V1[3].reshape(80, 128), pairs).reshape(10, 8, 256)
    grown = grow_y(e, 1)
    ez = (grow_y(ZH1[3, 0], 0), grow_y(ZH1[3, 1], 0))
    left(v2_faces)
    V0[2, 0] = V0[2, 0] + grown[0]
    V0[2, 17] = V0[2, 17] + grown[9]
    for i in range(16):
        V0[2, 1 + i] = V0[2, 1 + i] + grown[1 + i // 2]
        YH0[2, 0, i:i + 1, :] = YH0[2, 0, i:i + 1, :] + e[1 + i // 2, 1:2, :]
        YH0[2, 1, i:i + 1, :] = YH0[2, 1, i:i + 1, :] + e[1 + i // 2, 6:7, :]
    for c in chunks:
        v = V0[2, 1 + c:1 + c + CHUNK]
        y_low, y_high, z_low, z_high = halo0(2, c, zh)
        coarse = [jnp.stack([jnp.broadcast_to(side[:, (c + i) // 2:(c + i) // 2 + 1], (8, 256)) for i in range(CHUNK)])
                  for side in ez]
        total = around0(c, V0[2, c:c + CHUNK], V0[2, c + 2:c + 2 + CHUNK],
                        shifts0(v, y_low, y_high, z_low + coarse[0], z_high + coarse[1]))
        out[c:c + CHUNK] = KEEP * v + INV0[c:c + CHUNK] * (src[c:c + CHUNK] + total)

    left([copy for copy in copies if id(copy) not in sent])


def shards(source, phase_mask, density_factor):
    f32 = jnp.float32
    vmem = pl.BlockSpec(memory_space=pltpu.VMEM)
    return pl.pallas_call(
        kernel,
        out_shape=jax.ShapeDtypeStruct((16, 8, 256), f32),
        in_specs=[vmem] * 3,
        out_specs=vmem,
        scratch_shapes=[
            pltpu.VMEM((3, 18, 8, 256), f32),
            pltpu.VMEM((3, 2, 16, 256), f32),
            pltpu.VMEM((3, 2, 16, 256), f32),
            pltpu.VMEM((3, 2, 8, 128), f32),
            pltpu.VMEM((3, 2, 8, 128), f32),
            pltpu.VMEM((17, 8, 256), f32),
            pltpu.VMEM((4, 16, 8, 256), f32),
            pltpu.VMEM((16, 8, 256), f32),
            pltpu.VMEM((16, 8, 256), f32),
            pltpu.VMEM((16, 8, 256), f32),
            pltpu.VMEM((4, 10, 8, 128), f32),
            pltpu.VMEM((4, 2, 8, 128), f32),
            pltpu.VMEM((4, 2, 8, 128), f32),
            pltpu.VMEM((4, 2, 8, 128), f32),
            pltpu.VMEM((4, 2, 8, 128), f32),
            pltpu.VMEM((2, 4, 8, 128), f32),
            pltpu.VMEM((2, 4, 8, 128), f32),
            pltpu.VMEM((2, 2, 4, 8, 128), f32),
            pltpu.VMEM((20, 8, 128), f32),
            pltpu.VMEM((22, 8, 128), f32),
            pltpu.SemaphoreType.DMA((COPIES,)),
            pltpu.SemaphoreType.DMA((COPIES,)),
        ],
        compiler_params=pltpu.CompilerParams(collective_id=0, has_side_effects=True),
        name="vcycle",
    )(source, phase_mask, density_factor)


def solution(mesh):
    spec = P("gx", "gy", "gz")
    return jax.shard_map(shards, mesh=mesh, in_specs=(spec,) * 3, out_specs=spec, check_vma=False)
```

```python
import jax
import jax.numpy as jnp
from jax import lax
from jax.experimental import pallas as pl
from jax.experimental.pallas import tpu as pltpu
from jax.sharding import PartitionSpec as P

GAS_DENSITY = 0.001
RELAXATION = 0.8
KEEP = 1.0 - RELAXATION
COARSE_SWEEPS = 8
MESH = pl.DeviceIdType.MESH
CHUNK = 2
COPIES = 66
TINY = 1e-30
AXES = ("gx", "gy", "gz")
SIDES = [(a, b) for a in (-1, 0, 1) for b in (-1, 0, 1) if a or b]


def iota(shape, axis):
    return lax.broadcasted_iota(jnp.int32, shape, axis)


def dot(a, b):
    high = a.astype(jnp.bfloat16)
    rest = a - high.astype(jnp.float32)
    middle = rest.astype(jnp.bfloat16)
    low = (rest - middle.astype(jnp.float32)).astype(jnp.bfloat16)
    return sum(jnp.dot(part, b, preferred_element_type=jnp.float32) for part in (low, middle, high))


def ones_where(condition):
    return jnp.where(condition, 1.0, 0.0).astype(jnp.bfloat16)


def turn(x, shift, axis):
    shift %= x.shape[axis]
    return pltpu.roll(x, shift, axis) if shift else x


def coupling(a, b):
    return 2.0 / jnp.maximum(a + b, TINY)


def grow(t, axis):
    row = iota(t.shape, axis)
    moved = [t] + [pltpu.roll(t, n, axis) for n in (1, 2, 3, 4)]
    low = jnp.where(row < 1, moved[0], jnp.where(row < 3, moved[1], moved[2]))
    high = jnp.where(row < 5, moved[2], jnp.where(row < 7, moved[3], moved[4]))
    return jnp.where(row < 4, low, high)


def kernel(src, mask, fac, out, V0, SRC, YS0, YH0, ZS, ZH, HX, HY, CX0, C0, INV0, DIAG0,
           S1, H1, RHO1, CX1, C1, INV1, DIAG1, B1, W1, W2, E1, G, GB, XD, send_sem, recv_sem):
    f32 = jnp.float32
    sizes = {axis: lax.axis_size(axis) for axis in AXES}
    at = {axis: lax.axis_index(axis) for axis in AXES}
    gx, gy = at["gx"], at["gy"]

    def peer(way):
        return {axis: lax.rem(at[axis] + (d + sizes[axis]), sizes[axis]) for axis, d in way.items() if d}

    def exists(axis, d):
        place = at[axis] + d
        return (place >= 0) & (place < sizes[axis])

    above, below = exists("gz", 1), exists("gz", -1)
    copies = []

    def ready(source, target, way):
        k = len(copies)
        copy = pltpu.make_async_remote_copy(
            src_ref=source, dst_ref=target, send_sem=send_sem.at[k], recv_sem=recv_sem.at[k],
            device_id=peer(way), device_id_type=MESH)
        copies.append(copy)
        return copy

    def post(source, target, way):
        copy = ready(source, target, way)
        copy.start()
        return copy

    def arrived(group):
        for copy in group:
            copy.wait_recv()

    sent = set()

    def left(group):
        for copy in group:
            copy.wait_send()
            sent.add(id(copy))

    barrier = pltpu.get_barrier_semaphore()
    steady = [{"gx": a, "gy": b} for a in (-2, -1, 0, 1, 2) for b in (0, 1, 2, 3) if a or b] + [{"gx": -3}, {"gx": 3}]
    across = [{}, {"gx": -1}, {"gx": 1}, {"gy": -1}, {"gy": 1}]
    for way in steady:
        pl.semaphore_signal(barrier, inc=1, device_id=peer(way), device_id_type=MESH)
    for d, there in ((-1, below), (1, above)):
        ids = [peer({**way, "gz": d}) for way in across]

        @pl.when(there)
        def _():
            for other in ids:
                pl.semaphore_signal(barrier, inc=1, device_id=other, device_id_type=MESH)

    lane16 = iota((16, 8, 128), 2)
    row0 = iota((CHUNK, 8, 384), 1)
    chunks = range(0, 16, CHUNK)

    def pack_y0(k, c, v):
        n = v.shape[-1]
        for i in range(v.shape[0]):
            YS0[k, 0, c + i:c + i + 1, 0:n] = v[i, 0:1, :]
            YS0[k, 1, c + i:c + i + 1, 0:n] = v[i, 7:8, :]

    def halo0(k, c):
        return [jnp.stack([jnp.broadcast_to(YH0[k, side, c + i:c + i + 1, :], (8, 384)) for i in range(CHUNK)])
                for side in (0, 1)]

    def shifts0(v, y_low, y_high):
        return (jnp.where(row0 == 7, y_high, pltpu.roll(v, 7, 1)), jnp.where(row0 == 0, y_low, pltpu.roll(v, 1, 1)),
                pltpu.roll(v, 383, 2), pltpu.roll(v, 1, 2))

    def around0(k, c):
        v = V0[k, 1 + c:1 + c + CHUNK]
        total = CX0[c:c + CHUNK] * V0[k, c:c + CHUNK] + CX0[c + 1:c + 1 + CHUNK] * V0[k, c + 2:c + 2 + CHUNK]
        for n, other in enumerate(shifts0(v, *halo0(k, c))):
            total = total + C0[n, c:c + CHUNK] * other
        return v, total

    def faces0(k):
        return [post(V0.at[k, 1], V0.at[k, 17], {"gx": -1}), post(V0.at[k, 16], V0.at[k, 0], {"gx": 1}),
                post(YS0.at[k, 0], YH0.at[k, 1], {"gy": -1}), post(YS0.at[k, 1], YH0.at[k, 0], {"gy": 1})]

    def trim0(k):
        V0[k, 0] = jnp.where(exists("gx", -1), V0[k, 0], 0.0)
        V0[k, 17] = jnp.where(exists("gx", 1), V0[k, 17], 0.0)
        YH0[k, 0] = jnp.where(exists("gy", -1), YH0[k, 0], 0.0)
        YH0[k, 1] = jnp.where(exists("gy", 1), YH0[k, 1], 0.0)

    rho = jnp.where(mask[...] == 1, GAS_DENSITY, 1.0) * fac[...]
    V0[0, 1:17, :, 0:256] = rho
    source = src[...]
    ZS[0] = jnp.where(lane16 < 64, rho[:, :, 0:128], pltpu.roll(source[:, :, 0:128], 64, 2))
    ZS[1] = jnp.where(lane16 < 64, pltpu.roll(rho[:, :, 128:256], 64, 2), source[:, :, 128:256])
    pack_y0(0, 0, rho)
    SRC[:, :, 0:256] = source
    two = jnp.where(above, 1, 0) + jnp.where(below, 1, 0)
    pl.semaphore_wait(barrier, len(steady) + len(across) * two)

    low, high = pl.ds(0, 128), pl.ds(128, 128)
    to_below = [ready(ZS.at[0], ZH.at[1], {"gz": -1}),
                ready(V0.at[0, 1, :, low], HX.at[1, 1], {"gx": -1, "gz": -1}),
                ready(V0.at[0, 16, :, low], HX.at[0, 1], {"gx": 1, "gz": -1}),
                ready(YS0.at[0, 0, :, low], HY.at[1, 1], {"gy": -1, "gz": -1}),
                ready(YS0.at[0, 1, :, low], HY.at[0, 1], {"gy": 1, "gz": -1})]
    to_above = [ready(ZS.at[1], ZH.at[0], {"gz": 1}),
                ready(V0.at[0, 1, :, high], HX.at[1, 0], {"gx": -1, "gz": 1}),
                ready(V0.at[0, 16, :, high], HX.at[0, 0], {"gx": 1, "gz": 1}),
                ready(YS0.at[0, 0, :, high], HY.at[1, 0], {"gy": -1, "gz": 1}),
                ready(YS0.at[0, 1, :, high], HY.at[0, 0], {"gy": 1, "gz": 1})]
    for group, there in ((to_below, below), (to_above, above)):
        @pl.when(there)
        def _():
            for copy in group:
                copy.start()
    both = pl.ds(0, 256)
    rho0_faces = [post(V0.at[0, 1, :, both], V0.at[0, 17, :, both], {"gx": -1}),
                  post(V0.at[0, 16, :, both], V0.at[0, 0, :, both], {"gx": 1}),
                  post(YS0.at[0, 0, :, both], YH0.at[0, 1, :, both], {"gy": -1}),
                  post(YS0.at[0, 1, :, both], YH0.at[0, 0, :, both], {"gy": 1})]

    a, b = lax.shift_right_logical(iota((384, 256), 0), 1), iota((384, 256), 1)
    pairs0 = ones_where(b == jnp.where(a < 160, a, a + 64))
    pairs1 = ones_where(lax.shift_right_logical(iota((256, 128), 0), 1) == iota((256, 128), 1))
    a, b = iota((256, 384), 0), lax.shift_right_logical(iota((256, 384), 1), 1)
    spread0 = ones_where(a == jnp.where(b < 160, b, b + 64))
    spread1 = ones_where(iota((128, 256), 0) == lax.shift_right_logical(iota((128, 256), 1), 1))

    arrived(rho0_faces)
    for group, there in ((to_below, above), (to_above, below)):
        @pl.when(there)
        def _():
            arrived(group)
    for group, there in ((to_below, below), (to_above, above)):
        @pl.when(there)
        def _():
            left(group)

    ring = slice(256, 384)
    up, down = jnp.where(above, ZH[1], 0.0), jnp.where(below, ZH[0], 0.0)
    V0[0, 1:17, :, ring] = jnp.where(lane16 < 64, up, pltpu.roll(down, 64, 2))
    SRC[:, :, ring] = jnp.where(lane16 < 64, pltpu.roll(up, 64, 2), down)
    lane8, lane2 = iota((8, 128), 1), iota((16, 128), 1)
    for side in (0, 1):
        V0[0, 17 * side, :, ring] = jnp.where(
            lane8 < 64, jnp.where(above, HX[side, 1], 0.0), jnp.where(below, HX[side, 0], 0.0))
        YH0[0, side, :, ring] = jnp.where(
            lane2 < 64, jnp.where(above, HY[side, 1], 0.0), jnp.where(below, HY[side, 0], 0.0))
    trim0(0)

    for c in range(17):
        CX0[c] = coupling(V0[0, c], V0[0, c + 1])
    for c in chunks:
        rho = V0[0, 1 + c:1 + c + CHUNK]
        diag = CX0[c:c + CHUNK] + CX0[c + 1:c + 1 + CHUNK]
        for n, other in enumerate(shifts0(rho, *halo0(0, c))):
            between = coupling(rho, other)
            C0[n, c:c + CHUNK] = between
            diag = diag + between
        inv = jnp.where(rho > 0.0, RELAXATION / diag, 0.0)
        DIAG0[c:c + CHUNK] = diag
        INV0[c:c + CHUNK] = inv
        v = inv * SRC[c:c + CHUNK]
        V0[1, 1 + c:1 + c + CHUNK] = v
        pack_y0(1, c, v)
    v1_faces = faces0(1)

    row8 = iota((8, 256), 0)
    row8s = iota((8, 128), 0)

    def down0(plane):
        t = jnp.concatenate([plane(2 * p) + plane(2 * p + 1) for p in range(8)], axis=0)
        t = dot(t, pairs0).reshape(8, 8, 256)
        t = t + pltpu.roll(t, 7, 1)
        row = iota((8, 8, 256), 1)
        t = jnp.where(row < 1, t, jnp.where(row < 2, pltpu.roll(t, 7, 1), jnp.where(row < 3, pltpu.roll(t, 6, 1), pltpu.roll(t, 5, 1))))
        return [jnp.where(row8 < 4, t[2 * j], pltpu.roll(t[2 * j + 1], 4, 0)) for j in range(4)]

    def slot(a, b):
        return SIDES.index((a, b))

    def exchange1(k, packed):
        for j in range(4):
            S1[k, j] = packed[j]
        group = []
        for a, b in ((1, 0), (-1, 0), (0, 1), (0, -1), (1, 1), (1, -1), (-1, 1), (-1, -1)):
            some = {1: pl.ds(2, 2), -1: pl.ds(0, 2), 0: pl.ds(0, 4)}[a]
            group.append(post(S1.at[k, some], H1.at[k, slot(-a, -b), some], {"gx": a, "gy": b}))
        return group

    def unpack1(k, target, first, last, offset):
        for p in range(first, last):
            a = p // 8
            j, half = (p % 8) // 2, p % 2

            def block(b):
                if not a and not b:
                    return S1[k, j]
                return jnp.where(exists("gx", a) & exists("gy", b), H1[k, slot(a, b), j], 0.0)

            target[p - offset, 0:8] = jnp.where(row8 < 4, turn(block(0), -4 * half, 0), turn(block(1), 4 - 4 * half, 0))
            target[p - offset, 8:16] = jnp.where(row8 < 4, 0.0, turn(block(-1), 4 - 4 * half, 0))

    def shifts1(v):
        return pltpu.roll(v, 15, 0), pltpu.roll(v, 1, 0), pltpu.roll(v, 255, 1), pltpu.roll(v, 1, 1)

    def around1(V, p, base):
        v = V[p - base]
        total = CX1[p + 3] * V[p - 1 - base] + CX1[p + 4] * V[p + 1 - base]
        for n, other in enumerate(shifts1(v)):
            total = total + C1[n, p + 3] * other
        return v, total

    def down1(plane):
        packed = jnp.zeros((8, 256), f32)
        for x in range(4):
            t = plane(2 * x) + plane(2 * x + 1)
            t = t + pltpu.roll(t, 7, 0)
            for half in range(2):
                packed = jnp.where(row8 == 2 * x + half, turn(t, 2 * x - half, 0), packed)
        return dot(packed, pairs1)

    packed1 = [0.125 * t for t in down0(lambda p: V0[0, 1 + p])]
    rho1_copies = exchange1(0, packed1)
    G[gy] = 0.125 * down1(lambda p: packed1[p // 2] if p % 2 == 0 else pltpu.roll(packed1[p // 2], 4, 0))
    rho2_y = [post(G.at[gy], G.at[gy], {"gy": d}) for d in (1, 2, 3)]

    arrived(v1_faces)
    trim0(1)
    for c in chunks:
        v, total = around0(1, c)
        v = KEEP * v + INV0[c:c + CHUNK] * (SRC[c:c + CHUNK] + total)
        V0[2, 1 + c:1 + c + CHUNK] = v
        pack_y0(2, c, v)
    v2_faces = faces0(2)

    def rows_of(blocks):
        planes = []
        for x in range(4):
            t = turn(blocks[0], -2 * x, 0)
            for q in (1, 2, 3):
                t = jnp.where(row8s < 2 * q, t, turn(blocks[q], 2 * (q - x), 0))
            planes.append(t)
        return planes

    arrived(rho2_y)
    for x, t in enumerate(rows_of([G[q] for q in range(4)])):
        XD[9 + x] = t
    rho2_x = [post(XD.at[9:13], XD.at[9 - 4 * d:13 - 4 * d], {"gx": d}) for d in (-2, -1, 1, 2)]
    rho2_x += [post(XD.at[12], XD.at[0], {"gx": 3}), post(XD.at[9], XD.at[21], {"gx": -3})]

    arrived(rho1_copies)
    unpack1(0, RHO1, -4, 12, -4)
    for p in range(-3, 12):
        CX1[p + 3] = coupling(RHO1[p + 3], RHO1[p + 4])
    for p in range(-3, 11):
        rho = RHO1[p + 4]
        diag = CX1[p + 3] + CX1[p + 4]
        for n, other in enumerate(shifts1(rho)):
            between = coupling(rho, other)
            C1[n, p + 3] = between
            diag = diag + between
        INV1[p + 3] = jnp.where(rho > 0.0, RELAXATION / diag, 0.0)
        if 0 <= p < 8:
            DIAG1[p] = diag

    arrived(v2_faces)
    trim0(2)
    residual = []
    for c in chunks:
        v, total = around0(2, c)
        residual += list(SRC[c:c + CHUNK] + total - DIAG0[c:c + CHUNK] * v)
    b1_copies = exchange1(1, [0.5 * t for t in down0(lambda p: residual[p])])

    arrived(rho2_x)
    for d in (-2, -1, 1, 2):
        XD[9 - 4 * d:13 - 4 * d] = jnp.where(exists("gx", -d), XD[9 - 4 * d:13 - 4 * d], 0.0)
    XD[0] = jnp.where(exists("gx", -3), XD[0], 0.0)
    XD[21] = jnp.where(exists("gx", 3), XD[21], 0.0)
    row2 = iota((20, 8, 128), 1)
    rho = XD[1:21]
    cx2 = coupling(XD[0:21], XD[1:22])
    y_up = coupling(rho, jnp.where(row2 == 7, 0.0, pltpu.roll(rho, 7, 1)))
    y_down = coupling(rho, jnp.where(row2 == 0, 0.0, pltpu.roll(rho, 1, 1)))
    z_up = coupling(rho, pltpu.roll(rho, 127, 2))
    z_down = coupling(rho, pltpu.roll(rho, 1, 2))
    diag2 = cx2[0:20] + cx2[1:21] + ((y_up + y_down) + (z_up + z_down))
    inv2 = jnp.where(rho > 0.0, RELAXATION / diag2, 0.0)
    y_up = jnp.where(row2 == 7, 0.0, y_up)
    y_down = jnp.where(row2 == 0, 0.0, y_down)

    arrived(b1_copies)
    unpack1(1, B1, -3, 11, -3)
    for p in range(-3, 11):
        W1[p + 3] = INV1[p + 3] * B1[p + 3]
    for p in range(-2, 10):
        v, total = around1(W1, p, -3)
        W2[p + 2] = KEEP * v + INV1[p + 3] * (B1[p + 3] + total)
    residual = []
    for p in range(8):
        v, total = around1(W2, p, -2)
        residual.append((B1[p + 3] + total - DIAG1[p] * v)[0:8])

    GB[2, gy] = 0.5 * down1(lambda p: residual[p])
    b2_copies = [post(GB.at[2, gy], GB.at[2 - d, gy], {"gx": d, "gy": e})
                 for d in (0, 1, -1, 2, -2) for e in (1, 2, 3, 0) if d or e]
    arrived(b2_copies)
    planes = []
    for d in (-2, -1, 0, 1, 2):
        planes += [jnp.where(exists("gx", d), t, 0.0) if d else t for t in rows_of([GB[2 + d, q] for q in range(4)])]
    b2 = jnp.stack(planes)
    v = inv2 * b2
    for k in range(1, COARSE_SWEEPS):
        z = 20 - k
        here = v[1:-1]
        total = cx2[k:z] * v[:-2] + cx2[k + 1:z + 1] * v[2:]
        total = total + y_up[k:z] * pltpu.roll(here, 7, 1) + y_down[k:z] * pltpu.roll(here, 1, 1)
        total = total + z_up[k:z] * pltpu.roll(here, 127, 2) + z_down[k:z] * pltpu.roll(here, 1, 2)
        v = KEEP * here + inv2[k:z] * (b2[k:z] + total)

    row6 = iota((6, 8, 128), 1)
    t = pltpu.roll(v, lax.rem(8 - 2 * gy, 8), 1)
    own = jnp.where(row6 < jnp.where(exists("gy", 1), 8, 4), grow(t, 1), 0.0)
    under = jnp.where(row6 >= jnp.where(exists("gy", -1), 6, 8), jnp.where(row6 == 7, t, pltpu.roll(t, 7, 1)), 0.0)
    t = dot(jnp.concatenate([own, under], axis=1).reshape(96, 128), spread1).reshape(6, 16, 256)
    for p in range(-2, 10):
        W2[p + 2] = W2[p + 2] + t[p // 2 + 1]
    for p in range(-1, 9):
        v, total = around1(W2, p, -2)
        E1[p + 1] = KEEP * v + INV1[p + 3] * (B1[p + 3] + total)

    y_low = jnp.zeros((8, 256), f32)
    y_high = y_low
    for p in range(8):
        y_low = jnp.where(row8 == p, turn(E1[p + 1, 8:16], p - 7, 0), y_low)
        y_high = jnp.where(row8 == p, turn(E1[p + 1, 0:8], p - 4, 0), y_high)
    parts = [grow(E1[p, 0:8], 0) for p in range(10)]
    for t in (y_low, y_high):
        parts += [grow(t, 0), grow(pltpu.roll(t, 4, 0), 0)]
    e = dot(jnp.concatenate(parts, axis=0), spread0)
    left(v2_faces)
    for p in range(18):
        n = (p + 1) // 2
        V0[2, p] = V0[2, p] + e[8 * n:8 * n + 8]
    YH0[2, 0] = YH0[2, 0] + e[80:96]
    YH0[2, 1] = YH0[2, 1] + e[96:112]
    for c in chunks:
        v, total = around0(2, c)
        v = KEEP * v + INV0[c:c + CHUNK] * (SRC[c:c + CHUNK] + total)
        out[c:c + CHUNK] = v[:, :, 0:256]

    done = {id(copy) for copy in to_below + to_above}
    left([copy for copy in copies if id(copy) not in sent | done])


def shards(source, phase_mask, density_factor):
    f32 = jnp.float32
    vmem = pl.BlockSpec(memory_space=pltpu.VMEM)
    shapes = [
        (3, 18, 8, 384), (16, 8, 384), (3, 2, 16, 384), (3, 2, 16, 384), (2, 16, 8, 128), (2, 16, 8, 128),
        (2, 2, 8, 128), (2, 2, 16, 128), (17, 8, 384), (4, 16, 8, 384), (16, 8, 384), (16, 8, 384),
        (2, 4, 8, 256), (2, 8, 4, 8, 256), (16, 16, 256), (15, 16, 256), (4, 14, 16, 256), (14, 16, 256), (8, 16, 256),
        (14, 16, 256), (14, 16, 256), (12, 16, 256), (10, 16, 256), (4, 8, 128), (5, 4, 8, 128), (22, 8, 128),
    ]
    return pl.pallas_call(
        kernel,
        out_shape=jax.ShapeDtypeStruct((16, 8, 256), f32),
        in_specs=[vmem] * 3,
        out_specs=vmem,
        scratch_shapes=[pltpu.VMEM(shape, f32) for shape in shapes] + [pltpu.SemaphoreType.DMA((COPIES,))] * 2,
        compiler_params=pltpu.CompilerParams(collective_id=0, has_side_effects=True),
        name="vcycle",
    )(source, phase_mask, density_factor)


def solution(mesh):
    spec = P("gx", "gy", "gz")
    return jax.shard_map(shards, mesh=mesh, in_specs=(spec,) * 3, out_specs=spec, check_vma=False)
```

```python
import jax
import jax.numpy as jnp
from jax import lax
from jax.experimental import pallas as pl
from jax.experimental.pallas import tpu as pltpu
from jax.sharding import PartitionSpec as P

GAS_DENSITY = 0.001
RELAXATION = 0.8
KEEP = 1.0 - RELAXATION
COARSE_SWEEPS = 8
MESH = pl.DeviceIdType.MESH
CHUNK = 2
COPIES = 68
TINY = 1e-30
AXES = ("gx", "gy", "gz")
SIDES = [(a, b) for a in (-1, 0, 1) for b in (-1, 0, 1) if a or b]


def iota(shape, axis):
    return lax.broadcasted_iota(jnp.int32, shape, axis)


def dot(a, b):
    high = a.astype(jnp.bfloat16)
    rest = a - high.astype(jnp.float32)
    middle = rest.astype(jnp.bfloat16)
    low = (rest - middle.astype(jnp.float32)).astype(jnp.bfloat16)
    return sum(jnp.dot(part, b, preferred_element_type=jnp.float32) for part in (low, middle, high))


def ones_where(condition):
    return jnp.where(condition, 1.0, 0.0).astype(jnp.bfloat16)


def turn(x, shift, axis):
    shift %= x.shape[axis]
    return pltpu.roll(x, shift, axis) if shift else x


def coupling(a, b):
    return 2.0 / jnp.maximum(a + b, TINY)


def grow(t, axis):
    row = iota(t.shape, axis)
    moved = [t] + [pltpu.roll(t, n, axis) for n in (1, 2, 3, 4)]
    low = jnp.where(row < 1, moved[0], jnp.where(row < 3, moved[1], moved[2]))
    high = jnp.where(row < 5, moved[2], jnp.where(row < 7, moved[3], moved[4]))
    return jnp.where(row < 4, low, high)


def kernel(src_in, mask_in, fac_in, out, src, mask, fac, in_sem, V0, SRC, YS0, YH0, ZS, ZH, HX, HY, CX0, C0, CB0, KB0, INV0, DIAG0, R0,
           S1, H1, RHO1, CX1, C1, INV1, DIAG1, B1, W1, W2, E1, G, GB, XD, send_sem, recv_sem):
    f32 = jnp.float32
    sizes = {axis: lax.axis_size(axis) for axis in AXES}
    at = {axis: lax.axis_index(axis) for axis in AXES}
    gx, gy = at["gx"], at["gy"]

    def peer(way):
        return {axis: lax.rem(at[axis] + (d + sizes[axis]), sizes[axis]) for axis, d in way.items() if d}

    def exists(axis, d):
        place = at[axis] + d
        return (place >= 0) & (place < sizes[axis])

    above, below = exists("gz", 1), exists("gz", -1)
    copies = []

    def ready(source, target, way):
        k = len(copies)
        copy = pltpu.make_async_remote_copy(
            src_ref=source, dst_ref=target, send_sem=send_sem.at[k], recv_sem=recv_sem.at[k],
            device_id=peer(way), device_id_type=MESH)
        copies.append(copy)
        return copy

    def post(source, target, way):
        copy = ready(source, target, way)
        copy.start()
        return copy

    def arrived(group):
        for copy in group:
            copy.wait_recv()

    def left(group):
        for copy in group:
            copy.wait_send()

    inputs = [pltpu.make_async_copy(a, b, in_sem.at[n]) for n, (a, b) in enumerate(((fac_in, fac), (mask_in, mask), (src_in, src)))]
    for copy in inputs:
        copy.start()

    barrier = pltpu.get_barrier_semaphore()
    steady = [{"gx": a, "gy": b} for a in (0, -1, 1, -2, 2) for b in (0, 1, 3, 2) if a or b] + [{"gx": -3}, {"gx": 3}]
    across = [{}, {"gx": -1}, {"gx": 1}, {"gy": -1}, {"gy": 1}]
    for d, there in ((-1, below), (1, above)):
        ids = [peer({**way, "gz": d}) for way in across]

        @pl.when(there)
        def _():
            for other in ids:
                pl.semaphore_signal(barrier, inc=1, device_id=other, device_id_type=MESH)
    for way in steady:
        pl.semaphore_signal(barrier, inc=1, device_id=peer(way), device_id_type=MESH)

    lane16 = iota((8, 8, 128), 2)
    chunks = range(0, 16, CHUNK)
    own, ring = slice(0, 256), slice(256, 384)

    def pack_y0(k, c, v):
        n = v.shape[-1]
        for i in range(v.shape[0]):
            YS0[k, 0, c + i:c + i + 1, 0:n] = v[i, 0:1, :]
            YS0[k, 1, c + i:c + i + 1, 0:n] = v[i, 7:8, :]

    def outer(k, c, lanes=slice(0, 384)):
        shape = (8, lanes.stop - lanes.start)
        first = iota(shape, 0) < 4
        return jnp.stack([jnp.where(first, jnp.broadcast_to(YH0[k, 0, c + i:c + i + 1, lanes], shape),
                                    jnp.broadcast_to(YH0[k, 1, c + i:c + i + 1, lanes], shape)) for i in range(CHUNK)])

    def inner(k, c):
        v = V0[k, 1 + c:1 + c + CHUNK]
        parts = []
        for i in range(c, c + CHUNK):
            terms = ([CX0[i] * V0[k, i]] if i else []) + ([CX0[i + 1] * V0[k, i + 2]] if i < 15 else [])
            parts.append(sum(terms[1:], terms[0]))
        total = jnp.stack(parts) + C0[0, c:c + CHUNK] * pltpu.roll(v, 7, 1) + C0[1, c:c + CHUNK] * pltpu.roll(v, 1, 1)
        return v, total + C0[2, c:c + CHUNK] * pltpu.roll(v, 383, 2) + C0[3, c:c + CHUNK] * pltpu.roll(v, 1, 2)

    def ends(k, c):
        return {i: CX0[i + (i == 15)] * V0[k, 17 if i else 0] for i in (0, 15) if c <= i < c + CHUNK}

    def faces0(k):
        return [post(V0.at[k, 1], V0.at[k, 17], {"gx": -1}), post(V0.at[k, 16], V0.at[k, 0], {"gx": 1}),
                post(YS0.at[k, 0], YH0.at[k, 1], {"gy": -1}), post(YS0.at[k, 1], YH0.at[k, 0], {"gy": 1})]

    def trim0(k, lanes=slice(0, 384)):
        for side, d in ((0, -1), (1, 1)):
            V0[k, 17 * side, :, lanes] = jnp.where(exists("gx", d), V0[k, 17 * side, :, lanes], 0.0)
            YH0[k, side, :, lanes] = jnp.where(exists("gy", d), YH0[k, side, :, lanes], 0.0)

    def pack_z0(n, field):
        low, high = field[:, :, 0:128], field[:, :, 128:256]
        ZS[n, 0] = jnp.where(lane16 < 64, low[0:8], pltpu.roll(low[8:16], 64, 2))
        ZS[n, 1] = jnp.where(lane16 < 64, pltpu.roll(high[0:8], 64, 2), high[8:16])

    def unpack_z0(n):
        up, down = jnp.where(above, ZH[n, 1], 0.0), jnp.where(below, ZH[n, 0], 0.0)
        return (jnp.where(lane16 < 64, up, pltpu.roll(down, 64, 2)), jnp.where(lane16 < 64, pltpu.roll(up, 64, 2), down))

    inputs[0].wait()
    inputs[1].wait()
    rho = jnp.where(mask[...] == 1, GAS_DENSITY, 1.0) * fac[...]
    V0[0, 1:17, :, own] = rho
    pack_z0(0, rho)
    pack_y0(0, 0, rho)
    inputs[2].wait()
    pack_z0(1, src[...])
    two = jnp.where(above, 1, 0) + jnp.where(below, 1, 0)
    pl.semaphore_wait(barrier, len(steady) + len(across) * two)

    low, high = pl.ds(0, 128), pl.ds(128, 128)
    to_below = [ready(ZS.at[0, 0], ZH.at[0, 1], {"gz": -1}),
                ready(V0.at[0, 1, :, low], HX.at[1, 1], {"gx": -1, "gz": -1}),
                ready(V0.at[0, 16, :, low], HX.at[0, 1], {"gx": 1, "gz": -1}),
                ready(YS0.at[0, 0, :, low], HY.at[1, 1], {"gy": -1, "gz": -1}),
                ready(YS0.at[0, 1, :, low], HY.at[0, 1], {"gy": 1, "gz": -1}),
                ready(ZS.at[1, 0], ZH.at[1, 1], {"gz": -1})]
    to_above = [ready(ZS.at[0, 1], ZH.at[0, 0], {"gz": 1}),
                ready(V0.at[0, 1, :, high], HX.at[1, 0], {"gx": -1, "gz": 1}),
                ready(V0.at[0, 16, :, high], HX.at[0, 0], {"gx": 1, "gz": 1}),
                ready(YS0.at[0, 0, :, high], HY.at[1, 0], {"gy": -1, "gz": 1}),
                ready(YS0.at[0, 1, :, high], HY.at[0, 0], {"gy": 1, "gz": 1}),
                ready(ZS.at[1, 1], ZH.at[1, 0], {"gz": 1})]
    for group, there in ((to_below, below), (to_above, above)):
        @pl.when(there)
        def _():
            for copy in group:
                copy.start()
    both = pl.ds(0, 256)
    rho0_faces = [post(V0.at[0, 1, :, both], V0.at[0, 17, :, both], {"gx": -1}),
                  post(V0.at[0, 16, :, both], V0.at[0, 0, :, both], {"gx": 1}),
                  post(YS0.at[0, 0, :, both], YH0.at[0, 1, :, both], {"gy": -1}),
                  post(YS0.at[0, 1, :, both], YH0.at[0, 0, :, both], {"gy": 1})]

    a, b = lax.shift_right_logical(iota((384, 256), 0), 1), iota((384, 256), 1)
    pairs0 = ones_where(b == jnp.where(a < 160, a, a + 64))
    pairs1 = ones_where(lax.shift_right_logical(iota((256, 128), 0), 1) == iota((256, 128), 1))
    a, b = iota((256, 384), 0), lax.shift_right_logical(iota((256, 384), 1), 1)
    spread0 = ones_where(a == jnp.where(b < 160, b, b + 64))
    spread1 = ones_where(iota((128, 256), 0) == lax.shift_right_logical(iota((128, 256), 1), 1))

    def couple0(lanes, planes):
        for c in planes:
            CX0[c, :, lanes] = coupling(V0[0, c, :, lanes], V0[0, c + 1, :, lanes])

    def couple0_y(lanes):
        for c in chunks:
            rho = V0[0, 1 + c:1 + c + CHUNK, :, lanes]
            between = jnp.where(iota(rho.shape, 1) == 7, 0.0, coupling(rho, pltpu.roll(rho, 7, 1)))
            C0[0, c:c + CHUNK, :, lanes] = between
            C0[1, c:c + CHUNK, :, lanes] = pltpu.roll(between, 1, 1)

    def couple0_ends(lanes):
        for c in chunks:
            rho = V0[0, 1 + c:1 + c + CHUNK, :, lanes]
            row = iota(rho.shape, 1)
            CB0[c:c + CHUNK, :, lanes] = jnp.where((row == 0) | (row == 7), coupling(rho, outer(0, c, lanes)), 0.0)

    SRC[:, :, own] = src[...]
    couple0(own, range(1, 16))
    couple0_y(own)
    arrived(rho0_faces)
    trim0(0, own)
    couple0(own, (0, 16))
    couple0_ends(own)
    for group, there in ((to_below, above), (to_above, below)):
        @pl.when(there)
        def _():
            arrived(group[:5])
    first, second = unpack_z0(0)
    V0[0, 1:9, :, ring] = first
    V0[0, 9:17, :, ring] = second
    lane8, lane2 = iota((8, 128), 1), iota((16, 128), 1)
    for side in (0, 1):
        V0[0, 17 * side, :, ring] = jnp.where(
            lane8 < 64, jnp.where(above, HX[side, 1], 0.0), jnp.where(below, HX[side, 0], 0.0))
        YH0[0, side, :, ring] = jnp.where(
            lane2 < 64, jnp.where(above, HY[side, 1], 0.0), jnp.where(below, HY[side, 0], 0.0))
    trim0(0, ring)
    couple0(ring, range(17))
    couple0_y(ring)
    couple0_ends(ring)
    for c in chunks:
        some = slice(c, c + CHUNK)
        rho = V0[0, 1 + c:1 + c + CHUNK]
        between = coupling(rho, pltpu.roll(rho, 383, 2))
        after = pltpu.roll(between, 1, 2)
        C0[2, some] = between
        C0[3, some] = after
        diag = (CX0[some] + CX0[c + 1:c + 1 + CHUNK]) + (between + after) + (C0[0, some] + C0[1, some] + CB0[some])
        DIAG0[some] = diag
        INV0[some] = jnp.where(rho > 0.0, RELAXATION / diag, 0.0)
    for group, there in ((to_below, above), (to_above, below)):
        @pl.when(there)
        def _():
            arrived(group[5:])
    first, second = unpack_z0(1)
    SRC[0:8, :, ring] = first
    SRC[8:16, :, ring] = second

    for c in chunks:
        v = INV0[c:c + CHUNK] * SRC[c:c + CHUNK]
        V0[1, 1 + c:1 + c + CHUNK] = v
        pack_y0(1, c, v)
    v1_faces = faces0(1)
    for group, there in ((to_below, below), (to_above, above)):
        @pl.when(there)
        def _():
            left(group)
    for c in chunks:
        some = slice(c, c + CHUNK)
        v, total = inner(1, c)
        V0[2, 1 + c:1 + c + CHUNK] = KEEP * v + INV0[some] * (SRC[some] + total)
        KB0[some] = INV0[some] * CB0[some]

    row8 = iota((8, 256), 0)
    row8s = iota((8, 128), 0)

    def down0(plane):
        t = jnp.concatenate([plane(2 * p) + plane(2 * p + 1) for p in range(8)], axis=0)
        t = dot(t, pairs0).reshape(8, 8, 256)
        t = t + pltpu.roll(t, 7, 1)
        row = iota((8, 8, 256), 1)
        t = jnp.where(row < 1, t, jnp.where(row < 2, pltpu.roll(t, 7, 1), jnp.where(row < 3, pltpu.roll(t, 6, 1), pltpu.roll(t, 5, 1))))
        return [jnp.where(row8 < 4, t[2 * j], pltpu.roll(t[2 * j + 1], 4, 0)) for j in range(4)]

    def slot(a, b):
        return SIDES.index((a, b))

    def exchange1(k, packed):
        for j in range(4):
            S1[k, j] = packed[j]
        group = []
        for a, b in ((1, 0), (-1, 0), (0, 1), (0, -1), (1, 1), (1, -1), (-1, 1), (-1, -1)):
            some = {1: pl.ds(2, 2), -1: pl.ds(0, 2), 0: pl.ds(0, 4)}[a]
            if k and a and b:
                some = pl.ds(3 if a > 0 else 0, 1)
            group.append(post(S1.at[k, some], H1.at[k, slot(-a, -b), some], {"gx": a, "gy": b}))
        return group

    def unpack1(k, target, first, last, offset):
        for p in range(first, last):
            a = p // 8
            j, half = (p % 8) // 2, p % 2

            def block(b):
                if not a and not b:
                    return S1[k, j]
                if k and a and b and j in (1, 2):
                    return jnp.zeros((8, 256), f32)
                return jnp.where(exists("gx", a) & exists("gy", b), H1[k, slot(a, b), j], 0.0)

            target[p - offset, 0:8] = jnp.where(row8 < 4, turn(block(0), -4 * half, 0), turn(block(1), 4 - 4 * half, 0))
            target[p - offset, 8:16] = jnp.where(row8 < 4, 0.0, turn(block(-1), 4 - 4 * half, 0))

    def shifts1(v):
        return pltpu.roll(v, 15, 0), pltpu.roll(v, 1, 0), pltpu.roll(v, 255, 1), pltpu.roll(v, 1, 1)

    def around1(V, p, base):
        v = V[p - base]
        total = CX1[p + 3] * V[p - 1 - base] + CX1[p + 4] * V[p + 1 - base]
        for n, other in enumerate(shifts1(v)):
            total = total + C1[n, p + 3] * other
        return v, total

    def down1(plane):
        packed = jnp.zeros((8, 256), f32)
        for x in range(4):
            t = plane(2 * x) + plane(2 * x + 1)
            t = t + pltpu.roll(t, 7, 0)
            for half in range(2):
                packed = jnp.where(row8 == 2 * x + half, turn(t, 2 * x - half, 0), packed)
        return dot(packed, pairs1)

    packed1 = [0.125 * t for t in down0(lambda p: V0[0, 1 + p])]
    rho1_copies = exchange1(0, packed1)
    G[gy] = 0.125 * down1(lambda p: packed1[p // 2] if p % 2 == 0 else pltpu.roll(packed1[p // 2], 4, 0))
    rho2_y = [post(G.at[gy], G.at[gy], {"gy": d}) for d in (1, 2, 3)]

    arrived(v1_faces)
    trim0(1)
    for c in chunks:
        for i, term in ends(1, c).items():
            V0[2, 1 + i] = V0[2, 1 + i] + INV0[i] * term
        v = V0[2, 1 + c:1 + c + CHUNK] + KB0[c:c + CHUNK] * outer(1, c)
        V0[2, 1 + c:1 + c + CHUNK] = v
        pack_y0(2, c, v)
    v2_faces = faces0(2)
    for c in chunks:
        v, total = inner(2, c)
        R0[c:c + CHUNK] = SRC[c:c + CHUNK] + total - DIAG0[c:c + CHUNK] * v

    def rows_of(blocks):
        planes = []
        for x in range(4):
            t = turn(blocks[0], -2 * x, 0)
            for q in (1, 2, 3):
                t = jnp.where(row8s < 2 * q, t, turn(blocks[q], 2 * (q - x), 0))
            planes.append(t)
        return planes

    arrived(rho2_y)
    for x, t in enumerate(rows_of([G[q] for q in range(4)])):
        XD[9 + x] = t
    rho2_x = [post(XD.at[9:13], XD.at[9 - 4 * d:13 - 4 * d], {"gx": d}) for d in (-2, -1, 1, 2)]
    rho2_x += [post(XD.at[12], XD.at[0], {"gx": 3}), post(XD.at[9], XD.at[21], {"gx": -3})]

    arrived(rho1_copies)
    unpack1(0, RHO1, -4, 12, -4)
    for p in range(-3, 12):
        CX1[p + 3] = coupling(RHO1[p + 3], RHO1[p + 4])
    for p in range(-3, 11):
        rho = RHO1[p + 4]
        diag = CX1[p + 3] + CX1[p + 4]
        for n, other in enumerate(shifts1(rho)):
            between = coupling(rho, other)
            C1[n, p + 3] = between
            diag = diag + between
        INV1[p + 3] = jnp.where(rho > 0.0, RELAXATION / diag, 0.0)
        if 0 <= p < 8:
            DIAG1[p] = diag

    arrived(v2_faces)
    trim0(2)
    residual = []
    for c in chunks:
        r = R0[c:c + CHUNK] + CB0[c:c + CHUNK] * outer(2, c)
        more = ends(2, c)
        residual += [r[i] + more[c + i] if c + i in more else r[i] for i in range(CHUNK)]
    b1_copies = exchange1(1, [0.5 * t for t in down0(lambda p: residual[p])])

    arrived(rho2_x)
    for d in (-2, -1, 1, 2):
        XD[9 - 4 * d:13 - 4 * d] = jnp.where(exists("gx", -d), XD[9 - 4 * d:13 - 4 * d], 0.0)
    XD[0] = jnp.where(exists("gx", -3), XD[0], 0.0)
    XD[21] = jnp.where(exists("gx", 3), XD[21], 0.0)
    row2 = iota((20, 8, 128), 1)
    rho = XD[1:21]
    cx2 = coupling(XD[0:21], XD[1:22])
    y_up = coupling(rho, jnp.where(row2 == 7, 0.0, pltpu.roll(rho, 7, 1)))
    y_down = coupling(rho, jnp.where(row2 == 0, 0.0, pltpu.roll(rho, 1, 1)))
    z_up = coupling(rho, pltpu.roll(rho, 127, 2))
    z_down = coupling(rho, pltpu.roll(rho, 1, 2))
    diag2 = cx2[0:20] + cx2[1:21] + ((y_up + y_down) + (z_up + z_down))
    inv2 = jnp.where(rho > 0.0, RELAXATION / diag2, 0.0)
    y_up = jnp.where(row2 == 7, 0.0, y_up)
    y_down = jnp.where(row2 == 0, 0.0, y_down)

    arrived(b1_copies)
    unpack1(1, B1, -3, 11, -3)
    for p in range(-3, 11):
        W1[p + 3] = INV1[p + 3] * B1[p + 3]
    for p in range(-2, 10):
        v, total = around1(W1, p, -3)
        W2[p + 2] = KEEP * v + INV1[p + 3] * (B1[p + 3] + total)
    residual = []
    for p in range(8):
        v, total = around1(W2, p, -2)
        residual.append((B1[p + 3] + total - DIAG1[p] * v)[0:8])

    GB[2, gy] = 0.5 * down1(lambda p: residual[p])
    b2_copies = [post(GB.at[2, gy], GB.at[2 - d, gy], {"gx": d, "gy": e})
                 for e in (2, 1, 3, 0) for d in (2, -2, 1, -1, 0) if d or e]
    late = {id(copy) for copy in b2_copies + to_below + to_above}
    left([copy for copy in copies if id(copy) not in late])
    arrived(b2_copies)
    planes = []
    for d in (-2, -1, 0, 1, 2):
        planes += [jnp.where(exists("gx", d), t, 0.0) if d else t for t in rows_of([GB[2 + d, q] for q in range(4)])]
    b2 = jnp.stack(planes)
    v = inv2 * b2
    for k in range(1, COARSE_SWEEPS):
        z = 20 - k
        here = v[1:-1]
        total = cx2[k:z] * v[:-2] + cx2[k + 1:z + 1] * v[2:]
        total = total + y_up[k:z] * pltpu.roll(here, 7, 1) + y_down[k:z] * pltpu.roll(here, 1, 1)
        total = total + z_up[k:z] * pltpu.roll(here, 127, 2) + z_down[k:z] * pltpu.roll(here, 1, 2)
        v = KEEP * here + inv2[k:z] * (b2[k:z] + total)

    row6 = iota((6, 8, 128), 1)
    t = pltpu.roll(v, lax.rem(8 - 2 * gy, 8), 1)
    over = jnp.where(row6 < jnp.where(exists("gy", 1), 8, 4), grow(t, 1), 0.0)
    under = jnp.where(row6 >= jnp.where(exists("gy", -1), 6, 8), jnp.where(row6 == 7, t, pltpu.roll(t, 7, 1)), 0.0)
    t = dot(jnp.concatenate([over, under], axis=1).reshape(96, 128), spread1).reshape(6, 16, 256)
    for p in range(-2, 10):
        W2[p + 2] = W2[p + 2] + t[p // 2 + 1]
    for p in range(-1, 9):
        v, total = around1(W2, p, -2)
        E1[p + 1] = KEEP * v + INV1[p + 3] * (B1[p + 3] + total)

    y_low = jnp.zeros((8, 256), f32)
    y_high = y_low
    for p in range(8):
        y_low = jnp.where(row8 == p, turn(E1[p + 1, 8:16], p - 7, 0), y_low)
        y_high = jnp.where(row8 == p, turn(E1[p + 1, 0:8], p - 4, 0), y_high)
    parts = [grow(E1[p, 0:8], 0) for p in range(10)]
    for t in (y_low, y_high):
        parts += [grow(t, 0), grow(pltpu.roll(t, 4, 0), 0)]
    e = dot(jnp.concatenate(parts, axis=0), spread0)
    for p in range(18):
        n = (p + 1) // 2
        V0[2, p] = V0[2, p] + e[8 * n:8 * n + 8]
    YH0[2, 0] = YH0[2, 0] + e[80:96]
    YH0[2, 1] = YH0[2, 1] + e[96:112]
    for c in chunks:
        v, total = inner(2, c)
        more = ends(2, c)
        total = total + CB0[c:c + CHUNK] * outer(2, c)
        total = jnp.stack([total[i] + more[c + i] if c + i in more else total[i] for i in range(CHUNK)])
        v = KEEP * v + INV0[c:c + CHUNK] * (SRC[c:c + CHUNK] + total)
        out[c:c + CHUNK] = v[:, :, own]

    left(b2_copies)


def shards(source, phase_mask, density_factor):
    f32 = jnp.float32
    shapes = [
        (3, 18, 8, 384), (16, 8, 384), (3, 2, 16, 384), (3, 2, 16, 384), (2, 2, 8, 8, 128), (2, 2, 8, 8, 128),
        (2, 2, 8, 128), (2, 2, 16, 128), (17, 8, 384), (4, 16, 8, 384), (16, 8, 384), (16, 8, 384),
        (16, 8, 384), (16, 8, 384), (16, 8, 384),
        (2, 4, 8, 256), (2, 8, 4, 8, 256), (16, 16, 256), (15, 16, 256), (4, 14, 16, 256), (14, 16, 256), (8, 16, 256),
        (14, 16, 256), (14, 16, 256), (12, 16, 256), (10, 16, 256), (4, 8, 128), (5, 4, 8, 128), (22, 8, 128),
    ]
    return pl.pallas_call(
        kernel,
        out_shape=pltpu.VMEM((16, 8, 256), f32),
        in_specs=[pl.BlockSpec(memory_space=pl.ANY)] * 3,
        out_specs=pl.BlockSpec(memory_space=pltpu.VMEM),
        scratch_shapes=[pltpu.VMEM((16, 8, 256), kind) for kind in (f32, jnp.int32, f32)] + [pltpu.SemaphoreType.DMA((3,))]
        + [pltpu.VMEM(shape, f32) for shape in shapes] + [pltpu.SemaphoreType.DMA((COPIES,))] * 2,
        compiler_params=pltpu.CompilerParams(collective_id=0, has_side_effects=True),
        name="vcycle",
    )(source, phase_mask, density_factor)


def solution(mesh):
    spec = P("gx", "gy", "gz")
    return jax.shard_map(shards, mesh=mesh, in_specs=(spec,) * 3, out_specs=spec, check_vma=False)
```

```python
import jax
import jax.numpy as jnp
from jax import lax
from jax.experimental import pallas as pl
from jax.experimental.pallas import tpu as pltpu
from jax.sharding import PartitionSpec as P

GAS_DENSITY = 0.001
RELAXATION = 0.8
KEEP = 1.0 - RELAXATION
COARSE_SWEEPS = 8
MESH = pl.DeviceIdType.MESH
CHUNK = 2
COPIES = 68
TINY = 1e-30
AXES = ("gx", "gy", "gz")
SIDES = [(a, b) for a in (-1, 0, 1) for b in (-1, 0, 1) if a or b]


def iota(shape, axis):
    return lax.broadcasted_iota(jnp.int32, shape, axis)


def dot(a, b):
    high = a.astype(jnp.bfloat16)
    rest = a - high.astype(jnp.float32)
    middle = rest.astype(jnp.bfloat16)
    low = (rest - middle.astype(jnp.float32)).astype(jnp.bfloat16)
    return sum(jnp.dot(part, b, preferred_element_type=jnp.float32) for part in (low, middle, high))


def ones_where(condition):
    return jnp.where(condition, 1.0, 0.0).astype(jnp.bfloat16)


def turn(x, shift, axis):
    shift %= x.shape[axis]
    return pltpu.roll(x, shift, axis) if shift else x


def coupling(a, b):
    return 2.0 / jnp.maximum(a + b, TINY)


def grow(t, axis):
    row = iota(t.shape, axis)
    moved = [t] + [pltpu.roll(t, n, axis) for n in (1, 2, 3, 4)]
    low = jnp.where(row < 1, moved[0], jnp.where(row < 3, moved[1], moved[2]))
    high = jnp.where(row < 5, moved[2], jnp.where(row < 7, moved[3], moved[4]))
    return jnp.where(row < 4, low, high)


def kernel(src_in, mask_in, fac_in, out, src, mask, fac, in_sem, V0, SRC, YS0, YH0, ZS, ZH, HX, HY, CX0, C0, CB0, KB0, INV0, DIAG0, R0,
           S1, H1, RHO1, CX1, C1, INV1, DIAG1, B1, W1, W2, E1, G, GB, XD, send_sem, recv_sem):
    f32 = jnp.float32
    sizes = {axis: lax.axis_size(axis) for axis in AXES}
    at = {axis: lax.axis_index(axis) for axis in AXES}
    gx, gy = at["gx"], at["gy"]

    def peer(way):
        return {axis: lax.rem(at[axis] + (d + sizes[axis]), sizes[axis]) for axis, d in way.items() if d}

    def exists(axis, d):
        place = at[axis] + d
        return (place >= 0) & (place < sizes[axis])

    above, below = exists("gz", 1), exists("gz", -1)
    copies = []

    def ready(source, target, way):
        k = len(copies)
        copy = pltpu.make_async_remote_copy(
            src_ref=source, dst_ref=target, send_sem=send_sem.at[k], recv_sem=recv_sem.at[k],
            device_id=peer(way), device_id_type=MESH)
        copies.append(copy)
        return copy

    def post(source, target, way):
        copy = ready(source, target, way)
        copy.start()
        return copy

    def arrived(group):
        for copy in group:
            copy.wait_recv()

    def left(group):
        for copy in group:
            copy.wait_send()

    inputs = [pltpu.make_async_copy(a, b, in_sem.at[n]) for n, (a, b) in enumerate(((fac_in, fac), (mask_in, mask), (src_in, src)))]
    for copy in inputs:
        copy.start()

    barrier = pltpu.get_barrier_semaphore()
    steady = [{"gx": a, "gy": b} for a in (0, -1, 1, -2, 2) for b in (0, 1, 3, 2) if a or b] + [{"gx": -3}, {"gx": 3}]
    across = [{}, {"gx": -1}, {"gx": 1}, {"gy": -1}, {"gy": 1}]
    for d, there in ((-1, below), (1, above)):
        ids = [peer({**way, "gz": d}) for way in across]

        @pl.when(there)
        def _():
            for other in ids:
                pl.semaphore_signal(barrier, inc=1, device_id=other, device_id_type=MESH)
    for way in steady:
        pl.semaphore_signal(barrier, inc=1, device_id=peer(way), device_id_type=MESH)

    lane16 = iota((8, 8, 128), 2)
    chunks = range(0, 16, CHUNK)
    own, ring = slice(0, 256), slice(256, 384)

    def pack_y0(k, c, v):
        n = v.shape[-1]
        for i in range(v.shape[0]):
            YS0[k, 0, c + i:c + i + 1, 0:n] = v[i, 0:1, :]
            YS0[k, 1, c + i:c + i + 1, 0:n] = v[i, 7:8, :]

    def outer(k, c, lanes=slice(0, 384)):
        shape = (8, lanes.stop - lanes.start)
        first = iota(shape, 0) < 4
        return jnp.stack([jnp.where(first, jnp.broadcast_to(YH0[k, 0, c + i:c + i + 1, lanes], shape),
                                    jnp.broadcast_to(YH0[k, 1, c + i:c + i + 1, lanes], shape)) for i in range(CHUNK)])

    def inner(k, c):
        v = V0[k, 1 + c:1 + c + CHUNK]
        parts = []
        for i in range(c, c + CHUNK):
            terms = ([CX0[i] * V0[k, i]] if i else []) + ([CX0[i + 1] * V0[k, i + 2]] if i < 15 else [])
            parts.append(sum(terms[1:], terms[0]))
        total = jnp.stack(parts) + C0[0, c:c + CHUNK] * pltpu.roll(v, 7, 1) + C0[1, c:c + CHUNK] * pltpu.roll(v, 1, 1)
        return v, total + C0[2, c:c + CHUNK] * pltpu.roll(v, 383, 2) + C0[3, c:c + CHUNK] * pltpu.roll(v, 1, 2)

    def ends(k, c):
        return {i: CX0[i + (i == 15)] * V0[k, 17 if i else 0] for i in (0, 15) if c <= i < c + CHUNK}

    def faces0(k):
        return [post(YS0.at[k, 0], YH0.at[k, 1], {"gy": -1}), post(YS0.at[k, 1], YH0.at[k, 0], {"gy": 1}),
                post(V0.at[k, 1], V0.at[k, 17], {"gx": -1}), post(V0.at[k, 16], V0.at[k, 0], {"gx": 1})]

    def trim0(k, lanes=slice(0, 384)):
        for side, d in ((0, -1), (1, 1)):
            V0[k, 17 * side, :, lanes] = jnp.where(exists("gx", d), V0[k, 17 * side, :, lanes], 0.0)
            YH0[k, side, :, lanes] = jnp.where(exists("gy", d), YH0[k, side, :, lanes], 0.0)

    def pack_z0(n, field):
        low, high = field[:, :, 0:128], field[:, :, 128:256]
        ZS[n, 0] = jnp.where(lane16 < 64, low[0:8], pltpu.roll(low[8:16], 64, 2))
        ZS[n, 1] = jnp.where(lane16 < 64, pltpu.roll(high[0:8], 64, 2), high[8:16])

    def unpack_z0(n):
        up, down = jnp.where(above, ZH[n, 1], 0.0), jnp.where(below, ZH[n, 0], 0.0)
        return (jnp.where(lane16 < 64, up, pltpu.roll(down, 64, 2)), jnp.where(lane16 < 64, pltpu.roll(up, 64, 2), down))

    inputs[0].wait()
    inputs[1].wait()
    rho = jnp.where(mask[...] == 1, GAS_DENSITY, 1.0) * fac[...]
    V0[0, 1:17, :, own] = rho
    pack_z0(0, rho)
    pack_y0(0, 0, rho)
    inputs[2].wait()
    pack_z0(1, src[...])
    two = jnp.where(above, 1, 0) + jnp.where(below, 1, 0)
    pl.semaphore_wait(barrier, len(steady) + len(across) * two)

    low, high = pl.ds(0, 128), pl.ds(128, 128)
    to_below = [ready(ZS.at[0, 0], ZH.at[0, 1], {"gz": -1}),
                ready(V0.at[0, 1, :, low], HX.at[1, 1], {"gx": -1, "gz": -1}),
                ready(V0.at[0, 16, :, low], HX.at[0, 1], {"gx": 1, "gz": -1}),
                ready(YS0.at[0, 0, :, low], HY.at[1, 1], {"gy": -1, "gz": -1}),
                ready(YS0.at[0, 1, :, low], HY.at[0, 1], {"gy": 1, "gz": -1}),
                ready(ZS.at[1, 0], ZH.at[1, 1], {"gz": -1})]
    to_above = [ready(ZS.at[0, 1], ZH.at[0, 0], {"gz": 1}),
                ready(V0.at[0, 1, :, high], HX.at[1, 0], {"gx": -1, "gz": 1}),
                ready(V0.at[0, 16, :, high], HX.at[0, 0], {"gx": 1, "gz": 1}),
                ready(YS0.at[0, 0, :, high], HY.at[1, 0], {"gy": -1, "gz": 1}),
                ready(YS0.at[0, 1, :, high], HY.at[0, 0], {"gy": 1, "gz": 1}),
                ready(ZS.at[1, 1], ZH.at[1, 0], {"gz": 1})]
    for some in (slice(1, 5), slice(0, 1)):
        for group, there in ((to_below, below), (to_above, above)):
            @pl.when(there)
            def _():
                for copy in group[some]:
                    copy.start()
    both = pl.ds(0, 256)
    rho0_faces = [post(V0.at[0, 1, :, both], V0.at[0, 17, :, both], {"gx": -1}),
                  post(V0.at[0, 16, :, both], V0.at[0, 0, :, both], {"gx": 1}),
                  post(YS0.at[0, 0, :, both], YH0.at[0, 1, :, both], {"gy": -1}),
                  post(YS0.at[0, 1, :, both], YH0.at[0, 0, :, both], {"gy": 1})]
    for group, there in ((to_below, below), (to_above, above)):
        @pl.when(there)
        def _():
            group[5].start()

    a, b = lax.shift_right_logical(iota((384, 256), 0), 1), iota((384, 256), 1)
    pairs0 = ones_where(b == jnp.where(a < 160, a, a + 64))
    pairs1 = ones_where(lax.shift_right_logical(iota((256, 128), 0), 1) == iota((256, 128), 1))
    a, b = iota((256, 384), 0), lax.shift_right_logical(iota((256, 384), 1), 1)
    spread0 = ones_where(a == jnp.where(b < 160, b, b + 64))
    spread1 = ones_where(iota((128, 256), 0) == lax.shift_right_logical(iota((128, 256), 1), 1))

    def couple0(lanes, planes):
        for c in planes:
            CX0[c, :, lanes] = coupling(V0[0, c, :, lanes], V0[0, c + 1, :, lanes])

    def couple0_y(lanes):
        for c in chunks:
            rho = V0[0, 1 + c:1 + c + CHUNK, :, lanes]
            between = jnp.where(iota(rho.shape, 1) == 7, 0.0, coupling(rho, pltpu.roll(rho, 7, 1)))
            C0[0, c:c + CHUNK, :, lanes] = between
            C0[1, c:c + CHUNK, :, lanes] = pltpu.roll(between, 1, 1)

    def couple0_ends(lanes):
        for c in chunks:
            rho = V0[0, 1 + c:1 + c + CHUNK, :, lanes]
            row = iota(rho.shape, 1)
            CB0[c:c + CHUNK, :, lanes] = jnp.where((row == 0) | (row == 7), coupling(rho, outer(0, c, lanes)), 0.0)

    SRC[:, :, own] = src[...]
    couple0(own, range(1, 16))
    couple0_y(own)
    for c in chunks:
        rho = V0[0, 1 + c:1 + c + CHUNK, :, own]
        between = coupling(rho, pltpu.roll(rho, 255, 2))
        C0[2, c:c + CHUNK, :, own] = between
        C0[3, c:c + CHUNK, :, own] = pltpu.roll(between, 1, 2)
    arrived(rho0_faces)
    trim0(0, own)
    couple0(own, (0, 16))
    couple0_ends(own)
    for group, there in ((to_below, above), (to_above, below)):
        @pl.when(there)
        def _():
            arrived(group[:5])
    first, second = unpack_z0(0)
    V0[0, 1:9, :, ring] = first
    V0[0, 9:17, :, ring] = second
    lane8, lane2 = iota((8, 128), 1), iota((16, 128), 1)
    for side in (0, 1):
        V0[0, 17 * side, :, ring] = jnp.where(
            lane8 < 64, jnp.where(above, HX[side, 1], 0.0), jnp.where(below, HX[side, 0], 0.0))
        YH0[0, side, :, ring] = jnp.where(
            lane2 < 64, jnp.where(above, HY[side, 1], 0.0), jnp.where(below, HY[side, 0], 0.0))
    trim0(0, ring)
    couple0(ring, range(17))
    couple0_y(ring)
    couple0_ends(ring)
    for c in chunks:
        some = slice(c, c + CHUNK)
        rho = V0[0, 1 + c:1 + c + CHUNK]
        outside = rho[:, :, ring]
        lane = iota(outside.shape, 2)
        up = jnp.where(lane == 127, pltpu.roll(rho[:, :, 0:128], 127, 2), pltpu.roll(outside, 127, 2))
        down = jnp.where(lane == 0, pltpu.roll(rho[:, :, 128:256], 1, 2), pltpu.roll(outside, 1, 2))
        up, down = coupling(outside, up), coupling(outside, down)
        C0[2, some, :, ring] = up
        C0[3, some, :, ring] = down
        C0[2, some, :, 128:256] = jnp.where(lane == 127, pltpu.roll(down, 127, 2), C0[2, some, :, 128:256])
        C0[3, some, :, 0:128] = jnp.where(lane == 0, pltpu.roll(up, 1, 2), C0[3, some, :, 0:128])
        between, after = C0[2, some], C0[3, some]
        diag = (CX0[some] + CX0[c + 1:c + 1 + CHUNK]) + (between + after) + (C0[0, some] + C0[1, some] + CB0[some])
        DIAG0[some] = diag
        INV0[some] = jnp.where(rho > 0.0, RELAXATION / diag, 0.0)
    for group, there in ((to_below, above), (to_above, below)):
        @pl.when(there)
        def _():
            arrived(group[5:])
    first, second = unpack_z0(1)
    SRC[0:8, :, ring] = first
    SRC[8:16, :, ring] = second

    for c in chunks:
        v = INV0[c:c + CHUNK] * SRC[c:c + CHUNK]
        V0[1, 1 + c:1 + c + CHUNK] = v
        pack_y0(1, c, v)
    v1_faces = faces0(1)
    for group, there in ((to_below, below), (to_above, above)):
        @pl.when(there)
        def _():
            left(group)
    for c in chunks:
        some = slice(c, c + CHUNK)
        v, total = inner(1, c)
        V0[2, 1 + c:1 + c + CHUNK] = KEEP * v + INV0[some] * (SRC[some] + total)
        KB0[some] = INV0[some] * CB0[some]

    row8 = iota((8, 256), 0)
    row8s = iota((8, 128), 0)

    row24 = iota((8, 384), 0)

    def down0(plane):
        tiles = []
        for j in range(4):
            t, u = (plane(4 * j + n) + plane(4 * j + n + 1) for n in (0, 2))
            t, u = (x + pltpu.roll(x, 7, 0) for x in (t, u))
            tile = pltpu.roll(u, 1, 0)
            for n, part in ((7, pltpu.roll(u, 2, 0)), (6, pltpu.roll(u, 3, 0)), (5, pltpu.roll(u, 4, 0)),
                            (4, pltpu.roll(t, 5, 0)), (3, pltpu.roll(t, 6, 0)), (2, pltpu.roll(t, 7, 0)), (1, t)):
                tile = jnp.where(row24 < n, part, tile)
            tiles.append(tile)
        t = dot(jnp.concatenate(tiles, axis=0), pairs0)
        return [t[8 * j:8 * j + 8] for j in range(4)]

    def slot(a, b):
        return SIDES.index((a, b))

    def exchange1(k, packed):
        for j in range(4):
            S1[k, j] = packed[j]
        group = []
        for a, b in ((1, 1), (1, -1), (-1, 1), (-1, -1), (0, 1), (0, -1), (1, 0), (-1, 0)):
            some = {1: pl.ds(2, 2), -1: pl.ds(0, 2), 0: pl.ds(0, 4)}[a]
            if k and a and b:
                some = pl.ds(3 if a > 0 else 0, 1)
            group.append(post(S1.at[k, some], H1.at[k, slot(-a, -b), some], {"gx": a, "gy": b}))
        return group

    def unpack1(k, target, first, last, offset):
        for p in range(first, last):
            a = p // 8
            j, half = (p % 8) // 2, p % 2

            def block(b):
                if not a and not b:
                    return S1[k, j]
                if k and a and b and j in (1, 2):
                    return jnp.zeros((8, 256), f32)
                return jnp.where(exists("gx", a) & exists("gy", b), H1[k, slot(a, b), j], 0.0)

            target[p - offset, 0:8] = jnp.where(row8 < 4, turn(block(0), -4 * half, 0), turn(block(1), 4 - 4 * half, 0))
            target[p - offset, 8:16] = jnp.where(row8 < 4, 0.0, turn(block(-1), 4 - 4 * half, 0))

    def shifts1(v):
        return pltpu.roll(v, 15, 0), pltpu.roll(v, 1, 0), pltpu.roll(v, 255, 1), pltpu.roll(v, 1, 1)

    def around1(V, p, base):
        v = V[p - base]
        total = CX1[p + 3] * V[p - 1 - base] + CX1[p + 4] * V[p + 1 - base]
        for n, other in enumerate(shifts1(v)):
            total = total + C1[n, p + 3] * other
        return v, total

    def down1(plane):
        packed = jnp.zeros((8, 256), f32)
        for x in range(4):
            t = plane(2 * x) + plane(2 * x + 1)
            t = t + pltpu.roll(t, 7, 0)
            for half in range(2):
                packed = jnp.where(row8 == 2 * x + half, turn(t, 2 * x - half, 0), packed)
        return dot(packed, pairs1)

    packed1 = [0.125 * t for t in down0(lambda p: V0[0, 1 + p])]
    rho1_copies = exchange1(0, packed1)
    G[gy] = 0.125 * down1(lambda p: packed1[p // 2] if p % 2 == 0 else pltpu.roll(packed1[p // 2], 4, 0))
    rho2_y = [post(G.at[gy], G.at[gy], {"gy": d}) for d in (1, 2, 3)]

    arrived(v1_faces)
    trim0(1)
    for c in chunks:
        for i, term in ends(1, c).items():
            V0[2, 1 + i] = V0[2, 1 + i] + INV0[i] * term
        v = V0[2, 1 + c:1 + c + CHUNK] + KB0[c:c + CHUNK] * outer(1, c)
        V0[2, 1 + c:1 + c + CHUNK] = v
        pack_y0(2, c, v)
    v2_faces = faces0(2)
    for c in chunks:
        v, total = inner(2, c)
        R0[c:c + CHUNK] = SRC[c:c + CHUNK] + total - DIAG0[c:c + CHUNK] * v

    def rows_of(blocks):
        planes = []
        for x in range(4):
            t = turn(blocks[0], -2 * x, 0)
            for q in (1, 2, 3):
                t = jnp.where(row8s < 2 * q, t, turn(blocks[q], 2 * (q - x), 0))
            planes.append(t)
        return planes

    arrived(rho2_y)
    for x, t in enumerate(rows_of([G[q] for q in range(4)])):
        XD[9 + x] = t
    rho2_x = [post(XD.at[9:13], XD.at[9 - 4 * d:13 - 4 * d], {"gx": d}) for d in (-2, -1, 1, 2)]
    rho2_x += [post(XD.at[12], XD.at[0], {"gx": 3}), post(XD.at[9], XD.at[21], {"gx": -3})]

    arrived(rho1_copies)
    unpack1(0, RHO1, -4, 12, -4)
    for p in range(-3, 12):
        CX1[p + 3] = coupling(RHO1[p + 3], RHO1[p + 4])
    for p in range(-3, 11):
        rho = RHO1[p + 4]
        diag = CX1[p + 3] + CX1[p + 4]
        for n, other in enumerate(shifts1(rho)):
            between = coupling(rho, other)
            C1[n, p + 3] = between
            diag = diag + between
        INV1[p + 3] = jnp.where(rho > 0.0, RELAXATION / diag, 0.0)
        if 0 <= p < 8:
            DIAG1[p] = diag

    arrived(v2_faces)
    trim0(2)
    residual = []
    for c in chunks:
        r = R0[c:c + CHUNK] + CB0[c:c + CHUNK] * outer(2, c)
        more = ends(2, c)
        residual += [r[i] + more[c + i] if c + i in more else r[i] for i in range(CHUNK)]
    b1_copies = exchange1(1, [0.5 * t for t in down0(lambda p: residual[p])])

    arrived(rho2_x)
    for d in (-2, -1, 1, 2):
        XD[9 - 4 * d:13 - 4 * d] = jnp.where(exists("gx", -d), XD[9 - 4 * d:13 - 4 * d], 0.0)
    XD[0] = jnp.where(exists("gx", -3), XD[0], 0.0)
    XD[21] = jnp.where(exists("gx", 3), XD[21], 0.0)
    row2 = iota((20, 8, 128), 1)
    rho = XD[1:21]
    cx2 = coupling(XD[0:21], XD[1:22])
    y_up = coupling(rho, jnp.where(row2 == 7, 0.0, pltpu.roll(rho, 7, 1)))
    y_down = coupling(rho, jnp.where(row2 == 0, 0.0, pltpu.roll(rho, 1, 1)))
    z_up = coupling(rho, pltpu.roll(rho, 127, 2))
    z_down = coupling(rho, pltpu.roll(rho, 1, 2))
    diag2 = cx2[0:20] + cx2[1:21] + ((y_up + y_down) + (z_up + z_down))
    inv2 = jnp.where(rho > 0.0, RELAXATION / diag2, 0.0)
    y_up = jnp.where(row2 == 7, 0.0, y_up)
    y_down = jnp.where(row2 == 0, 0.0, y_down)

    arrived(b1_copies)
    unpack1(1, B1, -3, 11, -3)
    for p in range(-3, 11):
        W1[p + 3] = INV1[p + 3] * B1[p + 3]
    near, far = slice(0, 8), slice(8, 16)

    def second1(p, rows):
        v, total = around1(W1, p, -3)
        for some in rows:
            W2[p + 2, some] = (KEEP * v + INV1[p + 3] * (B1[p + 3] + total))[some]

    for p in range(-1, 9):
        second1(p, (near, far) if 0 <= p < 8 else (near,))
    residual = []
    for p in range(8):
        v, total = around1(W2, p, -2)
        residual.append((B1[p + 3] + total - DIAG1[p] * v)[near])

    GB[2, gy] = 0.5 * down1(lambda p: residual[p])
    b2_copies = [post(GB.at[2, gy], GB.at[2 - d, gy], {"gx": d, "gy": e})
                 for e in (2, 1, 3, 0) for d in (2, -2, 1, -1, 0) if d or e]
    second1(-2, (near,))
    second1(-1, (far,))
    second1(8, (far,))
    second1(9, (near,))
    late = {id(copy) for copy in b2_copies + to_below + to_above}
    left([copy for copy in copies if id(copy) not in late])
    arrived(b2_copies)
    planes = []
    for d in (-2, -1, 0, 1, 2):
        planes += [jnp.where(exists("gx", d), t, 0.0) if d else t for t in rows_of([GB[2 + d, q] for q in range(4)])]
    b2 = jnp.stack(planes)
    v = inv2 * b2
    for k in range(1, COARSE_SWEEPS):
        z = 20 - k
        here = v[1:-1]
        total = cx2[k:z] * v[:-2] + cx2[k + 1:z + 1] * v[2:]
        total = total + y_up[k:z] * pltpu.roll(here, 7, 1) + y_down[k:z] * pltpu.roll(here, 1, 1)
        total = total + z_up[k:z] * pltpu.roll(here, 127, 2) + z_down[k:z] * pltpu.roll(here, 1, 2)
        v = KEEP * here + inv2[k:z] * (b2[k:z] + total)

    row6 = iota((6, 8, 128), 1)
    t = pltpu.roll(v, lax.rem(8 - 2 * gy, 8), 1)
    over = jnp.where(row6 < jnp.where(exists("gy", 1), 8, 4), grow(t, 1), 0.0)
    under = jnp.where(row6 >= jnp.where(exists("gy", -1), 6, 8), jnp.where(row6 == 7, t, pltpu.roll(t, 7, 1)), 0.0)
    t = dot(jnp.concatenate([over, under], axis=1).reshape(96, 128), spread1).reshape(6, 16, 256)
    for p in range(-2, 10):
        for some in (near, far) if -2 < p < 9 else (near,):
            W2[p + 2, some] = W2[p + 2, some] + t[p // 2 + 1, some]
    for p in range(-1, 9):
        v, total = around1(W2, p, -2)
        v = KEEP * v + INV1[p + 3] * (B1[p + 3] + total)
        E1[p + 1, near] = v[near]
        if 0 <= p < 8:
            E1[p + 1, far] = v[far]

    y_low = jnp.zeros((8, 256), f32)
    y_high = y_low
    for p in range(8):
        y_low = jnp.where(row8 == p, turn(E1[p + 1, 8:16], p - 7, 0), y_low)
        y_high = jnp.where(row8 == p, turn(E1[p + 1, 0:8], p - 4, 0), y_high)
    parts = [grow(E1[p, 0:8], 0) for p in range(10)]
    for t in (y_low, y_high):
        parts += [grow(t, 0), grow(pltpu.roll(t, 4, 0), 0)]
    e = dot(jnp.concatenate(parts, axis=0), spread0)
    for p in range(18):
        n = (p + 1) // 2
        V0[2, p] = V0[2, p] + e[8 * n:8 * n + 8]
    YH0[2, 0] = YH0[2, 0] + e[80:96]
    YH0[2, 1] = YH0[2, 1] + e[96:112]
    for c in chunks:
        v, total = inner(2, c)
        more = ends(2, c)
        total = total + CB0[c:c + CHUNK] * outer(2, c)
        total = jnp.stack([total[i] + more[c + i] if c + i in more else total[i] for i in range(CHUNK)])
        v = KEEP * v + INV0[c:c + CHUNK] * (SRC[c:c + CHUNK] + total)
        out[c:c + CHUNK] = v[:, :, own]

    left(b2_copies)


def shards(source, phase_mask, density_factor):
    f32 = jnp.float32
    shapes = [
        (3, 18, 8, 384), (16, 8, 384), (3, 2, 16, 384), (3, 2, 16, 384), (2, 2, 8, 8, 128), (2, 2, 8, 8, 128),
        (2, 2, 8, 128), (2, 2, 16, 128), (17, 8, 384), (4, 16, 8, 384), (16, 8, 384), (16, 8, 384),
        (16, 8, 384), (16, 8, 384), (16, 8, 384),
        (2, 4, 8, 256), (2, 8, 4, 8, 256), (16, 16, 256), (15, 16, 256), (4, 14, 16, 256), (14, 16, 256), (8, 16, 256),
        (14, 16, 256), (14, 16, 256), (12, 16, 256), (10, 16, 256), (4, 8, 128), (5, 4, 8, 128), (22, 8, 128),
    ]
    return pl.pallas_call(
        kernel,
        out_shape=pltpu.VMEM((16, 8, 256), f32),
        in_specs=[pl.BlockSpec(memory_space=pl.ANY)] * 3,
        out_specs=pl.BlockSpec(memory_space=pltpu.VMEM),
        scratch_shapes=[pltpu.VMEM((16, 8, 256), kind) for kind in (f32, jnp.int32, f32)] + [pltpu.SemaphoreType.DMA((3,))]
        + [pltpu.VMEM(shape, f32) for shape in shapes] + [pltpu.SemaphoreType.DMA((COPIES,))] * 2,
        compiler_params=pltpu.CompilerParams(collective_id=0, has_side_effects=True),
        name="vcycle",
    )(source, phase_mask, density_factor)


def solution(mesh):
    spec = P("gx", "gy", "gz")
    return jax.shard_map(shards, mesh=mesh, in_specs=(spec,) * 3, out_specs=spec, check_vma=False)
```

```python
import jax
import jax.numpy as jnp
from jax import lax
from jax.experimental import pallas as pl
from jax.experimental.pallas import tpu as pltpu
from jax.sharding import PartitionSpec as P

GAS_DENSITY = 0.001
RELAXATION = 0.8
KEEP = 1.0 - RELAXATION
COARSE_SWEEPS = 8
MESH = pl.DeviceIdType.MESH
CHUNK = 2
COPIES = 68
TINY = 1e-30
AXES = ("gx", "gy", "gz")
SIDES = [(a, b) for a in (-1, 0, 1) for b in (-1, 0, 1) if a or b]


def iota(shape, axis):
    return lax.broadcasted_iota(jnp.int32, shape, axis)


def dot(a, b):
    high = a.astype(jnp.bfloat16)
    rest = a - high.astype(jnp.float32)
    middle = rest.astype(jnp.bfloat16)
    low = (rest - middle.astype(jnp.float32)).astype(jnp.bfloat16)
    return sum(jnp.dot(part, b, preferred_element_type=jnp.float32) for part in (low, middle, high))


def ones_where(condition):
    return jnp.where(condition, 1.0, 0.0).astype(jnp.bfloat16)


def turn(x, shift, axis):
    shift %= x.shape[axis]
    return pltpu.roll(x, shift, axis) if shift else x


def coupling(a, b):
    return 2.0 / jnp.maximum(a + b, TINY)


def grow(t, axis):
    row = iota(t.shape, axis)
    moved = [t] + [pltpu.roll(t, n, axis) for n in (1, 2, 3, 4)]
    low = jnp.where(row < 1, moved[0], jnp.where(row < 3, moved[1], moved[2]))
    high = jnp.where(row < 5, moved[2], jnp.where(row < 7, moved[3], moved[4]))
    return jnp.where(row < 4, low, high)


def kernel(src_in, mask_in, fac_in, out, src, mask, fac, in_sem, V0, SRC, YS0, YH0, ZS, ZH, HX, HY, CX0, C0, CB0, KB0, INV0, DIAG0, R0,
           S1, H1, RHO1, CX1, C1, INV1, DIAG1, B1, W1, W2, E1, G, GB, XD, send_sem, recv_sem):
    f32 = jnp.float32
    sizes = {axis: lax.axis_size(axis) for axis in AXES}
    at = {axis: lax.axis_index(axis) for axis in AXES}
    gx, gy = at["gx"], at["gy"]

    def peer(way):
        return {axis: lax.rem(at[axis] + (d + sizes[axis]), sizes[axis]) for axis, d in way.items() if d}

    def exists(axis, d):
        place = at[axis] + d
        return (place >= 0) & (place < sizes[axis])

    above, below = exists("gz", 1), exists("gz", -1)
    copies = []

    def ready(source, target, way):
        k = len(copies)
        copy = pltpu.make_async_remote_copy(
            src_ref=source, dst_ref=target, send_sem=send_sem.at[k], recv_sem=recv_sem.at[k],
            device_id=peer(way), device_id_type=MESH)
        copies.append(copy)
        return copy

    def post(source, target, way):
        copy = ready(source, target, way)
        copy.start()
        return copy

    def arrived(group):
        for copy in group:
            copy.wait_recv()

    def left(group):
        for copy in group:
            copy.wait_send()

    inputs = [pltpu.make_async_copy(a, b, in_sem.at[n]) for n, (a, b) in enumerate(((fac_in, fac), (mask_in, mask), (src_in, src)))]
    for copy in inputs:
        copy.start()

    barrier = pltpu.get_barrier_semaphore()
    steady = [{"gx": a, "gy": b} for a in (0, -1, 1, -2, 2) for b in (0, 1, 3, 2) if a or b] + [{"gx": -3}, {"gx": 3}]
    across = [{}, {"gx": -1}, {"gx": 1}, {"gy": -1}, {"gy": 1}]
    for d, there in ((-1, below), (1, above)):
        ids = [peer({**way, "gz": d}) for way in across]

        @pl.when(there)
        def _():
            for other in ids:
                pl.semaphore_signal(barrier, inc=1, device_id=other, device_id_type=MESH)
    for way in steady:
        pl.semaphore_signal(barrier, inc=1, device_id=peer(way), device_id_type=MESH)

    lane16 = iota((8, 8, 128), 2)
    chunks = range(0, 16, CHUNK)
    own, ring = slice(0, 256), slice(256, 384)

    def pack_y0(k, c, v):
        n = v.shape[-1]
        for i in range(v.shape[0]):
            YS0[k, 0, c + i:c + i + 1, 0:n] = v[i, 0:1, :]
            YS0[k, 1, c + i:c + i + 1, 0:n] = v[i, 7:8, :]

    def outer(k, c, lanes=slice(0, 384)):
        shape = (8, lanes.stop - lanes.start)
        first = iota(shape, 0) < 4
        return jnp.stack([jnp.where(first, jnp.broadcast_to(YH0[k, 0, c + i:c + i + 1, lanes], shape),
                                    jnp.broadcast_to(YH0[k, 1, c + i:c + i + 1, lanes], shape)) for i in range(CHUNK)])

    def inner(k, c):
        v = V0[k, 1 + c:1 + c + CHUNK]
        parts = []
        for i in range(c, c + CHUNK):
            terms = ([CX0[i] * V0[k, i]] if i else []) + ([CX0[i + 1] * V0[k, i + 2]] if i < 15 else [])
            parts.append(sum(terms[1:], terms[0]))
        total = jnp.stack(parts) + C0[0, c:c + CHUNK] * pltpu.roll(v, 7, 1) + C0[1, c:c + CHUNK] * pltpu.roll(v, 1, 1)
        return v, total + C0[2, c:c + CHUNK] * pltpu.roll(v, 383, 2) + C0[3, c:c + CHUNK] * pltpu.roll(v, 1, 2)

    def ends(k, c):
        return {i: CX0[i + (i == 15)] * V0[k, 17 if i else 0] for i in (0, 15) if c <= i < c + CHUNK}

    def faces0(k):
        return [post(YS0.at[k, 0], YH0.at[k, 1], {"gy": -1}), post(YS0.at[k, 1], YH0.at[k, 0], {"gy": 1}),
                post(V0.at[k, 1], V0.at[k, 17], {"gx": -1}), post(V0.at[k, 16], V0.at[k, 0], {"gx": 1})]

    def trim0(k, lanes=slice(0, 384)):
        for side, d in ((0, -1), (1, 1)):
            V0[k, 17 * side, :, lanes] = jnp.where(exists("gx", d), V0[k, 17 * side, :, lanes], 0.0)
            YH0[k, side, :, lanes] = jnp.where(exists("gy", d), YH0[k, side, :, lanes], 0.0)

    def pack_z0(n, field):
        low, high = field[:, :, 0:128], field[:, :, 128:256]
        ZS[n, 0] = jnp.where(lane16 < 64, low[0:8], pltpu.roll(low[8:16], 64, 2))
        ZS[n, 1] = jnp.where(lane16 < 64, pltpu.roll(high[0:8], 64, 2), high[8:16])

    def unpack_z0(n):
        up, down = jnp.where(above, ZH[n, 1], 0.0), jnp.where(below, ZH[n, 0], 0.0)
        return (jnp.where(lane16 < 64, up, pltpu.roll(down, 64, 2)), jnp.where(lane16 < 64, pltpu.roll(up, 64, 2), down))

    inputs[0].wait()
    inputs[1].wait()
    rho = jnp.where(mask[...] == 1, GAS_DENSITY, 1.0) * fac[...]
    V0[0, 1:17, :, own] = rho
    pack_z0(0, rho)
    pack_y0(0, 0, rho)
    inputs[2].wait()
    pack_z0(1, src[...])
    two = jnp.where(above, 1, 0) + jnp.where(below, 1, 0)
    pl.semaphore_wait(barrier, len(steady) + len(across) * two)

    low, high = pl.ds(0, 128), pl.ds(128, 128)
    to_below = [ready(ZS.at[0, 0], ZH.at[0, 1], {"gz": -1}),
                ready(V0.at[0, 1, :, low], HX.at[1, 1], {"gx": -1, "gz": -1}),
                ready(V0.at[0, 16, :, low], HX.at[0, 1], {"gx": 1, "gz": -1}),
                ready(YS0.at[0, 0, :, low], HY.at[1, 1], {"gy": -1, "gz": -1}),
                ready(YS0.at[0, 1, :, low], HY.at[0, 1], {"gy": 1, "gz": -1}),
                ready(ZS.at[1, 0], ZH.at[1, 1], {"gz": -1})]
    to_above = [ready(ZS.at[0, 1], ZH.at[0, 0], {"gz": 1}),
                ready(V0.at[0, 1, :, high], HX.at[1, 0], {"gx": -1, "gz": 1}),
                ready(V0.at[0, 16, :, high], HX.at[0, 0], {"gx": 1, "gz": 1}),
                ready(YS0.at[0, 0, :, high], HY.at[1, 0], {"gy": -1, "gz": 1}),
                ready(YS0.at[0, 1, :, high], HY.at[0, 0], {"gy": 1, "gz": 1}),
                ready(ZS.at[1, 1], ZH.at[1, 0], {"gz": 1})]
    for some in (slice(1, 5), slice(0, 1)):
        for group, there in ((to_below, below), (to_above, above)):
            @pl.when(there)
            def _():
                for copy in group[some]:
                    copy.start()
    both = pl.ds(0, 256)
    rho0_faces = [post(V0.at[0, 1, :, both], V0.at[0, 17, :, both], {"gx": -1}),
                  post(V0.at[0, 16, :, both], V0.at[0, 0, :, both], {"gx": 1}),
                  post(YS0.at[0, 0, :, both], YH0.at[0, 1, :, both], {"gy": -1}),
                  post(YS0.at[0, 1, :, both], YH0.at[0, 0, :, both], {"gy": 1})]
    for group, there in ((to_below, below), (to_above, above)):
        @pl.when(there)
        def _():
            group[5].start()

    a, b = lax.shift_right_logical(iota((384, 256), 0), 1), iota((384, 256), 1)
    pairs0 = ones_where(b == jnp.where(a < 160, a, a + 64))
    pairs1 = ones_where(lax.shift_right_logical(iota((256, 128), 0), 1) == iota((256, 128), 1))
    a, b = iota((256, 384), 0), lax.shift_right_logical(iota((256, 384), 1), 1)
    spread0 = ones_where(a == jnp.where(b < 160, b, b + 64))
    spread1 = ones_where(iota((128, 256), 0) == lax.shift_right_logical(iota((128, 256), 1), 1))

    def couple0(lanes, planes):
        for c in planes:
            CX0[c, :, lanes] = coupling(V0[0, c, :, lanes], V0[0, c + 1, :, lanes])

    def couple0_y(lanes):
        for c in chunks:
            rho = V0[0, 1 + c:1 + c + CHUNK, :, lanes]
            between = jnp.where(iota(rho.shape, 1) == 7, 0.0, coupling(rho, pltpu.roll(rho, 7, 1)))
            C0[0, c:c + CHUNK, :, lanes] = between
            C0[1, c:c + CHUNK, :, lanes] = pltpu.roll(between, 1, 1)

    def couple0_ends(lanes):
        for c in chunks:
            rho = V0[0, 1 + c:1 + c + CHUNK, :, lanes]
            row = iota(rho.shape, 1)
            CB0[c:c + CHUNK, :, lanes] = jnp.where((row == 0) | (row == 7), coupling(rho, outer(0, c, lanes)), 0.0)

    SRC[:, :, own] = src[...]
    couple0(own, range(1, 16))
    couple0_y(own)
    for c in chunks:
        rho = V0[0, 1 + c:1 + c + CHUNK, :, own]
        between = coupling(rho, pltpu.roll(rho, 255, 2))
        C0[2, c:c + CHUNK, :, own] = between
        C0[3, c:c + CHUNK, :, own] = pltpu.roll(between, 1, 2)
    arrived(rho0_faces)
    trim0(0, own)
    couple0(own, (0, 16))
    couple0_ends(own)
    for group, there in ((to_below, above), (to_above, below)):
        @pl.when(there)
        def _():
            arrived(group[:5])
    first, second = unpack_z0(0)
    V0[0, 1:9, :, ring] = first
    V0[0, 9:17, :, ring] = second
    lane8, lane2 = iota((8, 128), 1), iota((16, 128), 1)
    for side in (0, 1):
        V0[0, 17 * side, :, ring] = jnp.where(
            lane8 < 64, jnp.where(above, HX[side, 1], 0.0), jnp.where(below, HX[side, 0], 0.0))
        YH0[0, side, :, ring] = jnp.where(
            lane2 < 64, jnp.where(above, HY[side, 1], 0.0), jnp.where(below, HY[side, 0], 0.0))
    trim0(0, ring)
    couple0(ring, range(17))
    couple0_y(ring)
    couple0_ends(ring)
    for c in chunks:
        some = slice(c, c + CHUNK)
        rho = V0[0, 1 + c:1 + c + CHUNK]
        outside = rho[:, :, ring]
        lane = iota(outside.shape, 2)
        up = jnp.where(lane == 127, pltpu.roll(rho[:, :, 0:128], 127, 2), pltpu.roll(outside, 127, 2))
        down = jnp.where(lane == 0, pltpu.roll(rho[:, :, 128:256], 1, 2), pltpu.roll(outside, 1, 2))
        up, down = coupling(outside, up), coupling(outside, down)
        C0[2, some, :, ring] = up
        C0[3, some, :, ring] = down
        C0[2, some, :, 128:256] = jnp.where(lane == 127, pltpu.roll(down, 127, 2), C0[2, some, :, 128:256])
        C0[3, some, :, 0:128] = jnp.where(lane == 0, pltpu.roll(up, 1, 2), C0[3, some, :, 0:128])
        between, after = C0[2, some], C0[3, some]
        diag = (CX0[some] + CX0[c + 1:c + 1 + CHUNK]) + (between + after) + (C0[0, some] + C0[1, some] + CB0[some])
        DIAG0[some] = diag
        INV0[some] = jnp.where(rho > 0.0, RELAXATION / diag, 0.0)
    for group, there in ((to_below, above), (to_above, below)):
        @pl.when(there)
        def _():
            arrived(group[5:])
    first, second = unpack_z0(1)
    SRC[0:8, :, ring] = first
    SRC[8:16, :, ring] = second

    for c in chunks:
        v = INV0[c:c + CHUNK] * SRC[c:c + CHUNK]
        V0[1, 1 + c:1 + c + CHUNK] = v
        pack_y0(1, c, v)
    v1_faces = faces0(1)
    for group, there in ((to_below, below), (to_above, above)):
        @pl.when(there)
        def _():
            left(group)
    for c in chunks:
        some = slice(c, c + CHUNK)
        v, total = inner(1, c)
        V0[2, 1 + c:1 + c + CHUNK] = KEEP * v + INV0[some] * (SRC[some] + total)
        KB0[some] = INV0[some] * CB0[some]

    row8 = iota((8, 256), 0)
    row8s = iota((8, 128), 0)

    row24 = iota((8, 384), 0)

    def down0(plane):
        tiles = []
        for j in range(4):
            t, u = (plane(4 * j + n) + plane(4 * j + n + 1) for n in (0, 2))
            t, u = (x + pltpu.roll(x, 7, 0) for x in (t, u))
            tile = pltpu.roll(u, 1, 0)
            for n, part in ((7, pltpu.roll(u, 2, 0)), (6, pltpu.roll(u, 3, 0)), (5, pltpu.roll(u, 4, 0)),
                            (4, pltpu.roll(t, 5, 0)), (3, pltpu.roll(t, 6, 0)), (2, pltpu.roll(t, 7, 0)), (1, t)):
                tile = jnp.where(row24 < n, part, tile)
            tiles.append(tile)
        t = dot(jnp.concatenate(tiles, axis=0), pairs0)
        return [t[8 * j:8 * j + 8] for j in range(4)]

    def slot(a, b):
        return SIDES.index((a, b))

    def exchange1(k, packed):
        for j in range(4):
            S1[k, j] = packed[j]
        group = []
        for a, b in ((1, 1), (1, -1), (-1, 1), (-1, -1), (0, 1), (0, -1), (1, 0), (-1, 0)):
            some = {1: pl.ds(2, 2), -1: pl.ds(0, 2), 0: pl.ds(0, 4)}[a]
            if k and a and b:
                some = pl.ds(3 if a > 0 else 0, 1)
            group.append(post(S1.at[k, some], H1.at[k, slot(-a, -b), some], {"gx": a, "gy": b}))
        return group

    def unpack1(k, target, first, last, offset):
        for p in range(first, last):
            a = p // 8
            j, half = (p % 8) // 2, p % 2

            def block(b):
                if not a and not b:
                    return S1[k, j]
                if k and a and b and j in (1, 2):
                    return jnp.zeros((8, 256), f32)
                return jnp.where(exists("gx", a) & exists("gy", b), H1[k, slot(a, b), j], 0.0)

            target[p - offset, 0:8] = jnp.where(row8 < 4, turn(block(0), -4 * half, 0), turn(block(1), 4 - 4 * half, 0))
            target[p - offset, 8:16] = jnp.where(row8 < 4, 0.0, turn(block(-1), 4 - 4 * half, 0))

    def shifts1(v):
        return pltpu.roll(v, 15, 0), pltpu.roll(v, 1, 0), pltpu.roll(v, 255, 1), pltpu.roll(v, 1, 1)

    def around1(V, p, base):
        v = V[p - base]
        total = CX1[p + 3] * V[p - 1 - base] + CX1[p + 4] * V[p + 1 - base]
        for n, other in enumerate(shifts1(v)):
            total = total + C1[n, p + 3] * other
        return v, total

    def down1(plane):
        packed = jnp.zeros((8, 256), f32)
        for x in range(4):
            t = plane(2 * x) + plane(2 * x + 1)
            t = t + pltpu.roll(t, 7, 0)
            for half in range(2):
                packed = jnp.where(row8 == 2 * x + half, turn(t, 2 * x - half, 0), packed)
        return dot(packed, pairs1)

    packed1 = [0.125 * t for t in down0(lambda p: V0[0, 1 + p])]
    rho1_copies = exchange1(0, packed1)
    G[gy] = 0.125 * down1(lambda p: packed1[p // 2] if p % 2 == 0 else pltpu.roll(packed1[p // 2], 4, 0))
    rho2_y = [post(G.at[gy], G.at[gy], {"gy": d}) for d in (1, 2, 3)]

    arrived(v1_faces)
    trim0(1)
    for c in chunks:
        for i, term in ends(1, c).items():
            V0[2, 1 + i] = V0[2, 1 + i] + INV0[i] * term
        v = V0[2, 1 + c:1 + c + CHUNK] + KB0[c:c + CHUNK] * outer(1, c)
        V0[2, 1 + c:1 + c + CHUNK] = v
        pack_y0(2, c, v)
    v2_faces = faces0(2)
    for c in chunks:
        v, total = inner(2, c)
        R0[c:c + CHUNK] = SRC[c:c + CHUNK] + total - DIAG0[c:c + CHUNK] * v

    def rows_of(blocks):
        planes = []
        for x in range(4):
            t = turn(blocks[0], -2 * x, 0)
            for q in (1, 2, 3):
                t = jnp.where(row8s < 2 * q, t, turn(blocks[q], 2 * (q - x), 0))
            planes.append(t)
        return planes

    arrived(rho2_y)
    for x, t in enumerate(rows_of([G[q] for q in range(4)])):
        XD[9 + x] = t
    rho2_x = [post(XD.at[9:13], XD.at[9 - 4 * d:13 - 4 * d], {"gx": d}) for d in (-2, -1, 1, 2)]
    rho2_x += [post(XD.at[12], XD.at[0], {"gx": 3}), post(XD.at[9], XD.at[21], {"gx": -3})]

    arrived(rho1_copies)
    unpack1(0, RHO1, -4, 12, -4)
    for p in range(-3, 12):
        CX1[p + 3] = coupling(RHO1[p + 3], RHO1[p + 4])
    for p in range(-3, 11):
        rho = RHO1[p + 4]
        diag = CX1[p + 3] + CX1[p + 4]
        for n, other in enumerate(shifts1(rho)):
            between = coupling(rho, other)
            C1[n, p + 3] = between
            diag = diag + between
        INV1[p + 3] = jnp.where(rho > 0.0, RELAXATION / diag, 0.0)
        if 0 <= p < 8:
            DIAG1[p] = diag

    arrived(v2_faces)
    trim0(2)
    residual = []
    for c in chunks:
        r = R0[c:c + CHUNK] + CB0[c:c + CHUNK] * outer(2, c)
        more = ends(2, c)
        residual += [r[i] + more[c + i] if c + i in more else r[i] for i in range(CHUNK)]
    b1_copies = exchange1(1, [0.5 * t for t in down0(lambda p: residual[p])])

    arrived(rho2_x)
    for d in (-2, -1, 1, 2):
        XD[9 - 4 * d:13 - 4 * d] = jnp.where(exists("gx", -d), XD[9 - 4 * d:13 - 4 * d], 0.0)
    XD[0] = jnp.where(exists("gx", -3), XD[0], 0.0)
    XD[21] = jnp.where(exists("gx", 3), XD[21], 0.0)
    row2 = iota((20, 8, 128), 1)
    rho = XD[1:21]
    cx2 = coupling(XD[0:21], XD[1:22])
    y_up = coupling(rho, jnp.where(row2 == 7, 0.0, pltpu.roll(rho, 7, 1)))
    y_down = coupling(rho, jnp.where(row2 == 0, 0.0, pltpu.roll(rho, 1, 1)))
    z_up = coupling(rho, pltpu.roll(rho, 127, 2))
    z_down = coupling(rho, pltpu.roll(rho, 1, 2))
    diag2 = cx2[0:20] + cx2[1:21] + ((y_up + y_down) + (z_up + z_down))
    inv2 = jnp.where(rho > 0.0, RELAXATION / diag2, 0.0)
    y_up = jnp.where(row2 == 7, 0.0, y_up)
    y_down = jnp.where(row2 == 0, 0.0, y_down)

    arrived(b1_copies)
    unpack1(1, B1, -3, 11, -3)
    for p in range(-3, 11):
        W1[p + 3] = INV1[p + 3] * B1[p + 3]
    near, far = slice(0, 8), slice(8, 16)

    def second1(p, rows):
        v, total = around1(W1, p, -3)
        for some in rows:
            W2[p + 2, some] = (KEEP * v + INV1[p + 3] * (B1[p + 3] + total))[some]

    for p in range(-1, 9):
        second1(p, (near, far) if 0 <= p < 8 else (near,))
    residual = []
    for p in range(8):
        v, total = around1(W2, p, -2)
        residual.append((B1[p + 3] + total - DIAG1[p] * v)[near])

    GB[2, gy] = 0.5 * down1(lambda p: residual[p])
    b2_copies = [post(GB.at[2, gy], GB.at[2 - d, gy], {"gx": d, "gy": e})
                 for e in (2, 1, 3, 0) for d in (2, -2, 1, -1, 0) if d or e]
    @pl.when(gx >= 0)
    def _():
        second1(-2, (near,))
        second1(-1, (far,))
        second1(8, (far,))
        second1(9, (near,))
        for p in range(-1, 9):
            v, total = around1(W2, p, -2)
            v = KEEP * v + INV1[p + 3] * (B1[p + 3] + total)
            for some in (near, far) if 0 <= p < 8 else (near,):
                E1[p + 1, some] = v[some]
        for c in chunks:
            v, total = inner(2, c)
            more = ends(2, c)
            total = total + CB0[c:c + CHUNK] * outer(2, c)
            total = jnp.stack([total[i] + more[c + i] if c + i in more else total[i] for i in range(CHUNK)])
            v = KEEP * v + INV0[c:c + CHUNK] * (SRC[c:c + CHUNK] + total)
            out[c:c + CHUNK] = v[:, :, own]
    late = {id(copy) for copy in b2_copies + to_below + to_above}
    left([copy for copy in copies if id(copy) not in late])
    arrived(b2_copies)
    planes = []
    for d in (-2, -1, 0, 1, 2):
        planes += [jnp.where(exists("gx", d), t, 0.0) if d else t for t in rows_of([GB[2 + d, q] for q in range(4)])]
    b2 = jnp.stack(planes)
    v = inv2 * b2
    for k in range(1, COARSE_SWEEPS):
        z = 20 - k
        here = v[1:-1]
        total = cx2[k:z] * v[:-2] + cx2[k + 1:z + 1] * v[2:]
        total = total + y_up[k:z] * pltpu.roll(here, 7, 1) + y_down[k:z] * pltpu.roll(here, 1, 1)
        total = total + z_up[k:z] * pltpu.roll(here, 127, 2) + z_down[k:z] * pltpu.roll(here, 1, 2)
        v = KEEP * here + inv2[k:z] * (b2[k:z] + total)

    row6 = iota((6, 8, 128), 1)
    t = pltpu.roll(v, lax.rem(8 - 2 * gy, 8), 1)
    over = jnp.where(row6 < jnp.where(exists("gy", 1), 8, 4), grow(t, 1), 0.0)
    under = jnp.where(row6 >= jnp.where(exists("gy", -1), 6, 8), jnp.where(row6 == 7, t, pltpu.roll(t, 7, 1)), 0.0)
    t = dot(jnp.concatenate([over, under], axis=1).reshape(96, 128), spread1).reshape(6, 16, 256)
    moved = [shifts1(t[j]) for j in range(6)]
    for p in range(-1, 9):
        j = p // 2 + 1
        total = CX1[p + 3] * t[(p - 1) // 2 + 1] + CX1[p + 4] * t[(p + 1) // 2 + 1]
        for n, other in enumerate(moved[j]):
            total = total + C1[n, p + 3] * other
        v = E1[p + 1] + (KEEP * t[j] + INV1[p + 3] * total)
        for some in (near, far) if 0 <= p < 8 else (near,):
            E1[p + 1, some] = v[some]

    y_low = jnp.zeros((8, 256), f32)
    y_high = y_low
    for p in range(8):
        y_low = jnp.where(row8 == p, turn(E1[p + 1, far], p - 7, 0), y_low)
        y_high = jnp.where(row8 == p, turn(E1[p + 1, near], p - 4, 0), y_high)
    e = dot(jnp.concatenate([grow(E1[p, near], 0) for p in range(10)] + [y_low, y_high], axis=0), spread0)
    for m in range(8):
        here = e[8 * m + 8:8 * m + 16]
        beside = [x[:, own] for x in (pltpu.roll(here, 7, 0), pltpu.roll(here, 1, 0), pltpu.roll(here, 383, 1), pltpu.roll(here, 1, 1))]
        outside = jnp.where(row8 < 4, jnp.broadcast_to(e[80 + m:81 + m, own], (8, 256)), jnp.broadcast_to(e[88 + m:89 + m, own], (8, 256)))
        here = here[:, own]
        ways = ((e[8 * m:8 * m + 8, own], here), (here, e[8 * m + 16:8 * m + 24, own]))
        for i, (under, over) in zip((2 * m, 2 * m + 1), ways):
            total = CX0[i, :, own] * under + CX0[i + 1, :, own] * over + CB0[i, :, own] * outside
            for n in range(4):
                total = total + C0[n, i, :, own] * beside[n]
            out[i] = out[i] + (KEEP * here + INV0[i, :, own] * total)

    left(b2_copies)


def shards(source, phase_mask, density_factor):
    f32 = jnp.float32
    shapes = [
        (3, 18, 8, 384), (16, 8, 384), (3, 2, 16, 384), (3, 2, 16, 384), (2, 2, 8, 8, 128), (2, 2, 8, 8, 128),
        (2, 2, 8, 128), (2, 2, 16, 128), (17, 8, 384), (4, 16, 8, 384), (16, 8, 384), (16, 8, 384),
        (16, 8, 384), (16, 8, 384), (16, 8, 384),
        (2, 4, 8, 256), (2, 8, 4, 8, 256), (16, 16, 256), (15, 16, 256), (4, 14, 16, 256), (14, 16, 256), (8, 16, 256),
        (14, 16, 256), (14, 16, 256), (12, 16, 256), (10, 16, 256), (4, 8, 128), (5, 4, 8, 128), (22, 8, 128),
    ]
    return pl.pallas_call(
        kernel,
        out_shape=pltpu.VMEM((16, 8, 256), f32),
        in_specs=[pl.BlockSpec(memory_space=pl.ANY)] * 3,
        out_specs=pl.BlockSpec(memory_space=pltpu.VMEM),
        scratch_shapes=[pltpu.VMEM((16, 8, 256), kind) for kind in (f32, jnp.int32, f32)] + [pltpu.SemaphoreType.DMA((3,))]
        + [pltpu.VMEM(shape, f32) for shape in shapes] + [pltpu.SemaphoreType.DMA((COPIES,))] * 2,
        compiler_params=pltpu.CompilerParams(collective_id=0, has_side_effects=True),
        name="vcycle",
    )(source, phase_mask, density_factor)


def solution(mesh):
    spec = P("gx", "gy", "gz")
    return jax.shard_map(shards, mesh=mesh, in_specs=(spec,) * 3, out_specs=spec, check_vma=False)
```

```python
import jax
import jax.numpy as jnp
from jax import lax
from jax.experimental import pallas as pl
from jax.experimental.pallas import tpu as pltpu
from jax.sharding import PartitionSpec as P

GAS_DENSITY = 0.001
RELAXATION = 0.8
KEEP = 1.0 - RELAXATION
COARSE_SWEEPS = 8
MESH = pl.DeviceIdType.MESH
CHUNK = 2
COPIES = 68
TINY = 1e-30
AXES = ("gx", "gy", "gz")
SIDES = [(a, b) for a in (-1, 0, 1) for b in (-1, 0, 1) if a or b]


def iota(shape, axis):
    return lax.broadcasted_iota(jnp.int32, shape, axis)


def dot(a, b):
    high = a.astype(jnp.bfloat16)
    rest = a - high.astype(jnp.float32)
    middle = rest.astype(jnp.bfloat16)
    low = (rest - middle.astype(jnp.float32)).astype(jnp.bfloat16)
    return sum(jnp.dot(part, b, preferred_element_type=jnp.float32) for part in (low, middle, high))


def ones_where(condition):
    return jnp.where(condition, 1.0, 0.0).astype(jnp.bfloat16)


def turn(x, shift, axis):
    shift %= x.shape[axis]
    return pltpu.roll(x, shift, axis) if shift else x


def coupling(a, b):
    return 2.0 / jnp.maximum(a + b, TINY)


def grow(t, axis):
    row = iota(t.shape, axis)
    moved = [t] + [pltpu.roll(t, n, axis) for n in (1, 2, 3, 4)]
    low = jnp.where(row < 1, moved[0], jnp.where(row < 3, moved[1], moved[2]))
    high = jnp.where(row < 5, moved[2], jnp.where(row < 7, moved[3], moved[4]))
    return jnp.where(row < 4, low, high)


def kernel(src_in, mask_in, fac_in, out, src, mask, fac, in_sem, V0, SRC, YS0, YH0, ZS, ZH, HX, HY, CX0, C0, CB0, KB0, INV0, DIAG0, R0,
           S1, H1, RHO1, CX1, C1, INV1, DIAG1, B1, W1, W2, E1, G, GB, XD, send_sem, recv_sem):
    f32 = jnp.float32
    sizes = {axis: lax.axis_size(axis) for axis in AXES}
    at = {axis: lax.axis_index(axis) for axis in AXES}
    gx, gy = at["gx"], at["gy"]

    def peer(way):
        return {axis: lax.rem(at[axis] + (d + sizes[axis]), sizes[axis]) for axis, d in way.items() if d}

    def exists(axis, d):
        place = at[axis] + d
        return (place >= 0) & (place < sizes[axis])

    above, below = exists("gz", 1), exists("gz", -1)
    copies = []

    def ready(source, target, way):
        k = len(copies)
        copy = pltpu.make_async_remote_copy(
            src_ref=source, dst_ref=target, send_sem=send_sem.at[k], recv_sem=recv_sem.at[k],
            device_id=peer(way), device_id_type=MESH)
        copies.append(copy)
        return copy

    def post(source, target, way):
        copy = ready(source, target, way)
        copy.start()
        return copy

    def arrived(group):
        for copy in group:
            copy.wait_recv()

    def left(group):
        for copy in group:
            copy.wait_send()

    inputs = [pltpu.make_async_copy(a, b, in_sem.at[n]) for n, (a, b) in enumerate(((fac_in, fac), (mask_in, mask), (src_in, src)))]
    for copy in inputs:
        copy.start()

    barrier = pltpu.get_barrier_semaphore()
    steady = [{"gx": a, "gy": b} for a in (0, -1, 1, -2, 2) for b in (0, 1, 3, 2) if a or b] + [{"gx": -3}, {"gx": 3}]
    across = [{}, {"gx": -1}, {"gx": 1}, {"gy": -1}, {"gy": 1}]
    for d, there in ((-1, below), (1, above)):
        ids = [peer({**way, "gz": d}) for way in across]

        @pl.when(there)
        def _():
            for other in ids:
                pl.semaphore_signal(barrier, inc=1, device_id=other, device_id_type=MESH)
    for way in steady:
        pl.semaphore_signal(barrier, inc=1, device_id=peer(way), device_id_type=MESH)

    lane16 = iota((8, 8, 128), 2)
    chunks = range(0, 16, CHUNK)
    own, ring = slice(0, 256), slice(256, 384)

    def pack_y0(k, c, v):
        n = v.shape[-1]
        for i in range(v.shape[0]):
            YS0[k, 0, c + i:c + i + 1, 0:n] = v[i, 0:1, :]
            YS0[k, 1, c + i:c + i + 1, 0:n] = v[i, 7:8, :]

    def outer(k, c, lanes=slice(0, 384)):
        shape = (8, lanes.stop - lanes.start)
        first = iota(shape, 0) < 4
        return jnp.stack([jnp.where(first, jnp.broadcast_to(YH0[k, 0, c + i:c + i + 1, lanes], shape),
                                    jnp.broadcast_to(YH0[k, 1, c + i:c + i + 1, lanes], shape)) for i in range(CHUNK)])

    def inner(k, c):
        v = V0[k, 1 + c:1 + c + CHUNK]
        parts = []
        for i in range(c, c + CHUNK):
            terms = ([CX0[i] * V0[k, i]] if i else []) + ([CX0[i + 1] * V0[k, i + 2]] if i < 15 else [])
            parts.append(sum(terms[1:], terms[0]))
        total = jnp.stack(parts) + C0[0, c:c + CHUNK] * pltpu.roll(v, 7, 1) + C0[1, c:c + CHUNK] * pltpu.roll(v, 1, 1)
        return v, total + C0[2, c:c + CHUNK] * pltpu.roll(v, 383, 2) + C0[3, c:c + CHUNK] * pltpu.roll(v, 1, 2)

    def ends(k, c):
        return {i: CX0[i + (i == 15)] * V0[k, 17 if i else 0] for i in (0, 15) if c <= i < c + CHUNK}

    def faces0(k):
        return [post(YS0.at[k, 0], YH0.at[k, 1], {"gy": -1}), post(YS0.at[k, 1], YH0.at[k, 0], {"gy": 1}),
                post(V0.at[k, 1], V0.at[k, 17], {"gx": -1}), post(V0.at[k, 16], V0.at[k, 0], {"gx": 1})]

    def trim0(k, lanes=slice(0, 384)):
        for side, d in ((0, -1), (1, 1)):
            V0[k, 17 * side, :, lanes] = jnp.where(exists("gx", d), V0[k, 17 * side, :, lanes], 0.0)
            YH0[k, side, :, lanes] = jnp.where(exists("gy", d), YH0[k, side, :, lanes], 0.0)

    def pack_z0(n, field):
        low, high = field[:, :, 0:128], field[:, :, 128:256]
        ZS[n, 0] = jnp.where(lane16 < 64, low[0:8], pltpu.roll(low[8:16], 64, 2))
        ZS[n, 1] = jnp.where(lane16 < 64, pltpu.roll(high[0:8], 64, 2), high[8:16])

    def unpack_z0(n):
        up, down = jnp.where(above, ZH[n, 1], 0.0), jnp.where(below, ZH[n, 0], 0.0)
        return (jnp.where(lane16 < 64, up, pltpu.roll(down, 64, 2)), jnp.where(lane16 < 64, pltpu.roll(up, 64, 2), down))

    inputs[0].wait()
    inputs[1].wait()
    rho = jnp.where(mask[...] == 1, GAS_DENSITY, 1.0) * fac[...]
    V0[0, 1:17, :, own] = rho
    pack_z0(0, rho)
    pack_y0(0, 0, rho)
    inputs[2].wait()
    pack_z0(1, src[...])
    two = jnp.where(above, 1, 0) + jnp.where(below, 1, 0)
    pl.semaphore_wait(barrier, len(steady) + len(across) * two)

    low, high = pl.ds(0, 128), pl.ds(128, 128)
    to_below = [ready(ZS.at[0, 0], ZH.at[0, 1], {"gz": -1}),
                ready(V0.at[0, 1, :, low], HX.at[1, 1], {"gx": -1, "gz": -1}),
                ready(V0.at[0, 16, :, low], HX.at[0, 1], {"gx": 1, "gz": -1}),
                ready(YS0.at[0, 0, :, low], HY.at[1, 1], {"gy": -1, "gz": -1}),
                ready(YS0.at[0, 1, :, low], HY.at[0, 1], {"gy": 1, "gz": -1}),
                ready(ZS.at[1, 0], ZH.at[1, 1], {"gz": -1})]
    to_above = [ready(ZS.at[0, 1], ZH.at[0, 0], {"gz": 1}),
                ready(V0.at[0, 1, :, high], HX.at[1, 0], {"gx": -1, "gz": 1}),
                ready(V0.at[0, 16, :, high], HX.at[0, 0], {"gx": 1, "gz": 1}),
                ready(YS0.at[0, 0, :, high], HY.at[1, 0], {"gy": -1, "gz": 1}),
                ready(YS0.at[0, 1, :, high], HY.at[0, 0], {"gy": 1, "gz": 1}),
                ready(ZS.at[1, 1], ZH.at[1, 0], {"gz": 1})]
    for some in (slice(1, 5), slice(0, 1)):
        for group, there in ((to_below, below), (to_above, above)):
            @pl.when(there)
            def _():
                for copy in group[some]:
                    copy.start()
    both = pl.ds(0, 256)
    rho0_faces = [post(V0.at[0, 1, :, both], V0.at[0, 17, :, both], {"gx": -1}),
                  post(V0.at[0, 16, :, both], V0.at[0, 0, :, both], {"gx": 1}),
                  post(YS0.at[0, 0, :, both], YH0.at[0, 1, :, both], {"gy": -1}),
                  post(YS0.at[0, 1, :, both], YH0.at[0, 0, :, both], {"gy": 1})]
    for group, there in ((to_below, below), (to_above, above)):
        @pl.when(there)
        def _():
            group[5].start()

    a, b = lax.shift_right_logical(iota((384, 256), 0), 1), iota((384, 256), 1)
    pairs0 = ones_where(b == jnp.where(a < 160, a, a + 64))
    pairs1 = ones_where(lax.shift_right_logical(iota((256, 128), 0), 1) == iota((256, 128), 1))
    a, b = iota((256, 384), 0), lax.shift_right_logical(iota((256, 384), 1), 1)
    spread0 = ones_where(a == jnp.where(b < 160, b, b + 64))
    spread1 = ones_where(iota((128, 256), 0) == lax.shift_right_logical(iota((128, 256), 1), 1))

    def couple0(lanes, planes):
        for c in planes:
            CX0[c, :, lanes] = coupling(V0[0, c, :, lanes], V0[0, c + 1, :, lanes])

    def couple0_y(lanes):
        for c in chunks:
            rho = V0[0, 1 + c:1 + c + CHUNK, :, lanes]
            between = jnp.where(iota(rho.shape, 1) == 7, 0.0, coupling(rho, pltpu.roll(rho, 7, 1)))
            C0[0, c:c + CHUNK, :, lanes] = between
            C0[1, c:c + CHUNK, :, lanes] = pltpu.roll(between, 1, 1)

    def couple0_ends(lanes):
        for c in chunks:
            rho = V0[0, 1 + c:1 + c + CHUNK, :, lanes]
            row = iota(rho.shape, 1)
            CB0[c:c + CHUNK, :, lanes] = jnp.where((row == 0) | (row == 7), coupling(rho, outer(0, c, lanes)), 0.0)

    SRC[:, :, own] = src[...]
    couple0(own, range(1, 16))
    couple0_y(own)
    for c in chunks:
        rho = V0[0, 1 + c:1 + c + CHUNK, :, own]
        between = coupling(rho, pltpu.roll(rho, 255, 2))
        C0[2, c:c + CHUNK, :, own] = between
        C0[3, c:c + CHUNK, :, own] = pltpu.roll(between, 1, 2)
    arrived(rho0_faces)
    trim0(0, own)
    couple0(own, (0, 16))
    couple0_ends(own)
    def await_z(some):
        for group, there in ((to_below, above), (to_above, below)):
            @pl.when(there)
            def _():
                arrived(group[some])

    def invert0(lanes):
        for c in chunks:
            some = slice(c, c + CHUNK)
            diag = ((CX0[some, :, lanes] + CX0[c + 1:c + 1 + CHUNK, :, lanes]) + (C0[2, some, :, lanes] + C0[3, some, :, lanes])
                    + (C0[0, some, :, lanes] + C0[1, some, :, lanes] + CB0[some, :, lanes]))
            DIAG0[some, :, lanes] = diag
            INV0[some, :, lanes] = jnp.where(V0[0, 1 + c:1 + c + CHUNK, :, lanes] > 0.0, RELAXATION / diag, 0.0)

    await_z(slice(0, 1))
    first, second = unpack_z0(0)
    V0[0, 1:9, :, ring] = first
    V0[0, 9:17, :, ring] = second
    couple0(ring, range(1, 16))
    couple0_y(ring)
    for c in chunks:
        some = slice(c, c + CHUNK)
        rho = V0[0, 1 + c:1 + c + CHUNK]
        outside = rho[:, :, ring]
        lane = iota(outside.shape, 2)
        up = jnp.where(lane == 127, pltpu.roll(rho[:, :, 0:128], 127, 2), pltpu.roll(outside, 127, 2))
        down = jnp.where(lane == 0, pltpu.roll(rho[:, :, 128:256], 1, 2), pltpu.roll(outside, 1, 2))
        up, down = coupling(outside, up), coupling(outside, down)
        C0[2, some, :, ring] = up
        C0[3, some, :, ring] = down
        C0[2, some, :, 128:256] = jnp.where(lane == 127, pltpu.roll(down, 127, 2), C0[2, some, :, 128:256])
        C0[3, some, :, 0:128] = jnp.where(lane == 0, pltpu.roll(up, 1, 2), C0[3, some, :, 0:128])
    invert0(own)
    await_z(slice(1, 5))
    lane8, lane2 = iota((8, 128), 1), iota((16, 128), 1)
    for side in (0, 1):
        V0[0, 17 * side, :, ring] = jnp.where(
            lane8 < 64, jnp.where(above, HX[side, 1], 0.0), jnp.where(below, HX[side, 0], 0.0))
        YH0[0, side, :, ring] = jnp.where(
            lane2 < 64, jnp.where(above, HY[side, 1], 0.0), jnp.where(below, HY[side, 0], 0.0))
    trim0(0, ring)
    couple0(ring, (0, 16))
    couple0_ends(ring)
    invert0(ring)
    await_z(slice(5, 6))
    first, second = unpack_z0(1)
    SRC[0:8, :, ring] = first
    SRC[8:16, :, ring] = second

    for c in chunks:
        v = INV0[c:c + CHUNK] * SRC[c:c + CHUNK]
        V0[1, 1 + c:1 + c + CHUNK] = v
        pack_y0(1, c, v)
    v1_faces = faces0(1)
    for group, there in ((to_below, below), (to_above, above)):
        @pl.when(there)
        def _():
            left(group)
    for c in chunks:
        some = slice(c, c + CHUNK)
        v, total = inner(1, c)
        V0[2, 1 + c:1 + c + CHUNK] = KEEP * v + INV0[some] * (SRC[some] + total)
        KB0[some] = INV0[some] * CB0[some]

    row8 = iota((8, 256), 0)
    row8s = iota((8, 128), 0)

    row24 = iota((8, 384), 0)

    def down0(plane):
        tiles = []
        for j in range(4):
            t, u = (plane(4 * j + n) + plane(4 * j + n + 1) for n in (0, 2))
            t, u = (x + pltpu.roll(x, 7, 0) for x in (t, u))
            tile = pltpu.roll(u, 1, 0)
            for n, part in ((7, pltpu.roll(u, 2, 0)), (6, pltpu.roll(u, 3, 0)), (5, pltpu.roll(u, 4, 0)),
                            (4, pltpu.roll(t, 5, 0)), (3, pltpu.roll(t, 6, 0)), (2, pltpu.roll(t, 7, 0)), (1, t)):
                tile = jnp.where(row24 < n, part, tile)
            tiles.append(tile)
        t = dot(jnp.concatenate(tiles, axis=0), pairs0)
        return [t[8 * j:8 * j + 8] for j in range(4)]

    def slot(a, b):
        return SIDES.index((a, b))

    def exchange1(k, packed):
        for j in range(4):
            S1[k, j] = packed[j]
        group = []
        for a, b in ((1, 1), (1, -1), (-1, 1), (-1, -1), (0, 1), (0, -1), (1, 0), (-1, 0)):
            some = {1: pl.ds(2, 2), -1: pl.ds(0, 2), 0: pl.ds(0, 4)}[a]
            if k and a and b:
                some = pl.ds(3 if a > 0 else 0, 1)
            group.append(post(S1.at[k, some], H1.at[k, slot(-a, -b), some], {"gx": a, "gy": b}))
        return group

    def unpack1(k, target, first, last, offset):
        for p in range(first, last):
            a = p // 8
            j, half = (p % 8) // 2, p % 2

            def block(b):
                if not a and not b:
                    return S1[k, j]
                if k and a and b and j in (1, 2):
                    return jnp.zeros((8, 256), f32)
                return jnp.where(exists("gx", a) & exists("gy", b), H1[k, slot(a, b), j], 0.0)

            target[p - offset, 0:8] = jnp.where(row8 < 4, turn(block(0), -4 * half, 0), turn(block(1), 4 - 4 * half, 0))
            target[p - offset, 8:16] = jnp.where(row8 < 4, 0.0, turn(block(-1), 4 - 4 * half, 0))

    def shifts1(v):
        return pltpu.roll(v, 15, 0), pltpu.roll(v, 1, 0), pltpu.roll(v, 255, 1), pltpu.roll(v, 1, 1)

    def around1(V, p, base):
        v = V[p - base]
        total = CX1[p + 3] * V[p - 1 - base] + CX1[p + 4] * V[p + 1 - base]
        for n, other in enumerate(shifts1(v)):
            total = total + C1[n, p + 3] * other
        return v, total

    def down1(plane):
        packed = jnp.zeros((8, 256), f32)
        for x in range(4):
            t = plane(2 * x) + plane(2 * x + 1)
            t = t + pltpu.roll(t, 7, 0)
            for half in range(2):
                packed = jnp.where(row8 == 2 * x + half, turn(t, 2 * x - half, 0), packed)
        return dot(packed, pairs1)

    packed1 = [0.125 * t for t in down0(lambda p: V0[0, 1 + p])]
    rho1_copies = exchange1(0, packed1)
    G[gy] = 0.125 * down1(lambda p: packed1[p // 2] if p % 2 == 0 else pltpu.roll(packed1[p // 2], 4, 0))
    rho2_y = [post(G.at[gy], G.at[gy], {"gy": d}) for d in (1, 2, 3)]

    arrived(v1_faces)
    trim0(1)
    for c in chunks:
        for i, term in ends(1, c).items():
            V0[2, 1 + i] = V0[2, 1 + i] + INV0[i] * term
        v = V0[2, 1 + c:1 + c + CHUNK] + KB0[c:c + CHUNK] * outer(1, c)
        V0[2, 1 + c:1 + c + CHUNK] = v
        pack_y0(2, c, v)
    v2_faces = faces0(2)
    for c in chunks:
        v, total = inner(2, c)
        R0[c:c + CHUNK] = SRC[c:c + CHUNK] + total - DIAG0[c:c + CHUNK] * v

    def rows_of(blocks):
        planes = []
        for x in range(4):
            t = turn(blocks[0], -2 * x, 0)
            for q in (1, 2, 3):
                t = jnp.where(row8s < 2 * q, t, turn(blocks[q], 2 * (q - x), 0))
            planes.append(t)
        return planes

    arrived(rho2_y)
    for x, t in enumerate(rows_of([G[q] for q in range(4)])):
        XD[9 + x] = t
    rho2_x = [post(XD.at[9:13], XD.at[9 - 4 * d:13 - 4 * d], {"gx": d}) for d in (-2, -1, 1, 2)]
    rho2_x += [post(XD.at[12], XD.at[0], {"gx": 3}), post(XD.at[9], XD.at[21], {"gx": -3})]

    arrived(rho1_copies)
    unpack1(0, RHO1, -4, 12, -4)
    for p in range(-3, 12):
        CX1[p + 3] = coupling(RHO1[p + 3], RHO1[p + 4])
    for p in range(-3, 11):
        rho = RHO1[p + 4]
        diag = CX1[p + 3] + CX1[p + 4]
        for n, other in enumerate(shifts1(rho)):
            between = coupling(rho, other)
            C1[n, p + 3] = between
            diag = diag + between
        INV1[p + 3] = jnp.where(rho > 0.0, RELAXATION / diag, 0.0)
        if 0 <= p < 8:
            DIAG1[p] = diag

    arrived(v2_faces)
    trim0(2)
    residual = []
    for c in chunks:
        r = R0[c:c + CHUNK] + CB0[c:c + CHUNK] * outer(2, c)
        more = ends(2, c)
        residual += [r[i] + more[c + i] if c + i in more else r[i] for i in range(CHUNK)]
    b1_copies = exchange1(1, [0.5 * t for t in down0(lambda p: residual[p])])

    arrived(rho2_x)
    for d in (-2, -1, 1, 2):
        XD[9 - 4 * d:13 - 4 * d] = jnp.where(exists("gx", -d), XD[9 - 4 * d:13 - 4 * d], 0.0)
    XD[0] = jnp.where(exists("gx", -3), XD[0], 0.0)
    XD[21] = jnp.where(exists("gx", 3), XD[21], 0.0)
    row2 = iota((20, 8, 128), 1)
    rho = XD[1:21]
    cx2 = coupling(XD[0:21], XD[1:22])
    y_up = coupling(rho, jnp.where(row2 == 7, 0.0, pltpu.roll(rho, 7, 1)))
    y_down = coupling(rho, jnp.where(row2 == 0, 0.0, pltpu.roll(rho, 1, 1)))
    z_up = coupling(rho, pltpu.roll(rho, 127, 2))
    z_down = coupling(rho, pltpu.roll(rho, 1, 2))
    diag2 = cx2[0:20] + cx2[1:21] + ((y_up + y_down) + (z_up + z_down))
    inv2 = jnp.where(rho > 0.0, RELAXATION / diag2, 0.0)
    x_low, x_high = inv2 * cx2[0:20], inv2 * cx2[1:21]
    y_up = jnp.where(row2 == 7, 0.0, inv2 * y_up)
    y_down = jnp.where(row2 == 0, 0.0, inv2 * y_down)
    z_up, z_down = inv2 * z_up, inv2 * z_down

    arrived(b1_copies)
    unpack1(1, B1, -3, 11, -3)
    for p in range(-3, 11):
        W1[p + 3] = INV1[p + 3] * B1[p + 3]
    near, far = slice(0, 8), slice(8, 16)

    def second1(p, rows):
        v, total = around1(W1, p, -3)
        for some in rows:
            W2[p + 2, some] = (KEEP * v + INV1[p + 3] * (B1[p + 3] + total))[some]

    for p in range(-1, 9):
        second1(p, (near, far) if 0 <= p < 8 else (near,))
    residual = []
    for p in range(8):
        v, total = around1(W2, p, -2)
        residual.append((B1[p + 3] + total - DIAG1[p] * v)[near])

    GB[2, gy] = 0.5 * down1(lambda p: residual[p])
    b2_copies = [post(GB.at[2, gy], GB.at[2 - d, gy], {"gx": d, "gy": e})
                 for e in (2, 1, 3, 0) for d in (2, -2, 1, -1, 0) if d or e]
    @pl.when(gx >= 0)
    def _():
        second1(-2, (near,))
        second1(-1, (far,))
        second1(8, (far,))
        second1(9, (near,))
        for p in range(-1, 9):
            v, total = around1(W2, p, -2)
            v = KEEP * v + INV1[p + 3] * (B1[p + 3] + total)
            for some in (near, far) if 0 <= p < 8 else (near,):
                E1[p + 1, some] = v[some]
        for c in chunks:
            v, total = inner(2, c)
            more = ends(2, c)
            total = total + CB0[c:c + CHUNK] * outer(2, c)
            total = jnp.stack([total[i] + more[c + i] if c + i in more else total[i] for i in range(CHUNK)])
            v = KEEP * v + INV0[c:c + CHUNK] * (SRC[c:c + CHUNK] + total)
            out[c:c + CHUNK] = v[:, :, own]
    late = {id(copy) for copy in to_below + to_above}
    left([copy for copy in copies if id(copy) not in late])
    arrived(b2_copies)
    planes = []
    for d in (-2, -1, 0, 1, 2):
        planes += [jnp.where(exists("gx", d), t, 0.0) if d else t for t in rows_of([GB[2 + d, q] for q in range(4)])]
    start = inv2 * jnp.stack(planes)
    v = start
    for k in range(1, COARSE_SWEEPS):
        z = 20 - k
        here = v[1:-1]
        total = x_low[k:z] * v[:-2] + x_high[k:z] * v[2:]
        total = total + y_up[k:z] * pltpu.roll(here, 7, 1) + y_down[k:z] * pltpu.roll(here, 1, 1)
        total = total + z_up[k:z] * pltpu.roll(here, 127, 2) + z_down[k:z] * pltpu.roll(here, 1, 2)
        v = (KEEP * here + start[k:z]) + total

    row6 = iota((6, 8, 128), 1)
    t = pltpu.roll(v, lax.rem(8 - 2 * gy, 8), 1)
    over = jnp.where(row6 < jnp.where(exists("gy", 1), 8, 4), grow(t, 1), 0.0)
    under = jnp.where(row6 >= jnp.where(exists("gy", -1), 6, 8), jnp.where(row6 == 7, t, pltpu.roll(t, 7, 1)), 0.0)
    t = dot(jnp.concatenate([over, under], axis=1).reshape(96, 128), spread1).reshape(6, 16, 256)
    moved = [shifts1(t[j]) for j in range(6)]
    for p in range(-1, 9):
        j = p // 2 + 1
        total = CX1[p + 3] * t[(p - 1) // 2 + 1] + CX1[p + 4] * t[(p + 1) // 2 + 1]
        for n, other in enumerate(moved[j]):
            total = total + C1[n, p + 3] * other
        v = E1[p + 1] + (KEEP * t[j] + INV1[p + 3] * total)
        for some in (near, far) if 0 <= p < 8 else (near,):
            E1[p + 1, some] = v[some]

    y_low = jnp.zeros((8, 256), f32)
    y_high = y_low
    for p in range(8):
        y_low = jnp.where(row8 == p, turn(E1[p + 1, far], p - 7, 0), y_low)
        y_high = jnp.where(row8 == p, turn(E1[p + 1, near], p - 4, 0), y_high)
    e = dot(jnp.concatenate([grow(E1[p, near], 0) for p in range(10)] + [y_low, y_high], axis=0), spread0)
    for m in range(8):
        here = e[8 * m + 8:8 * m + 16]
        beside = [x[:, own] for x in (pltpu.roll(here, 7, 0), pltpu.roll(here, 1, 0), pltpu.roll(here, 383, 1), pltpu.roll(here, 1, 1))]
        outside = jnp.where(row8 < 4, jnp.broadcast_to(e[80 + m:81 + m, own], (8, 256)), jnp.broadcast_to(e[88 + m:89 + m, own], (8, 256)))
        here = here[:, own]
        ways = ((e[8 * m:8 * m + 8, own], here), (here, e[8 * m + 16:8 * m + 24, own]))
        for i, (under, over) in zip((2 * m, 2 * m + 1), ways):
            total = CX0[i, :, own] * under + CX0[i + 1, :, own] * over + CB0[i, :, own] * outside
            for n in range(4):
                total = total + C0[n, i, :, own] * beside[n]
            out[i] = out[i] + (KEEP * here + INV0[i, :, own] * total)


def shards(source, phase_mask, density_factor):
    f32 = jnp.float32
    shapes = [
        (3, 18, 8, 384), (16, 8, 384), (3, 2, 16, 384), (3, 2, 16, 384), (2, 2, 8, 8, 128), (2, 2, 8, 8, 128),
        (2, 2, 8, 128), (2, 2, 16, 128), (17, 8, 384), (4, 16, 8, 384), (16, 8, 384), (16, 8, 384),
        (16, 8, 384), (16, 8, 384), (16, 8, 384),
        (2, 4, 8, 256), (2, 8, 4, 8, 256), (16, 16, 256), (15, 16, 256), (4, 14, 16, 256), (14, 16, 256), (8, 16, 256),
        (14, 16, 256), (14, 16, 256), (12, 16, 256), (10, 16, 256), (4, 8, 128), (5, 4, 8, 128), (22, 8, 128),
    ]
    return pl.pallas_call(
        kernel,
        out_shape=pltpu.VMEM((16, 8, 256), f32),
        in_specs=[pl.BlockSpec(memory_space=pl.ANY)] * 3,
        out_specs=pl.BlockSpec(memory_space=pltpu.VMEM),
        scratch_shapes=[pltpu.VMEM((16, 8, 256), kind) for kind in (f32, jnp.int32, f32)] + [pltpu.SemaphoreType.DMA((3,))]
        + [pltpu.VMEM(shape, f32) for shape in shapes] + [pltpu.SemaphoreType.DMA((COPIES,))] * 2,
        compiler_params=pltpu.CompilerParams(collective_id=0, has_side_effects=True),
        name="vcycle",
    )(source, phase_mask, density_factor)


def solution(mesh):
    spec = P("gx", "gy", "gz")
    return jax.shard_map(shards, mesh=mesh, in_specs=(spec,) * 3, out_specs=spec, check_vma=False)
```

```python
import jax
import jax.numpy as jnp
from jax import lax
from jax.experimental import pallas as pl
from jax.experimental.pallas import tpu as pltpu
from jax.sharding import PartitionSpec as P

GAS_DENSITY = 0.001
RELAXATION = 0.8
KEEP = 1.0 - RELAXATION
COARSE_SWEEPS = 8
MESH = pl.DeviceIdType.MESH
CHUNK = 2
COPIES = 68
TINY = 1e-30
AXES = ("gx", "gy", "gz")
SIDES = [(a, b) for a in (-1, 0, 1) for b in (-1, 0, 1) if a or b]


def iota(shape, axis):
    return lax.broadcasted_iota(jnp.int32, shape, axis)


def dot(a, b):
    high = a.astype(jnp.bfloat16)
    rest = a - high.astype(jnp.float32)
    middle = rest.astype(jnp.bfloat16)
    low = (rest - middle.astype(jnp.float32)).astype(jnp.bfloat16)
    return sum(jnp.dot(part, b, preferred_element_type=jnp.float32) for part in (low, middle, high))


def ones_where(condition):
    return jnp.where(condition, 1.0, 0.0).astype(jnp.bfloat16)


def turn(x, shift, axis):
    shift %= x.shape[axis]
    return pltpu.roll(x, shift, axis) if shift else x


def coupling(a, b):
    return 2.0 / jnp.maximum(a + b, TINY)


def grow(t, axis):
    row = iota(t.shape, axis)
    moved = [t] + [pltpu.roll(t, n, axis) for n in (1, 2, 3, 4)]
    low = jnp.where(row < 1, moved[0], jnp.where(row < 3, moved[1], moved[2]))
    high = jnp.where(row < 5, moved[2], jnp.where(row < 7, moved[3], moved[4]))
    return jnp.where(row < 4, low, high)


def kernel(src_in, mask_in, fac_in, out, src, mask, fac, in_sem, V0, SRC, YS0, YH0, ZS, ZH, HX, HY, CX0, C0, CB0, KB0, INV0, DIAG0, R0,
           S1, H1, RHO1, CX1, C1, INV1, DIAG1, B1, W1, W2, E1, G, GB, XD, send_sem, recv_sem):
    f32 = jnp.float32
    sizes = {axis: lax.axis_size(axis) for axis in AXES}
    at = {axis: lax.axis_index(axis) for axis in AXES}
    gx, gy = at["gx"], at["gy"]

    def peer(way):
        return {axis: lax.rem(at[axis] + (d + sizes[axis]), sizes[axis]) for axis, d in way.items() if d}

    def exists(axis, d):
        place = at[axis] + d
        return (place >= 0) & (place < sizes[axis])

    above, below = exists("gz", 1), exists("gz", -1)
    copies = []

    def ready(source, target, way):
        k = len(copies)
        copy = pltpu.make_async_remote_copy(
            src_ref=source, dst_ref=target, send_sem=send_sem.at[k], recv_sem=recv_sem.at[k],
            device_id=peer(way), device_id_type=MESH)
        copies.append(copy)
        return copy

    def post(source, target, way):
        copy = ready(source, target, way)
        copy.start()
        return copy

    def arrived(group):
        for copy in group:
            copy.wait_recv()

    def left(group):
        for copy in group:
            copy.wait_send()

    inputs = [pltpu.make_async_copy(a, b, in_sem.at[n]) for n, (a, b) in enumerate(((fac_in, fac), (mask_in, mask), (src_in, src)))]
    for copy in inputs:
        copy.start()

    barrier = pltpu.get_barrier_semaphore()
    steady = [{"gx": a, "gy": b} for a in (0, -1, 1, -2, 2) for b in (0, 1, 3, 2) if a or b] + [{"gx": -3}, {"gx": 3}]
    across = [{}, {"gx": -1}, {"gx": 1}, {"gy": -1}, {"gy": 1}]
    for d, there in ((-1, below), (1, above)):
        ids = [peer({**way, "gz": d}) for way in across]

        @pl.when(there)
        def _():
            for other in ids:
                pl.semaphore_signal(barrier, inc=1, device_id=other, device_id_type=MESH)
    for way in steady:
        pl.semaphore_signal(barrier, inc=1, device_id=peer(way), device_id_type=MESH)

    lane16 = iota((8, 8, 128), 2)
    chunks = range(0, 16, CHUNK)
    own, ring = slice(0, 256), slice(256, 384)

    def pack_y0(k, c, v):
        n = v.shape[-1]
        for i in range(v.shape[0]):
            YS0[k, 0, c + i:c + i + 1, 0:n] = v[i, 0:1, :]
            YS0[k, 1, c + i:c + i + 1, 0:n] = v[i, 7:8, :]

    def outer(k, c, lanes=slice(0, 384)):
        shape = (8, lanes.stop - lanes.start)
        first = iota(shape, 0) < 4
        return jnp.stack([jnp.where(first, jnp.broadcast_to(YH0[k, 0, c + i:c + i + 1, lanes], shape),
                                    jnp.broadcast_to(YH0[k, 1, c + i:c + i + 1, lanes], shape)) for i in range(CHUNK)])

    def inner(k, c):
        v = V0[k, 1 + c:1 + c + CHUNK]
        parts = []
        for i in range(c, c + CHUNK):
            terms = ([CX0[i] * V0[k, i]] if i else []) + ([CX0[i + 1] * V0[k, i + 2]] if i < 15 else [])
            parts.append(sum(terms[1:], terms[0]))
        total = jnp.stack(parts) + C0[0, c:c + CHUNK] * pltpu.roll(v, 7, 1) + C0[1, c:c + CHUNK] * pltpu.roll(v, 1, 1)
        return v, total + C0[2, c:c + CHUNK] * pltpu.roll(v, 383, 2) + C0[3, c:c + CHUNK] * pltpu.roll(v, 1, 2)

    def ends(k, c):
        return {i: CX0[i + (i == 15)] * V0[k, 17 if i else 0] for i in (0, 15) if c <= i < c + CHUNK}

    def faces0(k):
        return [post(YS0.at[k, 0], YH0.at[k, 1], {"gy": -1}), post(YS0.at[k, 1], YH0.at[k, 0], {"gy": 1}),
                post(V0.at[k, 1], V0.at[k, 17], {"gx": -1}), post(V0.at[k, 16], V0.at[k, 0], {"gx": 1})]

    def trim0(k, lanes=slice(0, 384)):
        for side, d in ((0, -1), (1, 1)):
            V0[k, 17 * side, :, lanes] = jnp.where(exists("gx", d), V0[k, 17 * side, :, lanes], 0.0)
            YH0[k, side, :, lanes] = jnp.where(exists("gy", d), YH0[k, side, :, lanes], 0.0)

    def pack_z0(n, field):
        low, high = field[:, :, 0:128], field[:, :, 128:256]
        ZS[n, 0] = jnp.where(lane16 < 64, low[0:8], pltpu.roll(low[8:16], 64, 2))
        ZS[n, 1] = jnp.where(lane16 < 64, pltpu.roll(high[0:8], 64, 2), high[8:16])

    def unpack_z0(n):
        up, down = jnp.where(above, ZH[n, 1], 0.0), jnp.where(below, ZH[n, 0], 0.0)
        return (jnp.where(lane16 < 64, up, pltpu.roll(down, 64, 2)), jnp.where(lane16 < 64, pltpu.roll(up, 64, 2), down))

    inputs[0].wait()
    inputs[1].wait()
    rho = jnp.where(mask[...] == 1, GAS_DENSITY, 1.0) * fac[...]
    V0[0, 1:17, :, own] = rho
    pack_z0(0, rho)
    pack_y0(0, 0, rho)
    inputs[2].wait()
    pack_z0(1, src[...])
    two = jnp.where(above, 1, 0) + jnp.where(below, 1, 0)
    pl.semaphore_wait(barrier, len(steady) + len(across) * two)

    low, high = pl.ds(0, 128), pl.ds(128, 128)
    to_below = [ready(ZS.at[0, 0], ZH.at[0, 1], {"gz": -1}),
                ready(V0.at[0, 1, :, low], HX.at[1, 1], {"gx": -1, "gz": -1}),
                ready(V0.at[0, 16, :, low], HX.at[0, 1], {"gx": 1, "gz": -1}),
                ready(YS0.at[0, 0, :, low], HY.at[1, 1], {"gy": -1, "gz": -1}),
                ready(YS0.at[0, 1, :, low], HY.at[0, 1], {"gy": 1, "gz": -1}),
                ready(ZS.at[1, 0], ZH.at[1, 1], {"gz": -1})]
    to_above = [ready(ZS.at[0, 1], ZH.at[0, 0], {"gz": 1}),
                ready(V0.at[0, 1, :, high], HX.at[1, 0], {"gx": -1, "gz": 1}),
                ready(V0.at[0, 16, :, high], HX.at[0, 0], {"gx": 1, "gz": 1}),
                ready(YS0.at[0, 0, :, high], HY.at[1, 0], {"gy": -1, "gz": 1}),
                ready(YS0.at[0, 1, :, high], HY.at[0, 0], {"gy": 1, "gz": 1}),
                ready(ZS.at[1, 1], ZH.at[1, 0], {"gz": 1})]
    for some in (slice(1, 5), slice(0, 1)):
        for group, there in ((to_below, below), (to_above, above)):
            @pl.when(there)
            def _():
                for copy in group[some]:
                    copy.start()
    both = pl.ds(0, 256)
    rho0_faces = [post(V0.at[0, 1, :, both], V0.at[0, 17, :, both], {"gx": -1}),
                  post(V0.at[0, 16, :, both], V0.at[0, 0, :, both], {"gx": 1}),
                  post(YS0.at[0, 0, :, both], YH0.at[0, 1, :, both], {"gy": -1}),
                  post(YS0.at[0, 1, :, both], YH0.at[0, 0, :, both], {"gy": 1})]
    for group, there in ((to_below, below), (to_above, above)):
        @pl.when(there)
        def _():
            group[5].start()

    a, b = lax.shift_right_logical(iota((384, 256), 0), 1), iota((384, 256), 1)
    pairs0 = ones_where(b == jnp.where(a < 160, a, a + 64))
    pairs1 = ones_where(lax.shift_right_logical(iota((256, 128), 0), 1) == iota((256, 128), 1))
    a, b = iota((256, 384), 0), lax.shift_right_logical(iota((256, 384), 1), 1)
    spread0 = ones_where(a == jnp.where(b < 160, b, b + 64))
    spread1 = ones_where(iota((128, 256), 0) == lax.shift_right_logical(iota((128, 256), 1), 1))

    def couple0(lanes, planes):
        for c in planes:
            CX0[c, :, lanes] = coupling(V0[0, c, :, lanes], V0[0, c + 1, :, lanes])

    def couple0_y(lanes):
        for c in chunks:
            rho = V0[0, 1 + c:1 + c + CHUNK, :, lanes]
            between = jnp.where(iota(rho.shape, 1) == 7, 0.0, coupling(rho, pltpu.roll(rho, 7, 1)))
            C0[0, c:c + CHUNK, :, lanes] = between
            C0[1, c:c + CHUNK, :, lanes] = pltpu.roll(between, 1, 1)

    def couple0_ends(lanes):
        for c in chunks:
            rho = V0[0, 1 + c:1 + c + CHUNK, :, lanes]
            row = iota(rho.shape, 1)
            CB0[c:c + CHUNK, :, lanes] = jnp.where((row == 0) | (row == 7), coupling(rho, outer(0, c, lanes)), 0.0)

    SRC[:, :, own] = src[...]
    couple0(own, range(1, 16))
    couple0_y(own)
    for c in chunks:
        rho = V0[0, 1 + c:1 + c + CHUNK, :, own]
        between = coupling(rho, pltpu.roll(rho, 255, 2))
        C0[2, c:c + CHUNK, :, own] = between
        C0[3, c:c + CHUNK, :, own] = pltpu.roll(between, 1, 2)
    arrived(rho0_faces)
    trim0(0, own)
    couple0(own, (0, 16))
    couple0_ends(own)
    def await_z(some):
        for group, there in ((to_below, above), (to_above, below)):
            @pl.when(there)
            def _():
                arrived(group[some])

    def invert0(lanes):
        for c in chunks:
            some = slice(c, c + CHUNK)
            diag = ((CX0[some, :, lanes] + CX0[c + 1:c + 1 + CHUNK, :, lanes]) + (C0[2, some, :, lanes] + C0[3, some, :, lanes])
                    + (C0[0, some, :, lanes] + C0[1, some, :, lanes] + CB0[some, :, lanes]))
            DIAG0[some, :, lanes] = diag
            INV0[some, :, lanes] = jnp.where(V0[0, 1 + c:1 + c + CHUNK, :, lanes] > 0.0, RELAXATION / diag, 0.0)

    await_z(slice(0, 1))
    first, second = unpack_z0(0)
    V0[0, 1:9, :, ring] = first
    V0[0, 9:17, :, ring] = second
    couple0(ring, range(1, 16))
    couple0_y(ring)
    for c in chunks:
        some = slice(c, c + CHUNK)
        rho = V0[0, 1 + c:1 + c + CHUNK]
        outside = rho[:, :, ring]
        lane = iota(outside.shape, 2)
        up = jnp.where(lane == 127, pltpu.roll(rho[:, :, 0:128], 127, 2), pltpu.roll(outside, 127, 2))
        down = jnp.where(lane == 0, pltpu.roll(rho[:, :, 128:256], 1, 2), pltpu.roll(outside, 1, 2))
        up, down = coupling(outside, up), coupling(outside, down)
        C0[2, some, :, ring] = up
        C0[3, some, :, ring] = down
        C0[2, some, :, 128:256] = jnp.where(lane == 127, pltpu.roll(down, 127, 2), C0[2, some, :, 128:256])
        C0[3, some, :, 0:128] = jnp.where(lane == 0, pltpu.roll(up, 1, 2), C0[3, some, :, 0:128])
    invert0(own)
    await_z(slice(1, 5))
    lane8, lane2 = iota((8, 128), 1), iota((16, 128), 1)
    for side in (0, 1):
        V0[0, 17 * side, :, ring] = jnp.where(
            lane8 < 64, jnp.where(above, HX[side, 1], 0.0), jnp.where(below, HX[side, 0], 0.0))
        YH0[0, side, :, ring] = jnp.where(
            lane2 < 64, jnp.where(above, HY[side, 1], 0.0), jnp.where(below, HY[side, 0], 0.0))
    trim0(0, ring)
    couple0(ring, (0, 16))
    couple0_ends(ring)
    invert0(ring)
    await_z(slice(5, 6))
    first, second = unpack_z0(1)
    SRC[0:8, :, ring] = first
    SRC[8:16, :, ring] = second

    for c in chunks:
        v = INV0[c:c + CHUNK] * SRC[c:c + CHUNK]
        V0[1, 1 + c:1 + c + CHUNK] = v
        pack_y0(1, c, v)
    v1_faces = faces0(1)
    for group, there in ((to_below, below), (to_above, above)):
        @pl.when(there)
        def _():
            left(group)
    for c in chunks:
        some = slice(c, c + CHUNK)
        v, total = inner(1, c)
        V0[2, 1 + c:1 + c + CHUNK] = KEEP * v + INV0[some] * (SRC[some] + total)
        KB0[some] = INV0[some] * CB0[some]

    row8 = iota((8, 256), 0)
    row8s = iota((8, 128), 0)

    row24 = iota((8, 384), 0)

    def down0(plane):
        tiles = []
        for j in range(4):
            t, u = (plane(4 * j + n) + plane(4 * j + n + 1) for n in (0, 2))
            t, u = (x + pltpu.roll(x, 7, 0) for x in (t, u))
            tile = pltpu.roll(u, 1, 0)
            for n, part in ((7, pltpu.roll(u, 2, 0)), (6, pltpu.roll(u, 3, 0)), (5, pltpu.roll(u, 4, 0)),
                            (4, pltpu.roll(t, 5, 0)), (3, pltpu.roll(t, 6, 0)), (2, pltpu.roll(t, 7, 0)), (1, t)):
                tile = jnp.where(row24 < n, part, tile)
            tiles.append(tile)
        t = dot(jnp.concatenate(tiles, axis=0), pairs0)
        return [t[8 * j:8 * j + 8] for j in range(4)]

    def slot(a, b):
        return SIDES.index((a, b))

    def exchange1(k, packed):
        for j in range(4):
            S1[k, j] = packed[j]
        group = []
        for a, b in ((1, 1), (1, -1), (-1, 1), (-1, -1), (0, 1), (0, -1), (1, 0), (-1, 0)):
            some = {1: pl.ds(2, 2), -1: pl.ds(0, 2), 0: pl.ds(0, 4)}[a]
            if k and a and b:
                some = pl.ds(3 if a > 0 else 0, 1)
            group.append(post(S1.at[k, some], H1.at[k, slot(-a, -b), some], {"gx": a, "gy": b}))
        return group

    def unpack1(k, target, first, last, offset):
        for p in range(first, last):
            a = p // 8
            j, half = (p % 8) // 2, p % 2

            def block(b):
                if not a and not b:
                    return S1[k, j]
                if k and a and b and j in (1, 2):
                    return jnp.zeros((8, 256), f32)
                return jnp.where(exists("gx", a) & exists("gy", b), H1[k, slot(a, b), j], 0.0)

            target[p - offset, 0:8] = jnp.where(row8 < 4, turn(block(0), -4 * half, 0), turn(block(1), 4 - 4 * half, 0))
            target[p - offset, 8:16] = jnp.where(row8 < 4, 0.0, turn(block(-1), 4 - 4 * half, 0))

    def shifts1(v):
        return pltpu.roll(v, 15, 0), pltpu.roll(v, 1, 0), pltpu.roll(v, 255, 1), pltpu.roll(v, 1, 1)

    def around1(V, p, base):
        v = V[p - base]
        total = CX1[p + 3] * V[p - 1 - base] + CX1[p + 4] * V[p + 1 - base]
        for n, other in enumerate(shifts1(v)):
            total = total + C1[n, p + 3] * other
        return v, total

    def down1(plane):
        packed = jnp.zeros((8, 256), f32)
        for x in range(4):
            t = plane(2 * x) + plane(2 * x + 1)
            t = t + pltpu.roll(t, 7, 0)
            for half in range(2):
                packed = jnp.where(row8 == 2 * x + half, turn(t, 2 * x - half, 0), packed)
        return dot(packed, pairs1)

    packed1 = [0.125 * t for t in down0(lambda p: V0[0, 1 + p])]
    rho1_copies = exchange1(0, packed1)
    G[gy] = 0.125 * down1(lambda p: packed1[p // 2] if p % 2 == 0 else pltpu.roll(packed1[p // 2], 4, 0))
    rho2_y = [post(G.at[gy], G.at[gy], {"gy": d}) for d in (1, 2, 3)]

    arrived(v1_faces)
    trim0(1)
    for c in chunks:
        for i, term in ends(1, c).items():
            V0[2, 1 + i] = V0[2, 1 + i] + INV0[i] * term
        v = V0[2, 1 + c:1 + c + CHUNK] + KB0[c:c + CHUNK] * outer(1, c)
        V0[2, 1 + c:1 + c + CHUNK] = v
        pack_y0(2, c, v)
    v2_faces = faces0(2)
    for c in chunks:
        v, total = inner(2, c)
        R0[c:c + CHUNK] = SRC[c:c + CHUNK] + total - DIAG0[c:c + CHUNK] * v

    def rows_of(blocks):
        planes = []
        for x in range(4):
            t = turn(blocks[0], -2 * x, 0)
            for q in (1, 2, 3):
                t = jnp.where(row8s < 2 * q, t, turn(blocks[q], 2 * (q - x), 0))
            planes.append(t)
        return planes

    arrived(rho2_y)
    for x, t in enumerate(rows_of([G[q] for q in range(4)])):
        XD[9 + x] = t
    rho2_x = [post(XD.at[9:13], XD.at[9 - 4 * d:13 - 4 * d], {"gx": d}) for d in (-2, -1, 1, 2)]
    rho2_x += [post(XD.at[12], XD.at[0], {"gx": 3}), post(XD.at[9], XD.at[21], {"gx": -3})]

    arrived(rho1_copies)
    unpack1(0, RHO1, -4, 12, -4)
    for p in range(-3, 12):
        CX1[p + 3] = coupling(RHO1[p + 3], RHO1[p + 4])
    for p in range(-3, 11):
        rho = RHO1[p + 4]
        diag = CX1[p + 3] + CX1[p + 4]
        for n, other in enumerate(shifts1(rho)):
            between = coupling(rho, other)
            C1[n, p + 3] = between
            diag = diag + between
        INV1[p + 3] = jnp.where(rho > 0.0, RELAXATION / diag, 0.0)
        if 0 <= p < 8:
            DIAG1[p] = diag

    arrived(v2_faces)
    trim0(2)
    residual = []
    for c in chunks:
        r = R0[c:c + CHUNK] + CB0[c:c + CHUNK] * outer(2, c)
        more = ends(2, c)
        residual += [r[i] + more[c + i] if c + i in more else r[i] for i in range(CHUNK)]
    b1_copies = exchange1(1, [0.5 * t for t in down0(lambda p: residual[p])])

    arrived(rho2_x)
    for d in (-2, -1, 1, 2):
        XD[9 - 4 * d:13 - 4 * d] = jnp.where(exists("gx", -d), XD[9 - 4 * d:13 - 4 * d], 0.0)
    XD[0] = jnp.where(exists("gx", -3), XD[0], 0.0)
    XD[21] = jnp.where(exists("gx", 3), XD[21], 0.0)
    row2 = iota((20, 8, 128), 1)
    rho = XD[1:21]
    cx2 = coupling(XD[0:21], XD[1:22])
    y_up = coupling(rho, jnp.where(row2 == 7, 0.0, pltpu.roll(rho, 7, 1)))
    y_down = coupling(rho, jnp.where(row2 == 0, 0.0, pltpu.roll(rho, 1, 1)))
    z_up = coupling(rho, pltpu.roll(rho, 127, 2))
    z_down = coupling(rho, pltpu.roll(rho, 1, 2))
    diag2 = cx2[0:20] + cx2[1:21] + ((y_up + y_down) + (z_up + z_down))
    inv2 = jnp.where(rho > 0.0, RELAXATION / diag2, 0.0)
    x_low, x_high = inv2 * cx2[0:20], inv2 * cx2[1:21]
    y_up = jnp.where(row2 == 7, 0.0, inv2 * y_up)
    y_down = jnp.where(row2 == 0, 0.0, inv2 * y_down)
    z_up, z_down = inv2 * z_up, inv2 * z_down

    near, far = slice(0, 8), slice(8, 16)

    def first1(planes):
        for p in planes:
            W1[p + 3] = INV1[p + 3] * B1[p + 3]

    def second1(p, rows):
        v, total = around1(W1, p, -3)
        for some in rows:
            W2[p + 2, some] = (KEEP * v + INV1[p + 3] * (B1[p + 3] + total))[some]

    def residual1(p):
        v, total = around1(W2, p, -2)
        return (B1[p + 3] + total - DIAG1[p] * v)[near]

    residual = {}
    arrived(b1_copies[4:6])
    unpack1(1, B1, 0, 8, -3)
    first1(range(8))
    for p in range(1, 7):
        second1(p, (near, far))
    for p in range(2, 6):
        residual[p] = residual1(p)
    arrived(b1_copies[0:4] + b1_copies[6:8])
    unpack1(1, B1, -3, 0, -3)
    unpack1(1, B1, 8, 11, -3)
    first1((-3, -2, -1, 8, 9, 10))
    for p, rows in ((-1, (near,)), (0, (near, far)), (7, (near, far)), (8, (near,))):
        second1(p, rows)
    for p in (0, 1, 6, 7):
        residual[p] = residual1(p)

    GB[2, gy] = 0.5 * down1(lambda p: residual[p])
    b2_copies = [post(GB.at[2, gy], GB.at[2 - d, gy], {"gx": d, "gy": e})
                 for e in (2, 1, 3, 0) for d in (2, -2, 1, -1, 0) if d or e]
    @pl.when(gx >= 0)
    def _():
        second1(-2, (near,))
        second1(-1, (far,))
        second1(8, (far,))
        second1(9, (near,))
        for p in range(-1, 9):
            v, total = around1(W2, p, -2)
            v = KEEP * v + INV1[p + 3] * (B1[p + 3] + total)
            for some in (near, far) if 0 <= p < 8 else (near,):
                E1[p + 1, some] = v[some]
        for c in chunks:
            v, total = inner(2, c)
            more = ends(2, c)
            total = total + CB0[c:c + CHUNK] * outer(2, c)
            total = jnp.stack([total[i] + more[c + i] if c + i in more else total[i] for i in range(CHUNK)])
            v = KEEP * v + INV0[c:c + CHUNK] * (SRC[c:c + CHUNK] + total)
            out[c:c + CHUNK] = v[:, :, own]
    late = {id(copy) for copy in to_below + to_above}
    left([copy for copy in copies if id(copy) not in late])
    arrived(b2_copies)
    planes = []
    for d in (-2, -1, 0, 1, 2):
        planes += [jnp.where(exists("gx", d), t, 0.0) if d else t for t in rows_of([GB[2 + d, q] for q in range(4)])]
    start = inv2 * jnp.stack(planes)
    v = start
    for k in range(1, COARSE_SWEEPS):
        z = 20 - k
        here = v[1:-1]
        total = x_low[k:z] * v[:-2] + x_high[k:z] * v[2:]
        total = total + y_up[k:z] * pltpu.roll(here, 7, 1) + y_down[k:z] * pltpu.roll(here, 1, 1)
        total = total + z_up[k:z] * pltpu.roll(here, 127, 2) + z_down[k:z] * pltpu.roll(here, 1, 2)
        v = (KEEP * here + start[k:z]) + total

    row6 = iota((6, 8, 128), 1)
    t = pltpu.roll(v, lax.rem(8 - 2 * gy, 8), 1)
    over = jnp.where(row6 < jnp.where(exists("gy", 1), 8, 4), grow(t, 1), 0.0)
    under = jnp.where(row6 >= jnp.where(exists("gy", -1), 6, 8), jnp.where(row6 == 7, t, pltpu.roll(t, 7, 1)), 0.0)
    t = dot(jnp.concatenate([over, under], axis=1).reshape(96, 128), spread1).reshape(6, 16, 256)
    moved = [shifts1(t[j]) for j in range(6)]
    for p in range(-1, 9):
        j = p // 2 + 1
        total = CX1[p + 3] * t[(p - 1) // 2 + 1] + CX1[p + 4] * t[(p + 1) // 2 + 1]
        for n, other in enumerate(moved[j]):
            total = total + C1[n, p + 3] * other
        v = E1[p + 1] + (KEEP * t[j] + INV1[p + 3] * total)
        for some in (near, far) if 0 <= p < 8 else (near,):
            E1[p + 1, some] = v[some]

    y_low = jnp.zeros((8, 256), f32)
    y_high = y_low
    for p in range(8):
        y_low = jnp.where(row8 == p, turn(E1[p + 1, far], p - 7, 0), y_low)
        y_high = jnp.where(row8 == p, turn(E1[p + 1, near], p - 4, 0), y_high)
    e = dot(jnp.concatenate([grow(E1[p, near], 0) for p in range(10)] + [y_low, y_high], axis=0), spread0)
    for m in range(8):
        here = e[8 * m + 8:8 * m + 16]
        beside = [x[:, own] for x in (pltpu.roll(here, 7, 0), pltpu.roll(here, 1, 0), pltpu.roll(here, 383, 1), pltpu.roll(here, 1, 1))]
        outside = jnp.where(row8 < 4, jnp.broadcast_to(e[80 + m:81 + m, own], (8, 256)), jnp.broadcast_to(e[88 + m:89 + m, own], (8, 256)))
        here = here[:, own]
        ways = ((e[8 * m:8 * m + 8, own], here), (here, e[8 * m + 16:8 * m + 24, own]))
        for i, (under, over) in zip((2 * m, 2 * m + 1), ways):
            total = CX0[i, :, own] * under + CX0[i + 1, :, own] * over + CB0[i, :, own] * outside
            for n in range(4):
                total = total + C0[n, i, :, own] * beside[n]
            out[i] = out[i] + (KEEP * here + INV0[i, :, own] * total)


def shards(source, phase_mask, density_factor):
    f32 = jnp.float32
    shapes = [
        (3, 18, 8, 384), (16, 8, 384), (3, 2, 16, 384), (3, 2, 16, 384), (2, 2, 8, 8, 128), (2, 2, 8, 8, 128),
        (2, 2, 8, 128), (2, 2, 16, 128), (17, 8, 384), (4, 16, 8, 384), (16, 8, 384), (16, 8, 384),
        (16, 8, 384), (16, 8, 384), (16, 8, 384),
        (2, 4, 8, 256), (2, 8, 4, 8, 256), (16, 16, 256), (15, 16, 256), (4, 14, 16, 256), (14, 16, 256), (8, 16, 256),
        (14, 16, 256), (14, 16, 256), (12, 16, 256), (10, 16, 256), (4, 8, 128), (5, 4, 8, 128), (22, 8, 128),
    ]
    return pl.pallas_call(
        kernel,
        out_shape=pltpu.VMEM((16, 8, 256), f32),
        in_specs=[pl.BlockSpec(memory_space=pl.ANY)] * 3,
        out_specs=pl.BlockSpec(memory_space=pltpu.VMEM),
        scratch_shapes=[pltpu.VMEM((16, 8, 256), kind) for kind in (f32, jnp.int32, f32)] + [pltpu.SemaphoreType.DMA((3,))]
        + [pltpu.VMEM(shape, f32) for shape in shapes] + [pltpu.SemaphoreType.DMA((COPIES,))] * 2,
        compiler_params=pltpu.CompilerParams(collective_id=0, has_side_effects=True),
        name="vcycle",
    )(source, phase_mask, density_factor)


def solution(mesh):
    spec = P("gx", "gy", "gz")
    return jax.shard_map(shards, mesh=mesh, in_specs=(spec,) * 3, out_specs=spec, check_vma=False)
```

```python
import jax
import jax.numpy as jnp
from jax import lax
from jax.experimental import pallas as pl
from jax.experimental.pallas import tpu as pltpu
from jax.sharding import PartitionSpec as P

GAS_DENSITY = 0.001
RELAXATION = 0.8
KEEP = 1.0 - RELAXATION
COARSE_SWEEPS = 8
MESH = pl.DeviceIdType.MESH
CHUNK = 2
COPIES = 68
TINY = 1e-30
AXES = ("gx", "gy", "gz")
SIDES = [(a, b) for a in (-1, 0, 1) for b in (-1, 0, 1) if a or b]


def iota(shape, axis):
    return lax.broadcasted_iota(jnp.int32, shape, axis)


def dot(a, b):
    high = a.astype(jnp.bfloat16)
    rest = a - high.astype(jnp.float32)
    middle = rest.astype(jnp.bfloat16)
    low = (rest - middle.astype(jnp.float32)).astype(jnp.bfloat16)
    return sum(jnp.dot(part, b, preferred_element_type=jnp.float32) for part in (low, middle, high))


def ones_where(condition):
    return jnp.where(condition, 1.0, 0.0).astype(jnp.bfloat16)


def turn(x, shift, axis):
    shift %= x.shape[axis]
    return pltpu.roll(x, shift, axis) if shift else x


def coupling(a, b):
    return 2.0 / jnp.maximum(a + b, TINY)


def grow(t, axis):
    row = iota(t.shape, axis)
    moved = [t] + [pltpu.roll(t, n, axis) for n in (1, 2, 3, 4)]
    low = jnp.where(row < 1, moved[0], jnp.where(row < 3, moved[1], moved[2]))
    high = jnp.where(row < 5, moved[2], jnp.where(row < 7, moved[3], moved[4]))
    return jnp.where(row < 4, low, high)


def kernel(src_in, mask_in, fac_in, out, src, mask, fac, in_sem, V0, SRC, YS0, YH0, ZS, ZH, HX, HY, CX0, C0, CB0, KB0, INV0, DIAG0, R0,
           S1, H1, RHO1, CX1, C1, INV1, DIAG1, B1, W1, W2, E1, G, GB, XD, send_sem, recv_sem):
    f32 = jnp.float32
    sizes = {axis: lax.axis_size(axis) for axis in AXES}
    at = {axis: lax.axis_index(axis) for axis in AXES}
    gx, gy = at["gx"], at["gy"]

    def peer(way):
        return {axis: lax.rem(at[axis] + (d + sizes[axis]), sizes[axis]) for axis, d in way.items() if d}

    def exists(axis, d):
        place = at[axis] + d
        return (place >= 0) & (place < sizes[axis])

    above, below = exists("gz", 1), exists("gz", -1)
    copies = []

    def ready(source, target, way):
        k = len(copies)
        copy = pltpu.make_async_remote_copy(
            src_ref=source, dst_ref=target, send_sem=send_sem.at[k], recv_sem=recv_sem.at[k],
            device_id=peer(way), device_id_type=MESH)
        copies.append(copy)
        return copy

    def post(source, target, way):
        copy = ready(source, target, way)
        copy.start()
        return copy

    def arrived(group):
        for copy in group:
            copy.wait_recv()

    def left(group):
        for copy in group:
            copy.wait_send()

    inputs = [pltpu.make_async_copy(a, b, in_sem.at[n]) for n, (a, b) in enumerate(((fac_in, fac), (mask_in, mask), (src_in, src)))]
    for copy in inputs:
        copy.start()

    barrier = pltpu.get_barrier_semaphore()
    steady = [{"gx": a, "gy": b} for a in (0, -1, 1, -2, 2) for b in (0, 1, 3, 2) if a or b] + [{"gx": -3}, {"gx": 3}]
    across = [{}, {"gx": -1}, {"gx": 1}, {"gy": -1}, {"gy": 1}]
    for d, there in ((-1, below), (1, above)):
        ids = [peer({**way, "gz": d}) for way in across]

        @pl.when(there)
        def _():
            for other in ids:
                pl.semaphore_signal(barrier, inc=1, device_id=other, device_id_type=MESH)
    for way in steady:
        pl.semaphore_signal(barrier, inc=1, device_id=peer(way), device_id_type=MESH)

    lane16 = iota((8, 8, 128), 2)
    chunks = range(0, 16, CHUNK)
    own, ring = slice(0, 256), slice(256, 384)

    def pack_y0(k, c, v):
        n = v.shape[-1]
        for i in range(v.shape[0]):
            YS0[k, 0, c + i:c + i + 1, 0:n] = v[i, 0:1, :]
            YS0[k, 1, c + i:c + i + 1, 0:n] = v[i, 7:8, :]

    def outer(k, c, lanes=slice(0, 384)):
        shape = (8, lanes.stop - lanes.start)
        first = iota(shape, 0) < 4
        return jnp.stack([jnp.where(first, jnp.broadcast_to(YH0[k, 0, c + i:c + i + 1, lanes], shape),
                                    jnp.broadcast_to(YH0[k, 1, c + i:c + i + 1, lanes], shape)) for i in range(CHUNK)])

    def inner(k, c):
        v = V0[k, 1 + c:1 + c + CHUNK]
        parts = []
        for i in range(c, c + CHUNK):
            terms = ([CX0[i] * V0[k, i]] if i else []) + ([CX0[i + 1] * V0[k, i + 2]] if i < 15 else [])
            parts.append(sum(terms[1:], terms[0]))
        total = jnp.stack(parts) + C0[0, c:c + CHUNK] * pltpu.roll(v, 7, 1) + C0[1, c:c + CHUNK] * pltpu.roll(v, 1, 1)
        return v, total + C0[2, c:c + CHUNK] * pltpu.roll(v, 383, 2) + C0[3, c:c + CHUNK] * pltpu.roll(v, 1, 2)

    def ends(k, c):
        return {i: CX0[i + (i == 15)] * V0[k, 17 if i else 0] for i in (0, 15) if c <= i < c + CHUNK}

    def faces0(k):
        return [post(YS0.at[k, 0], YH0.at[k, 1], {"gy": -1}), post(YS0.at[k, 1], YH0.at[k, 0], {"gy": 1}),
                post(V0.at[k, 1], V0.at[k, 17], {"gx": -1}), post(V0.at[k, 16], V0.at[k, 0], {"gx": 1})]

    def trim0(k, lanes=slice(0, 384)):
        for side, d in ((0, -1), (1, 1)):
            V0[k, 17 * side, :, lanes] = jnp.where(exists("gx", d), V0[k, 17 * side, :, lanes], 0.0)
            YH0[k, side, :, lanes] = jnp.where(exists("gy", d), YH0[k, side, :, lanes], 0.0)

    def pack_z0(n, field):
        low, high = field[:, :, 0:128], field[:, :, 128:256]
        ZS[n, 0] = jnp.where(lane16 < 64, low[0:8], pltpu.roll(low[8:16], 64, 2))
        ZS[n, 1] = jnp.where(lane16 < 64, pltpu.roll(high[0:8], 64, 2), high[8:16])

    def unpack_z0(n):
        up, down = jnp.where(above, ZH[n, 1], 0.0), jnp.where(below, ZH[n, 0], 0.0)
        return (jnp.where(lane16 < 64, up, pltpu.roll(down, 64, 2)), jnp.where(lane16 < 64, pltpu.roll(up, 64, 2), down))

    inputs[0].wait()
    inputs[1].wait()
    rho = jnp.where(mask[...] == 1, GAS_DENSITY, 1.0) * fac[...]
    V0[0, 1:17, :, own] = rho
    pack_z0(0, rho)
    pack_y0(0, 0, rho)
    inputs[2].wait()
    pack_z0(1, src[...])
    two = jnp.where(above, 1, 0) + jnp.where(below, 1, 0)
    pl.semaphore_wait(barrier, len(steady) + len(across) * two)

    low, high = pl.ds(0, 128), pl.ds(128, 128)
    to_below = [ready(ZS.at[0, 0], ZH.at[0, 1], {"gz": -1}),
                ready(V0.at[0, 1, :, low], HX.at[1, 1], {"gx": -1, "gz": -1}),
                ready(V0.at[0, 16, :, low], HX.at[0, 1], {"gx": 1, "gz": -1}),
                ready(YS0.at[0, 0, :, low], HY.at[1, 1], {"gy": -1, "gz": -1}),
                ready(YS0.at[0, 1, :, low], HY.at[0, 1], {"gy": 1, "gz": -1}),
                ready(ZS.at[1, 0], ZH.at[1, 1], {"gz": -1})]
    to_above = [ready(ZS.at[0, 1], ZH.at[0, 0], {"gz": 1}),
                ready(V0.at[0, 1, :, high], HX.at[1, 0], {"gx": -1, "gz": 1}),
                ready(V0.at[0, 16, :, high], HX.at[0, 0], {"gx": 1, "gz": 1}),
                ready(YS0.at[0, 0, :, high], HY.at[1, 0], {"gy": -1, "gz": 1}),
                ready(YS0.at[0, 1, :, high], HY.at[0, 0], {"gy": 1, "gz": 1}),
                ready(ZS.at[1, 1], ZH.at[1, 0], {"gz": 1})]
    for some in (slice(1, 5), slice(0, 1)):
        for group, there in ((to_below, below), (to_above, above)):
            @pl.when(there)
            def _():
                for copy in group[some]:
                    copy.start()
    both = pl.ds(0, 256)
    rho0_faces = [post(V0.at[0, 1, :, both], V0.at[0, 17, :, both], {"gx": -1}),
                  post(V0.at[0, 16, :, both], V0.at[0, 0, :, both], {"gx": 1}),
                  post(YS0.at[0, 0, :, both], YH0.at[0, 1, :, both], {"gy": -1}),
                  post(YS0.at[0, 1, :, both], YH0.at[0, 0, :, both], {"gy": 1})]
    for group, there in ((to_below, below), (to_above, above)):
        @pl.when(there)
        def _():
            group[5].start()

    a, b = lax.shift_right_logical(iota((384, 256), 0), 1), iota((384, 256), 1)
    pairs0 = ones_where(b == jnp.where(a < 160, a, a + 64))
    pairs1 = ones_where(lax.shift_right_logical(iota((256, 128), 0), 1) == iota((256, 128), 1))
    a, b = iota((256, 384), 0), lax.shift_right_logical(iota((256, 384), 1), 1)
    spread0 = ones_where(a == jnp.where(b < 160, b, b + 64))
    spread1 = ones_where(iota((128, 256), 0) == lax.shift_right_logical(iota((128, 256), 1), 1))

    def couple0(lanes, planes):
        for c in planes:
            CX0[c, :, lanes] = coupling(V0[0, c, :, lanes], V0[0, c + 1, :, lanes])

    def couple0_y(lanes):
        for c in chunks:
            rho = V0[0, 1 + c:1 + c + CHUNK, :, lanes]
            between = jnp.where(iota(rho.shape, 1) == 7, 0.0, coupling(rho, pltpu.roll(rho, 7, 1)))
            C0[0, c:c + CHUNK, :, lanes] = between
            C0[1, c:c + CHUNK, :, lanes] = pltpu.roll(between, 1, 1)

    def couple0_ends(lanes):
        for c in chunks:
            rho = V0[0, 1 + c:1 + c + CHUNK, :, lanes]
            row = iota(rho.shape, 1)
            CB0[c:c + CHUNK, :, lanes] = jnp.where((row == 0) | (row == 7), coupling(rho, outer(0, c, lanes)), 0.0)

    SRC[:, :, own] = src[...]
    couple0(own, range(1, 16))
    couple0_y(own)
    for c in chunks:
        rho = V0[0, 1 + c:1 + c + CHUNK, :, own]
        between = coupling(rho, pltpu.roll(rho, 255, 2))
        C0[2, c:c + CHUNK, :, own] = between
        C0[3, c:c + CHUNK, :, own] = pltpu.roll(between, 1, 2)
    arrived(rho0_faces)
    trim0(0, own)
    couple0(own, (0, 16))
    couple0_ends(own)
    def await_z(some):
        for group, there in ((to_below, above), (to_above, below)):
            @pl.when(there)
            def _():
                arrived(group[some])

    def invert0(lanes):
        for c in chunks:
            some = slice(c, c + CHUNK)
            diag = ((CX0[some, :, lanes] + CX0[c + 1:c + 1 + CHUNK, :, lanes]) + (C0[2, some, :, lanes] + C0[3, some, :, lanes])
                    + (C0[0, some, :, lanes] + C0[1, some, :, lanes] + CB0[some, :, lanes]))
            DIAG0[some, :, lanes] = diag
            INV0[some, :, lanes] = jnp.where(V0[0, 1 + c:1 + c + CHUNK, :, lanes] > 0.0, RELAXATION / diag, 0.0)

    await_z(slice(0, 1))
    first, second = unpack_z0(0)
    V0[0, 1:9, :, ring] = first
    V0[0, 9:17, :, ring] = second
    couple0(ring, range(1, 16))
    couple0_y(ring)
    for c in chunks:
        some = slice(c, c + CHUNK)
        rho = V0[0, 1 + c:1 + c + CHUNK]
        outside = rho[:, :, ring]
        lane = iota(outside.shape, 2)
        up = jnp.where(lane == 127, pltpu.roll(rho[:, :, 0:128], 127, 2), pltpu.roll(outside, 127, 2))
        down = jnp.where(lane == 0, pltpu.roll(rho[:, :, 128:256], 1, 2), pltpu.roll(outside, 1, 2))
        up, down = coupling(outside, up), coupling(outside, down)
        C0[2, some, :, ring] = up
        C0[3, some, :, ring] = down
        C0[2, some, :, 128:256] = jnp.where(lane == 127, pltpu.roll(down, 127, 2), C0[2, some, :, 128:256])
        C0[3, some, :, 0:128] = jnp.where(lane == 0, pltpu.roll(up, 1, 2), C0[3, some, :, 0:128])
    invert0(own)
    await_z(slice(1, 5))
    lane8, lane2 = iota((8, 128), 1), iota((16, 128), 1)
    for side in (0, 1):
        V0[0, 17 * side, :, ring] = jnp.where(
            lane8 < 64, jnp.where(above, HX[side, 1], 0.0), jnp.where(below, HX[side, 0], 0.0))
        YH0[0, side, :, ring] = jnp.where(
            lane2 < 64, jnp.where(above, HY[side, 1], 0.0), jnp.where(below, HY[side, 0], 0.0))
    trim0(0, ring)
    couple0(ring, (0, 16))
    couple0_ends(ring)
    invert0(ring)
    await_z(slice(5, 6))
    first, second = unpack_z0(1)
    SRC[0:8, :, ring] = first
    SRC[8:16, :, ring] = second

    for c in chunks:
        v = INV0[c:c + CHUNK] * SRC[c:c + CHUNK]
        V0[1, 1 + c:1 + c + CHUNK] = v
        pack_y0(1, c, v)
    v1_faces = faces0(1)
    for group, there in ((to_below, below), (to_above, above)):
        @pl.when(there)
        def _():
            left(group)
    for c in chunks:
        some = slice(c, c + CHUNK)
        v, total = inner(1, c)
        V0[2, 1 + c:1 + c + CHUNK] = KEEP * v + INV0[some] * (SRC[some] + total)
        KB0[some] = INV0[some] * CB0[some]

    row8 = iota((8, 256), 0)
    row8s = iota((8, 128), 0)

    row24 = iota((8, 384), 0)

    def down0(plane):
        tiles = []
        for j in range(4):
            t, u = (plane(4 * j + n) + plane(4 * j + n + 1) for n in (0, 2))
            t, u = (x + pltpu.roll(x, 7, 0) for x in (t, u))
            tile = pltpu.roll(u, 1, 0)
            for n, part in ((7, pltpu.roll(u, 2, 0)), (6, pltpu.roll(u, 3, 0)), (5, pltpu.roll(u, 4, 0)),
                            (4, pltpu.roll(t, 5, 0)), (3, pltpu.roll(t, 6, 0)), (2, pltpu.roll(t, 7, 0)), (1, t)):
                tile = jnp.where(row24 < n, part, tile)
            tiles.append(tile)
        t = dot(jnp.concatenate(tiles, axis=0), pairs0)
        return [t[8 * j:8 * j + 8] for j in range(4)]

    def slot(a, b):
        return SIDES.index((a, b))

    def exchange1(k, packed):
        for j in range(4):
            S1[k, j] = packed[j]
        group = []
        for a, b in ((1, 1), (1, -1), (-1, 1), (-1, -1), (0, 1), (0, -1), (1, 0), (-1, 0)):
            some = {1: pl.ds(2, 2), -1: pl.ds(0, 2), 0: pl.ds(0, 4)}[a]
            if k and a and b:
                some = pl.ds(3 if a > 0 else 0, 1)
            group.append(post(S1.at[k, some], H1.at[k, slot(-a, -b), some], {"gx": a, "gy": b}))
        return group

    def unpack1(k, target, first, last, offset):
        for p in range(first, last):
            a = p // 8
            j, half = (p % 8) // 2, p % 2

            def block(b):
                if not a and not b:
                    return S1[k, j]
                if k and a and b and j in (1, 2):
                    return jnp.zeros((8, 256), f32)
                return jnp.where(exists("gx", a) & exists("gy", b), H1[k, slot(a, b), j], 0.0)

            target[p - offset, 0:8] = jnp.where(row8 < 4, turn(block(0), -4 * half, 0), turn(block(1), 4 - 4 * half, 0))
            target[p - offset, 8:16] = jnp.where(row8 < 4, 0.0, turn(block(-1), 4 - 4 * half, 0))

    def shifts1(v):
        return pltpu.roll(v, 15, 0), pltpu.roll(v, 1, 0), pltpu.roll(v, 255, 1), pltpu.roll(v, 1, 1)

    def around1(V, p, base):
        v = V[p - base]
        total = CX1[p + 3] * V[p - 1 - base] + CX1[p + 4] * V[p + 1 - base]
        for n, other in enumerate(shifts1(v)):
            total = total + C1[n, p + 3] * other
        return v, total

    def down1(plane):
        packed = jnp.zeros((8, 256), f32)
        for x in range(4):
            t = plane(2 * x) + plane(2 * x + 1)
            t = t + pltpu.roll(t, 7, 0)
            for half in range(2):
                packed = jnp.where(row8 == 2 * x + half, turn(t, 2 * x - half, 0), packed)
        return dot(packed, pairs1)

    packed1 = [0.125 * t for t in down0(lambda p: V0[0, 1 + p])]
    rho1_copies = exchange1(0, packed1)
    G[gy] = 0.125 * down1(lambda p: packed1[p // 2] if p % 2 == 0 else pltpu.roll(packed1[p // 2], 4, 0))
    rho2_y = [post(G.at[gy], G.at[gy], {"gy": d}) for d in (1, 2, 3)]

    arrived(v1_faces)
    trim0(1)
    for c in chunks:
        for i, term in ends(1, c).items():
            V0[2, 1 + i] = V0[2, 1 + i] + INV0[i] * term
        v = V0[2, 1 + c:1 + c + CHUNK] + KB0[c:c + CHUNK] * outer(1, c)
        V0[2, 1 + c:1 + c + CHUNK] = v
        pack_y0(2, c, v)
    v2_faces = faces0(2)
    for c in chunks:
        v, total = inner(2, c)
        R0[c:c + CHUNK] = SRC[c:c + CHUNK] + total - DIAG0[c:c + CHUNK] * v

    def rows_of(blocks):
        planes = []
        for x in range(4):
            t = turn(blocks[0], -2 * x, 0)
            for q in (1, 2, 3):
                t = jnp.where(row8s < 2 * q, t, turn(blocks[q], 2 * (q - x), 0))
            planes.append(t)
        return planes

    arrived(rho2_y)
    for x, t in enumerate(rows_of([G[q] for q in range(4)])):
        XD[9 + x] = t
    rho2_x = [post(XD.at[9:13], XD.at[9 - 4 * d:13 - 4 * d], {"gx": d}) for d in (-2, -1, 1, 2)]
    rho2_x += [post(XD.at[12], XD.at[0], {"gx": 3}), post(XD.at[9], XD.at[21], {"gx": -3})]

    arrived(rho1_copies)
    unpack1(0, RHO1, -4, 12, -4)
    for p in range(-3, 12):
        CX1[p + 3] = coupling(RHO1[p + 3], RHO1[p + 4])
    for p in range(-3, 11):
        rho = RHO1[p + 4]
        diag = CX1[p + 3] + CX1[p + 4]
        for n, other in enumerate(shifts1(rho)):
            between = coupling(rho, other)
            C1[n, p + 3] = between
            diag = diag + between
        INV1[p + 3] = jnp.where(rho > 0.0, RELAXATION / diag, 0.0)
        if 0 <= p < 8:
            DIAG1[p] = diag

    arrived(v2_faces)
    trim0(2)
    residual = []
    for c in chunks:
        r = R0[c:c + CHUNK] + CB0[c:c + CHUNK] * outer(2, c)
        more = ends(2, c)
        residual += [r[i] + more[c + i] if c + i in more else r[i] for i in range(CHUNK)]
    b1_copies = exchange1(1, [0.5 * t for t in down0(lambda p: residual[p])])

    arrived(rho2_x)
    for d in (-2, -1, 1, 2):
        XD[9 - 4 * d:13 - 4 * d] = jnp.where(exists("gx", -d), XD[9 - 4 * d:13 - 4 * d], 0.0)
    XD[0] = jnp.where(exists("gx", -3), XD[0], 0.0)
    XD[21] = jnp.where(exists("gx", 3), XD[21], 0.0)
    row2 = iota((20, 8, 128), 1)
    rho = XD[1:21]
    cx2 = coupling(XD[0:21], XD[1:22])
    y_up = coupling(rho, jnp.where(row2 == 7, 0.0, pltpu.roll(rho, 7, 1)))
    y_down = coupling(rho, jnp.where(row2 == 0, 0.0, pltpu.roll(rho, 1, 1)))
    z_up = coupling(rho, pltpu.roll(rho, 127, 2))
    z_down = coupling(rho, pltpu.roll(rho, 1, 2))
    diag2 = cx2[0:20] + cx2[1:21] + ((y_up + y_down) + (z_up + z_down))
    inv2 = jnp.where(rho > 0.0, RELAXATION / diag2, 0.0)
    x_low, x_high = inv2 * cx2[0:20], inv2 * cx2[1:21]
    y_up = jnp.where(row2 == 7, 0.0, inv2 * y_up)
    y_down = jnp.where(row2 == 0, 0.0, inv2 * y_down)
    z_up, z_down = inv2 * z_up, inv2 * z_down

    near, far = slice(0, 8), slice(8, 16)

    def first1(planes):
        for p in planes:
            W1[p + 3] = INV1[p + 3] * B1[p + 3]

    def second1(p, rows):
        v, total = around1(W1, p, -3)
        for some in rows:
            W2[p + 2, some] = (KEEP * v + INV1[p + 3] * (B1[p + 3] + total))[some]

    def residual1(p):
        v, total = around1(W2, p, -2)
        return (B1[p + 3] + total - DIAG1[p] * v)[near]

    residual = {}
    arrived(b1_copies[4:6])
    unpack1(1, B1, 0, 8, -3)
    first1(range(8))
    for p in range(1, 7):
        second1(p, (near, far))
    for p in range(2, 6):
        residual[p] = residual1(p)
    arrived(b1_copies[0:4] + b1_copies[6:8])
    unpack1(1, B1, -3, 0, -3)
    unpack1(1, B1, 8, 11, -3)
    first1((-3, -2, -1, 8, 9, 10))
    for p, rows in ((-1, (near,)), (0, (near, far)), (7, (near, far)), (8, (near,))):
        second1(p, rows)
    for p in (0, 1, 6, 7):
        residual[p] = residual1(p)

    GB[2, gy] = 0.5 * down1(lambda p: residual[p])
    order = [(d, e) for e in (2, 1, 3, 0) for d in (2, -2, 1, -1, 0) if d or e]
    b2_copies = [post(GB.at[2, gy], GB.at[2 - d, gy], {"gx": d, "gy": e})
                 for d, e in order]
    @pl.when(gx >= 0)
    def _():
        second1(-2, (near,))
        second1(-1, (far,))
        second1(8, (far,))
        second1(9, (near,))
        for p in range(-1, 9):
            v, total = around1(W2, p, -2)
            v = KEEP * v + INV1[p + 3] * (B1[p + 3] + total)
            for some in (near, far) if 0 <= p < 8 else (near,):
                E1[p + 1, some] = v[some]
        for c in chunks:
            v, total = inner(2, c)
            more = ends(2, c)
            total = total + CB0[c:c + CHUNK] * outer(2, c)
            total = jnp.stack([total[i] + more[c + i] if c + i in more else total[i] for i in range(CHUNK)])
            v = KEEP * v + INV0[c:c + CHUNK] * (SRC[c:c + CHUNK] + total)
            out[c:c + CHUNK] = v[:, :, own]
    late = {id(copy) for copy in to_below + to_above}
    left([copy for copy in copies if id(copy) not in late])
    parts = {}
    for d in (0, 1, -1, 2, -2):
        arrived([copy for copy, way in zip(b2_copies, order) if way[0] == -d])
        planes = [jnp.where(exists("gx", d), t, 0.0) if d else t for t in rows_of([GB[2 + d, q] for q in range(4)])]
        parts[d] = inv2[4 * d + 8:4 * d + 12] * jnp.stack(planes)
    start = jnp.concatenate([parts[d] for d in (-2, -1, 0, 1, 2)], axis=0)
    v = start
    for k in range(1, COARSE_SWEEPS):
        z = 20 - k
        here = v[1:-1]
        total = x_low[k:z] * v[:-2] + x_high[k:z] * v[2:]
        total = total + y_up[k:z] * pltpu.roll(here, 7, 1) + y_down[k:z] * pltpu.roll(here, 1, 1)
        total = total + z_up[k:z] * pltpu.roll(here, 127, 2) + z_down[k:z] * pltpu.roll(here, 1, 2)
        v = (KEEP * here + start[k:z]) + total

    row6 = iota((6, 8, 128), 1)
    t = pltpu.roll(v, lax.rem(8 - 2 * gy, 8), 1)
    over = jnp.where(row6 < jnp.where(exists("gy", 1), 8, 4), grow(t, 1), 0.0)
    under = jnp.where(row6 >= jnp.where(exists("gy", -1), 6, 8), jnp.where(row6 == 7, t, pltpu.roll(t, 7, 1)), 0.0)
    t = dot(jnp.concatenate([over, under], axis=1).reshape(96, 128), spread1).reshape(6, 16, 256)
    moved = [shifts1(t[j]) for j in range(6)]
    for p in range(-1, 9):
        j = p // 2 + 1
        total = CX1[p + 3] * t[(p - 1) // 2 + 1] + CX1[p + 4] * t[(p + 1) // 2 + 1]
        for n, other in enumerate(moved[j]):
            total = total + C1[n, p + 3] * other
        v = E1[p + 1] + (KEEP * t[j] + INV1[p + 3] * total)
        for some in (near, far) if 0 <= p < 8 else (near,):
            E1[p + 1, some] = v[some]

    y_low = jnp.zeros((8, 256), f32)
    y_high = y_low
    for p in range(8):
        y_low = jnp.where(row8 == p, turn(E1[p + 1, far], p - 7, 0), y_low)
        y_high = jnp.where(row8 == p, turn(E1[p + 1, near], p - 4, 0), y_high)
    e = dot(jnp.concatenate([grow(E1[p, near], 0) for p in range(10)] + [y_low, y_high], axis=0), spread0)
    for m in range(8):
        here = e[8 * m + 8:8 * m + 16]
        beside = [x[:, own] for x in (pltpu.roll(here, 7, 0), pltpu.roll(here, 1, 0), pltpu.roll(here, 383, 1), pltpu.roll(here, 1, 1))]
        outside = jnp.where(row8 < 4, jnp.broadcast_to(e[80 + m:81 + m, own], (8, 256)), jnp.broadcast_to(e[88 + m:89 + m, own], (8, 256)))
        here = here[:, own]
        ways = ((e[8 * m:8 * m + 8, own], here), (here, e[8 * m + 16:8 * m + 24, own]))
        for i, (under, over) in zip((2 * m, 2 * m + 1), ways):
            total = CX0[i, :, own] * under + CX0[i + 1, :, own] * over + CB0[i, :, own] * outside
            for n in range(4):
                total = total + C0[n, i, :, own] * beside[n]
            out[i] = out[i] + (KEEP * here + INV0[i, :, own] * total)


def shards(source, phase_mask, density_factor):
    f32 = jnp.float32
    shapes = [
        (3, 18, 8, 384), (16, 8, 384), (3, 2, 16, 384), (3, 2, 16, 384), (2, 2, 8, 8, 128), (2, 2, 8, 8, 128),
        (2, 2, 8, 128), (2, 2, 16, 128), (17, 8, 384), (4, 16, 8, 384), (16, 8, 384), (16, 8, 384),
        (16, 8, 384), (16, 8, 384), (16, 8, 384),
        (2, 4, 8, 256), (2, 8, 4, 8, 256), (16, 16, 256), (15, 16, 256), (4, 14, 16, 256), (14, 16, 256), (8, 16, 256),
        (14, 16, 256), (14, 16, 256), (12, 16, 256), (10, 16, 256), (4, 8, 128), (5, 4, 8, 128), (22, 8, 128),
    ]
    return pl.pallas_call(
        kernel,
        out_shape=pltpu.VMEM((16, 8, 256), f32),
        in_specs=[pl.BlockSpec(memory_space=pl.ANY)] * 3,
        out_specs=pl.BlockSpec(memory_space=pltpu.VMEM),
        scratch_shapes=[pltpu.VMEM((16, 8, 256), kind) for kind in (f32, jnp.int32, f32)] + [pltpu.SemaphoreType.DMA((3,))]
        + [pltpu.VMEM(shape, f32) for shape in shapes] + [pltpu.SemaphoreType.DMA((COPIES,))] * 2,
        compiler_params=pltpu.CompilerParams(collective_id=0, has_side_effects=True),
        name="vcycle",
    )(source, phase_mask, density_factor)


def solution(mesh):
    spec = P("gx", "gy", "gz")
    return jax.shard_map(shards, mesh=mesh, in_specs=(spec,) * 3, out_specs=spec, check_vma=False)
```
